32 devices in a mesh: batch: 16 (over z, x, core), seq: 2 (over y).
Axes of the slice: x: 2, y: 2, z: 4, core: 2. Of those that a mesh axis runs over, the one named last changes fastest.
Arguments:
- latent_in: bfloat16 [32, 1024, 1152], P('batch', 'seq'), may hold values from -6 to 6
- conditioning: bfloat16 [32, 1152], P('batch'), may hold values from -6 to 6
- ada_weight: bfloat16 [7962624], P(('batch', 'seq')), may hold values from -0.1875 to 0.1875
- qkv_weight: bfloat16 [3981312], P(('batch', 'seq')), may hold values from -0.1875 to 0.1875
- proj_weight: bfloat16 [1327104], P(('batch', 'seq')), may hold values from -1 to 1
- up_weight: bfloat16 [5308416], P(('batch', 'seq')), may hold values from -0.1875 to 0.1875
- down_weight: bfloat16 [5308416], P(('batch', 'seq')), may hold values from -0.09375 to 0.09375
- bias_pack: bfloat16 [16128], P(('batch', 'seq')), may hold values from -2 to 2
- cotangent: bfloat16 [32, 1024, 1152], P('batch', 'seq'), may hold values from -6 to 6
Outputs:
- output: bfloat16 [32, 1024, 1152], P('batch', 'seq')
- grad_input: bfloat16 [32, 1024, 1152], P('batch', 'seq')
- grad_cond: bfloat16 [32, 1152], P('batch')
- grad_ada: float32 [7962624], P(('batch', 'seq'))
- grad_qkv: float32 [3981312], P(('batch', 'seq'))
- grad_proj: float32 [1327104], P(('batch', 'seq'))
- grad_up: float32 [5308416], P(('batch', 'seq'))
- grad_down: float32 [5308416], P(('batch', 'seq'))
- grad_bias: float32 [16128], P(('batch', 'seq'))
The draws below stay inside these ranges and needn't reach their ends.
All inputs are finite; a program needn't handle non-finite values.
Results may differ from the reference program's by a relative error of at most 0.015.
The reference program's roundings to bfloat16 on the way count: a program that leaves them out, or rounds other values in their place, can miss the bound.
Values may be sent and summed in bfloat16 or wider, within the bound.
No kernel may reach another device: no remote copies, remote signals or barrier semaphores. Data moves between devices by JAX's collectives and lax.ppermute only.
A program may use at most 512 MiB of HBM per device.

```python
from functools import partial
import jax
import jax.numpy as jnp
from jax import lax

H = 16
HD = 72
D = 1152
FF = 4608
SEQ_LEN = 1024
LATENTS = 32


def shard_levels(rng, extent, pieces, least, high):
    level = 1.0
    for dim, shards_of in pieces:
        draws = jax.random.uniform(jax.random.fold_in(jax.random.fold_in(rng, 6), dim), (shards_of,), jnp.float32, least / len(pieces), high / len(pieces))
        level = level * jnp.repeat(jnp.exp(draws), extent[dim] // shards_of).reshape((-1,) + (1,) * (len(extent) - 1 - dim))
    return level


def bell_draw(stream_key, extent, scale, reach, cuts=(), dtype=jnp.bfloat16):
    level = shard_levels(stream_key, extent, cuts, -0.22, 0.18) if cuts else 1.0
    drawn = jax.random.normal(stream_key, extent, jnp.float32) * scale * level
    return jnp.minimum(jnp.maximum(drawn, -reach), reach).astype(dtype)


def setup_inputs(seed: int = 0) -> dict:
    key_list = jax.random.split(jax.random.key(seed), 10)
    return {
        "latent_in": bell_draw(key_list[0], (LATENTS, SEQ_LEN, D), 1.0, 6.0, ((0, 16), (1, 2))),
        "conditioning": bell_draw(key_list[1], (LATENTS, D), 1.0, 6.0, ((0, 16),)),
        "ada_weight": bell_draw(key_list[2], (6 * D * D,), D ** -0.5, 0.1875, ((0, 32),)),
        "qkv_weight": bell_draw(key_list[3], (3 * D * D,), D ** -0.5, 0.1875, ((0, 32),)),
        "proj_weight": bell_draw(key_list[4], (D * D,), (D // 32) ** -0.5, 1.0, ((0, 32),)),
        "up_weight": bell_draw(key_list[5], (D * FF,), D ** -0.5, 0.1875, ((0, 32),)),
        "down_weight": bell_draw(key_list[6], (FF * D,), FF ** -0.5, 0.09375, ((0, 32),)),
        "bias_pack": bell_draw(key_list[7], (10 * D + FF,), 0.3, 2.0, ((0, 32),)),
        "cotangent": bell_draw(key_list[8], (LATENTS, SEQ_LEN, D), 1.0, 6.0, ((0, 16), (1, 2))),
    }


EPS = 1e-06
GELU_COEF = 0.7978845608028654
HIGHEST_PRECISION = lax.Precision.HIGHEST

@jax.custom_vjp
def low(v):
    return lax.optimization_barrier(v.astype(jnp.bfloat16)).astype(jnp.float32)

@jax.custom_vjp
def low_back(v):
    return v

def low_keep(v):
    return (low(v), None)

def low_pass(kept, grad):
    return (grad,)

def back_keep(v):
    return (v, None)

def back_low(kept, grad):
    return (low(grad),)
low.defvjp(low_keep, low_pass)
low_back.defvjp(back_keep, back_low)

def norm_modulate(inputs, shift_term, scale_term):
    center = inputs - lax.optimization_barrier(jnp.mean(inputs, axis=-1, keepdims=True))
    spread = lax.optimization_barrier(jnp.mean(center * center, axis=-1, keepdims=True))
    return center * lax.rsqrt(spread + EPS) * (1.0 + scale_term) + shift_term

def gelu_tanh(values):
    return 0.5 * values * (1.0 + jnp.tanh(GELU_COEF * (values + 0.044715 * values * values * values)))

def latent_layer(matrices, latent_pair):
    ada_matrix, qkv_matrix, proj_matrix, up_matrix, down_matrix, biases = matrices
    tokens, condition = latent_pair
    ada_bias = biases[:6 * D]
    query_bias = biases[6 * D:7 * D]
    value_bias = biases[7 * D:8 * D]
    proj_bias = biases[8 * D:9 * D]
    up_bias = biases[9 * D:9 * D + FF]
    down_bias = biases[9 * D + FF:]
    silu_cond = low(jax.nn.silu(condition))
    modulations = low_back(jnp.dot(silu_cond, ada_matrix, precision=HIGHEST_PRECISION) + ada_bias)
    shift_attention, scale_attention, gate_attention, shift_feed, scale_feed, gate_feed = jnp.split(modulations, 6)
    normed = low(norm_modulate(tokens, shift_attention, scale_attention))
    projected = jnp.dot(normed, qkv_matrix, precision=HIGHEST_PRECISION)
    queries = low(low_back(projected[:, :D] + query_bias))
    keys = low(low_back(projected[:, D:2 * D]))
    values = low(low_back(projected[:, 2 * D:] + value_bias))
    query_heads = queries.reshape(SEQ_LEN, H, HD)
    key_heads = keys.reshape(SEQ_LEN, H, HD)
    value_heads = values.reshape(SEQ_LEN, H, HD)
    scores = low_back(jnp.einsum('qhe,khe->hqk', query_heads, key_heads, precision=HIGHEST_PRECISION)) * HD ** (-0.5)
    attention_probs = low(jax.nn.softmax(scores, axis=-1))
    attended = jnp.einsum('hqk,khe->qhe', attention_probs, value_heads, precision=HIGHEST_PRECISION).reshape(SEQ_LEN, D)
    attended = low(low_back(attended))
    branch = low_back(jnp.dot(attended, proj_matrix, precision=HIGHEST_PRECISION) + proj_bias)
    middle = tokens + gate_attention * branch
    normed_feed = low(norm_modulate(middle, shift_feed, scale_feed))
    before = low_back(jnp.dot(normed_feed, up_matrix, precision=HIGHEST_PRECISION) + up_bias)
    activated = low(gelu_tanh(before))
    feed_out = low_back(jnp.dot(activated, down_matrix, precision=HIGHEST_PRECISION) + down_bias)
    return middle + gate_feed * feed_out

def forward(tokens, conditions, matrices):
    return lax.map(jax.checkpoint(partial(latent_layer, matrices)), (tokens, conditions))

def reference(latent_in, conditioning, ada_weight, qkv_weight, proj_weight, up_weight, down_weight, bias_pack, cotangent):
    matrices = (ada_weight.astype(jnp.float32).reshape(D, 6 * D), qkv_weight.astype(jnp.float32).reshape(D, 3 * D), proj_weight.astype(jnp.float32).reshape(D, D), up_weight.astype(jnp.float32).reshape(D, FF), down_weight.astype(jnp.float32).reshape(FF, D), bias_pack.astype(jnp.float32))
    result, pullback = jax.vjp(forward, latent_in.astype(jnp.float32), conditioning.astype(jnp.float32), matrices)
    grad_tokens, grad_conditions, grad_matrices = pullback(cotangent.astype(jnp.float32))
    return (result.astype(jnp.bfloat16), grad_tokens.astype(jnp.bfloat16), grad_conditions.astype(jnp.bfloat16), grad_matrices[0].reshape(-1), grad_matrices[1].reshape(-1), grad_matrices[2].reshape(-1), grad_matrices[3].reshape(-1), grad_matrices[4].reshape(-1), grad_matrices[5])
```

```python
import functools

import jax
import jax.numpy as jnp
from jax import lax
from jax.experimental import pallas as pl
from jax.experimental.pallas import tpu as pltpu
from jax.sharding import Mesh
from jax.sharding import PartitionSpec as P

H = 16
HD = 72
FF = 4608


EPS = 1e-06
GELU_COEF = 0.7978845608028654
SCALE = HD ** (-0.5)
LOG2E = 1.4426950408889634
WIN = 256
ALL = ("z", "x", "c", "y")
SWAP = [(0, 1), (1, 0)]


def norm_modulate(inputs, shift_term, scale_term):
    center = inputs - jnp.mean(inputs, axis=-1, keepdims=True)
    spread = jnp.mean(center * center, axis=-1, keepdims=True)
    return center * lax.rsqrt(spread + EPS) * (1.0 + scale_term) + shift_term


def gelu_tanh(values):
    return (
        0.5 * values * (1.0 + jnp.tanh(GELU_COEF * (values + 0.044715 * values * values * values)))
    )


def flat_term(left, right):
    product = jnp.einsum("nd,nf->df", left, right, preferred_element_type=jnp.float32).reshape(-1)
    return product


def split_heads(queries, keys_values):
    query_rows = queries.shape[0]
    key_rows = keys_values.shape[0]
    model_width = queries.shape[1]
    query_heads = queries.reshape(query_rows, H, HD)
    key_heads = keys_values[:, :model_width].reshape(key_rows, H, HD)
    value_heads = keys_values[:, model_width:].reshape(key_rows, H, HD)
    scores = jnp.einsum(
        "qhe,khe->hqk", query_heads, key_heads, preferred_element_type=jnp.float32
    ) * HD ** (-0.5)
    return (query_heads, key_heads, value_heads, scores)


def attend_latent(block_items):
    queries, keys_values = block_items
    query_heads, key_heads, value_heads, scores = split_heads(queries, keys_values)
    top_score = jnp.max(scores, axis=-1, keepdims=True)
    exp_scores = jnp.exp(scores - top_score)
    exp_total = jnp.sum(exp_scores, axis=-1, keepdims=True)
    probs_low = (exp_scores / exp_total).astype(jnp.bfloat16)
    attended = jnp.einsum(
        "hqk,khe->qhe", probs_low, value_heads, preferred_element_type=jnp.float32
    )
    return (
        attended.reshape(queries.shape[0], queries.shape[1]),
        (top_score + jnp.log(exp_total))[..., 0],
    )


def attend_back(block_items):
    queries, keys_values, log_total, d_attended = block_items
    query_rows = queries.shape[0]
    key_rows = keys_values.shape[0]
    model_width = queries.shape[1]
    query_heads, key_heads, value_heads, scores = split_heads(queries, keys_values)
    attention_probs = jnp.exp(scores - log_total[..., None])
    d_heads = d_attended.reshape(query_rows, H, HD)
    d_probs = jnp.einsum("qhe,khe->hqk", d_heads, value_heads, preferred_element_type=jnp.float32)
    centered = d_probs - jnp.sum(attention_probs * d_probs, axis=-1, keepdims=True)
    d_scores = (HD ** (-0.5) * (attention_probs * centered)).astype(jnp.bfloat16)
    d_queries = jnp.einsum("hqk,khe->qhe", d_scores, key_heads, preferred_element_type=jnp.float32)
    d_keys = jnp.einsum("hqk,qhe->khe", d_scores, query_heads, preferred_element_type=jnp.float32)
    d_values = jnp.einsum(
        "hqk,qhe->khe",
        attention_probs.astype(jnp.bfloat16),
        d_heads,
        preferred_element_type=jnp.float32,
    )
    joined = jnp.concatenate(
        [d_keys.reshape(key_rows, model_width), d_values.reshape(key_rows, model_width)], axis=1
    )
    return (d_queries.reshape(query_rows, model_width), joined)


def shape_all(gathered, model_width):
    ada_full, qkv_full, proj_full, up_full, down_full, bias_full = gathered
    return (
        ada_full.reshape(model_width, 6 * model_width),
        qkv_full.reshape(model_width, 3 * model_width),
        proj_full.reshape(model_width, model_width),
        up_full.reshape(model_width, FF),
        down_full.reshape(FF, model_width),
        bias_full.astype(jnp.float32),
    )


def head_window(head, width):
    start = jnp.minimum((head * HD) // 128, width // 128 - 2) * 128
    return pl.multiple_of(start, 128), head * HD - start


def attn_fwd_kernel(q_ref, k_ref, v_ref, *refs, tile, first):
    o_ref, lse_ref = refs[-2:]
    head = pl.program_id(0) + first
    rows, width = q_ref.shape

    if len(refs) > 2:

        @pl.when(pl.program_id(0) == 0)
        def _():
            o_ref[...] = refs[0][...]
            lse_ref[...] = refs[1][...]

    lo, off = head_window(head, width)
    lane = lax.broadcasted_iota(jnp.int32, (1, WIN), 1)
    inside = (lane >= off) & (lane < off + HD)
    keep = inside.astype(jnp.bfloat16)
    kw = k_ref[:, pl.ds(lo, WIN)]
    vw = v_ref[:, pl.ds(lo, WIN)]
    col = lax.broadcasted_iota(jnp.int32, (1, 128), 1) == head
    for t in range(rows // tile):
        r = pl.ds(t * tile, tile)
        qm = q_ref[r, pl.ds(lo, WIN)] * keep
        s = lax.dot_general(qm, kw, (((1,), (1,)), ((), ())), preferred_element_type=jnp.float32)
        top = jnp.max(s, axis=-1, keepdims=True)
        p = jnp.exp2((s - top) * (SCALE * LOG2E))
        total = jnp.sum(p, axis=-1, keepdims=True)
        o = jnp.dot(p.astype(jnp.bfloat16), vw, preferred_element_type=jnp.float32)
        o = o * (1.0 / total)
        old = o_ref[r, pl.ds(lo, WIN)].astype(jnp.float32)
        o_ref[r, pl.ds(lo, WIN)] = jnp.where(inside, o, old).astype(jnp.bfloat16)
        lse_ref[r, :] = jnp.where(col, top * SCALE + jnp.log(total), lse_ref[r, :])


def whole(array_or_shape):
    shape = array_or_shape.shape
    return pl.BlockSpec(shape, lambda h: (0,) * len(shape), pipeline_mode=pl.Buffered(1))


def attn_fwd(q, k, v, heads, into=(), tile=256):
    rows, width = q.shape
    keys = k.shape[0]
    first, count = heads
    outs = [
        jax.ShapeDtypeStruct(q.shape, jnp.bfloat16),
        jax.ShapeDtypeStruct((rows, 128), jnp.float32),
    ]
    ins = (q, k, v, *into)
    return pl.pallas_call(
        functools.partial(attn_fwd_kernel, tile=tile, first=first),
        grid=(count,),
        in_specs=[whole(a) for a in ins],
        out_specs=[whole(a) for a in outs],
        out_shape=outs,
        compiler_params=pltpu.CompilerParams(vmem_limit_bytes=40 << 20),
        cost_estimate=pl.CostEstimate(
            flops=4 * count * rows * keys * WIN,
            bytes_accessed=8 * rows * width,
            transcendentals=count * rows * keys,
        ),
        name="attention_forward",
    )(*ins)


def attn_bwd_kernel(q_ref, k_ref, v_ref, g_ref, lse_ref, *refs, tile, first):
    dq_ref, dk_ref, dv_ref = refs[-3:]
    head = pl.program_id(0) + first
    rows, width = q_ref.shape
    keys = k_ref.shape[0]

    if len(refs) > 3:

        @pl.when(pl.program_id(0) == 0)
        def _():
            dq_ref[...] = refs[0][...]
            dk_ref[...] = refs[1][...]
            dv_ref[...] = refs[2][...]

    lo, off = head_window(head, width)
    lane = lax.broadcasted_iota(jnp.int32, (1, WIN), 1)
    inside = (lane >= off) & (lane < off + HD)
    keep = inside.astype(jnp.bfloat16)
    kw = k_ref[:, pl.ds(lo, WIN)]
    vw = v_ref[:, pl.ds(lo, WIN)]
    ktw = kw.T
    dk = jnp.zeros((keys, WIN), jnp.float32)
    dv = jnp.zeros((keys, WIN), jnp.float32)
    for t in range(rows // tile):
        r = pl.ds(t * tile, tile)
        lse = lse_ref[pl.ds(head, 1), r]
        qw = q_ref[r, pl.ds(lo, WIN)]
        gw = g_ref[r, pl.ds(lo, WIN)]
        st = jnp.dot(kw, (qw * keep).T, preferred_element_type=jnp.float32)
        pt = jnp.exp2(st * (SCALE * LOG2E) - lse * LOG2E)
        dpt = jnp.dot(vw, (gw * keep).T, preferred_element_type=jnp.float32)
        delta = jnp.sum(pt * dpt, axis=0, keepdims=True)
        dst = (pt * (dpt - delta) * SCALE).astype(jnp.bfloat16)
        dv = dv + jnp.dot(pt.astype(jnp.bfloat16), gw, preferred_element_type=jnp.float32)
        dk = dk + jnp.dot(dst, qw, preferred_element_type=jnp.float32)
        dq = jnp.dot(ktw, dst, preferred_element_type=jnp.float32).T
        old = dq_ref[r, pl.ds(lo, WIN)].astype(jnp.float32)
        dq_ref[r, pl.ds(lo, WIN)] = jnp.where(inside, dq, old).astype(jnp.bfloat16)
    old = dk_ref[:, pl.ds(lo, WIN)].astype(jnp.float32)
    dk_ref[:, pl.ds(lo, WIN)] = jnp.where(inside, dk, old).astype(jnp.bfloat16)
    old = dv_ref[:, pl.ds(lo, WIN)].astype(jnp.float32)
    dv_ref[:, pl.ds(lo, WIN)] = jnp.where(inside, dv, old).astype(jnp.bfloat16)


def attn_bwd(q, k, v, g, lse_rows, heads, into=(), tile=512):
    rows, width = q.shape
    keys = k.shape[0]
    first, count = heads
    outs = [jax.ShapeDtypeStruct(a.shape, jnp.bfloat16) for a in (q, k, v)]
    ins = (q, k, v, g, lse_rows, *into)
    return pl.pallas_call(
        functools.partial(attn_bwd_kernel, tile=tile, first=first),
        grid=(count,),
        in_specs=[whole(a) for a in ins],
        out_specs=[whole(a) for a in outs],
        out_shape=outs,
        compiler_params=pltpu.CompilerParams(vmem_limit_bytes=52 << 20),
        cost_estimate=pl.CostEstimate(
            flops=10 * count * rows * keys * WIN,
            bytes_accessed=14 * rows * width,
            transcendentals=count * rows * keys,
        ),
        name="attention_backward",
    )(*ins)


def after(array, *earlier):
    return lax.optimization_barrier((array, earlier))[0]


def assemble(pieces, places, where, kind, height):
    width = pieces[0].shape[-1]
    blocks = [(i, b) for i, piece in enumerate(pieces) for b in range(piece.shape[0])]

    def body(where_ref, *refs):
        ins, out = refs[: len(pieces)], refs[len(pieces)]
        held, arrived, left = refs[len(pieces) + 1 :]
        zi = where_ref[0]
        loads, stores = [], []
        start = 0
        for piece, (first, x_bit, c_bit, y_bit, offset) in zip(ins, places):
            xi = where_ref[1] if x_bit == 0 else 1 - where_ref[1]
            ci = where_ref[2] if c_bit == 0 else 1 - where_ref[2]
            yi = where_ref[3] if y_bit == 0 else 1 - where_ref[3]
            size = piece.shape[1]
            for block in range(piece.shape[0]):
                slot = start + block
                row = ((zi ^ (first + block)) * 2 + xi) * height + offset
                quarter = (ci * 2 + yi) * (8 * height)
                if kind == "columns":
                    rows = pl.ds(pl.multiple_of(row, 16), size)
                    quarter = (ci * 2 + yi) * width
                    target = out.at[rows, pl.ds(pl.multiple_of(quarter, 128), width)]
                else:
                    target = out.at[pl.ds(pl.multiple_of(quarter + row, 16), size), :]
                here = held.at[slot, pl.ds(0, size)]
                loads.append(pltpu.make_async_copy(piece.at[block], here, arrived.at[slot]))
                stores.append(pltpu.make_async_copy(here, target, left.at[slot]))
            start += piece.shape[0]
        for load in loads:
            load.start()
        for load, store in zip(loads, stores):
            load.wait()
            store.start()
        for store in stores:
            store.wait()

    shape = (8 * height, 4 * width) if kind == "columns" else (32 * height, width)
    tallest = max(piece.shape[1] for piece in pieces)
    return pl.pallas_call(
        body,
        grid_spec=pltpu.PrefetchScalarGridSpec(
            num_scalar_prefetch=1,
            grid=(1,),
            in_specs=[pl.BlockSpec(memory_space=pl.ANY)] * len(pieces),
            out_specs=pl.BlockSpec(memory_space=pl.ANY),
            scratch_shapes=[
                pltpu.VMEM((len(blocks), tallest, width), pieces[0].dtype),
                pltpu.SemaphoreType.DMA((len(blocks),)),
                pltpu.SemaphoreType.DMA((len(blocks),)),
            ],
        ),
        out_shape=jax.ShapeDtypeStruct(shape, pieces[0].dtype),
        compiler_params=pltpu.CompilerParams(vmem_limit_bytes=20 << 20),
        cost_estimate=pl.CostEstimate(
            flops=0, bytes_accessed=4 * shape[0] * shape[1], transcendentals=0
        ),
        name="assemble_" + kind,
    )(where, *pieces)


def swap(array, axis):
    return lax.ppermute(array, axis, SWAP)


def line_gather(unit):
    hops = [lax.ppermute(unit, "z", [(i, i ^ step) for i in range(4)]) for step in range(1, 4)]
    return jnp.stack([unit] + hops)


def plane_gather(line):
    return swap(line, "x"), swap(line, "y")


def corner_gather(from_x, from_y):
    return swap(from_x[:2], "y"), swap(from_y[2:], "x")


PLACES = [(0, 0, 0, 0), (0, 1, 0, 0), (0, 0, 0, 1), (0, 1, 0, 1), (2, 1, 0, 1)]


def with_core(pieces, others, offset=0):
    places = [(first, x, c, y, offset) for first, x, c, y in PLACES]
    places += [(first, x, 1 - c, y, offset) for first, x, c, y in PLACES]
    return list(pieces) + list(others), places


def add_low(*terms):
    total = terms[0].astype(jnp.float32)
    for term in terms[1:]:
        total = total + term.astype(jnp.float32)
    return total.astype(jnp.bfloat16)


def part_columns(half, yy, xx):
    width = half.shape[1] // 2
    cut = lax.dynamic_slice(
        half.reshape(4, 2, 144, 2 * width), (0, xx, 0, yy * width), (4, 1, 144, width)
    )
    return cut.reshape(4, 144, width)


def part_rows(half, yy, xx):
    width = half.shape[1]
    cut = lax.dynamic_slice(
        half.reshape(2, 4, 2, 144, width), (yy, 0, xx, 0, 0), (1, 4, 1, 144, width)
    )
    return cut.reshape(4, 144, width)


class ScatterSum:
    def __init__(self, part, xi, yi, zi):
        self.part, self.xi, self.yi, self.zi = part, xi, yi, zi

    def corner(self, half):
        self.half = half
        corner = self.part(half, 1 - self.yi, 1 - self.xi)
        self.low, self.high = swap(corner[:2], "x"), swap(corner[2:], "y")
        return self.low, self.high

    def plane(self, *earlier):
        half = after(self.half, *earlier) if earlier else self.half
        to_y, to_x = self.part(half, 1 - self.yi, self.xi), self.part(half, self.yi, 1 - self.xi)
        to_y = jnp.concatenate([add_low(to_y[:2], self.low), to_y[2:]])
        to_x = jnp.concatenate([to_x[:2], add_low(to_x[2:], self.high)])
        self.from_y, self.from_x = swap(to_y, "y"), swap(to_x, "x")
        return self.from_y, self.from_x

    def line(self, *earlier):
        half = after(self.half, *earlier) if earlier else self.half
        own = add_low(self.part(half, self.yi, self.xi), self.from_y, self.from_x)
        self.own = lax.dynamic_index_in_dim(own, self.zi, 0, False)
        self.hops = []
        for step in range(1, 4):
            block = lax.dynamic_index_in_dim(own, self.zi ^ step, 0, False)
            self.hops.append(lax.ppermute(block, "z", [(i, i ^ step) for i in range(4)]))
        return self.hops

    def total(self):
        total = self.own.astype(jnp.float32)
        for hop in self.hops:
            total = total + hop.astype(jnp.float32)
        return total


def local_pairs(
    latent_in,
    conditioning,
    ada_weight,
    qkv_weight,
    proj_weight,
    up_weight,
    down_weight,
    bias_pack,
    cotangent,
):
    width = latent_in.shape[2]
    half_rows = latent_in.shape[1]
    zi, xi, ci, yi = [lax.axis_index(name) for name in ALL]
    device = ((zi * 2 + xi) * 2 + ci) * 2 + yi
    where = jnp.stack([zi, xi, ci, yi]).astype(jnp.int32)
    rows = width // 32

    def whole_latent(array):
        own = lax.dynamic_index_in_dim(array, yi, 0, False)
        other = lax.dynamic_index_in_dim(array, 1 - yi, 0, False)
        return jnp.concatenate([own, swap(other, "y")])

    def half_latents(array):
        back = swap(array[half_rows:], "y")
        own = array[:half_rows]
        first = jnp.where(yi == 0, own, back)
        second = jnp.where(yi == 0, back, own)
        return jnp.stack([first, second])

    def exchange(array):
        return lax.all_to_all(array, ALL, 0, 0, tiled=True)

    def to_all(vector):
        return exchange(jnp.broadcast_to(vector, (32,) + vector.shape))

    def over_tokens(left, right):
        return lax.dot_general(
            left, right, (((0,), (0,)), ((), ())), preferred_element_type=jnp.float32
        )

    def times_transposed(left, right):
        return lax.dot_general(
            left, right, (((1,), (1,)), ((), ())), preferred_element_type=jnp.float32
        )

    qkv_rows = qkv_weight.reshape(rows, 3 * width)
    quarters = jnp.stack(
        [qkv_rows[:, i * width : (i + 1) * width] for i in range(3)]
        + [proj_weight.reshape(rows, width)]
    )
    unit_a = lax.all_to_all(quarters, ("c", "y"), 0, 0, tiled=True).reshape(4 * rows, width)
    line_a0 = line_gather(unit_a[:64])
    line_a1 = line_gather(after(unit_a[64:], line_a0))
    own_condition = lax.dynamic_index_in_dim(conditioning, yi, 0, False)
    small = to_all(jnp.concatenate([bias_pack, own_condition]))
    bias_share = bias_pack.shape[0]
    biases = small[:, :bias_share].reshape(-1).astype(jnp.float32)
    conditions = small[:, bias_share:].astype(jnp.float32)
    tokens_low = whole_latent(latent_in)
    silu_all = jax.nn.silu(conditions).astype(jnp.bfloat16)
    silu_cut = lax.dynamic_slice(silu_all, (0, device * rows), (32, rows))
    ada_rows = ada_weight.reshape(rows, 6 * width)
    shares = exchange(jnp.dot(silu_cut, ada_rows, preferred_element_type=jnp.float32))
    modulations = jnp.sum(shares, axis=0, keepdims=True) + biases[: 6 * width]
    shift_attention, scale_attention, gate_attention, shift_feed, scale_feed, gate_feed = jnp.split(
        modulations, 6, axis=1
    )

    up_quarters = up_weight.reshape(rows, 8, 4, 144).transpose(2, 0, 1, 3).reshape(4, rows, width)
    unit_u = lax.all_to_all(after(up_quarters, unit_a), ("c", "y"), 0, 0, tiled=True)
    unit_u = unit_u.reshape(4 * rows, width)
    unit_d = down_weight.reshape(4 * rows, width)

    plane_a0 = plane_gather(line_a0)
    core_a0 = [swap(p, "c") for p in (line_a0, *plane_a0)]
    line_u = line_gather(after(unit_u, line_a1))
    corner_a0 = corner_gather(*plane_a0)
    plane_a1 = plane_gather(after(line_a1, *plane_a0))
    core_a0 += [swap(p, "c") for p in corner_a0]
    core_a1 = [swap(p, "c") for p in (line_a1, *plane_a1)]
    corner_a1 = corner_gather(*plane_a1)
    core_a1 += [swap(p, "c") for p in corner_a1]
    pieces_0, places_0 = with_core((line_a0, *plane_a0, *corner_a0), core_a0)
    pieces_1, places_1 = with_core((line_a1, *plane_a1, *corner_a1), core_a1, 64)
    attention_matrix = assemble(
        pieces_0 + pieces_1, places_0 + places_1, where, "columns", 4 * rows
    )
    plane_u = plane_gather(after(line_u, *corner_a1))
    line_d = line_gather(after(unit_d, line_u))
    qkv_matrix = attention_matrix[:, : 3 * width]
    proj_matrix = attention_matrix[:, 3 * width :]

    query_bias = biases[6 * width : 7 * width]
    value_bias = biases[7 * width : 8 * width]
    proj_bias = biases[8 * width : 9 * width]
    up_bias = biases[9 * width : 9 * width + FF].reshape(8, 4, 144).transpose(1, 0, 2).reshape(-1)
    down_bias = biases[9 * width + FF :]

    tokens = tokens_low.astype(jnp.float32)
    normed = norm_modulate(tokens, shift_attention, scale_attention).astype(jnp.bfloat16)
    projected = jnp.dot(normed, qkv_matrix, preferred_element_type=jnp.float32)
    queries = (projected[:, :width] + query_bias).astype(jnp.bfloat16)
    keys = projected[:, width : 2 * width].astype(jnp.bfloat16)
    values = (projected[:, 2 * width :] + value_bias).astype(jnp.bfloat16)
    part_one = attn_fwd(queries, keys, values, (0, 8))

    plane_u = [after(p, *part_one) for p in plane_u]
    corner_u = corner_gather(*plane_u)
    core_u = [swap(p, "c") for p in (after(line_u, *part_one), *plane_u)]
    plane_d = plane_gather(after(line_d, *plane_u))
    upstream_low = whole_latent(after(cotangent, *part_one))

    attended, log_total = attn_fwd(queries, keys, values, (8, 8), tuple(part_one))
    corner_u = [after(p, attended) for p in corner_u]
    core_u += [swap(p, "c") for p in corner_u]
    branch = jnp.dot(attended, proj_matrix, preferred_element_type=jnp.float32) + proj_bias
    middle = tokens + gate_attention * branch
    normed_feed = norm_modulate(middle, shift_feed, scale_feed).astype(jnp.bfloat16)
    pieces, places = with_core((line_u, *plane_u, *corner_u), core_u)
    up_matrix = assemble(
        [after(p, normed_feed) for p in pieces], places, where, "columns", 4 * rows
    )
    plane_d = [after(p, up_matrix) for p in plane_d]
    corner_d = corner_gather(*plane_d)
    core_d = [swap(p, "c") for p in (after(line_d, up_matrix), *plane_d)]

    before = jnp.dot(normed_feed, up_matrix, preferred_element_type=jnp.float32) + up_bias
    activated = gelu_tanh(before).astype(jnp.bfloat16)
    corner_d = [after(p, activated) for p in corner_d]
    core_d += [swap(p, "c") for p in corner_d]
    pieces, places = with_core((line_d, *plane_d, *corner_d), core_d)
    down_matrix = assemble(
        [after(p, activated) for p in pieces], places, where, "rows", 4 * rows
    )
    upstream = upstream_low.astype(jnp.float32)
    d_feed = (gate_feed * upstream).astype(jnp.bfloat16)

    def pick(array, core):
        return lax.dynamic_slice_in_dim(array, core * 2 * width, 2 * width, 1)

    down_sent = over_tokens(pick(activated, 1 - ci), d_feed).astype(jnp.bfloat16)
    down_received = swap(down_sent, "c")
    feed_out = jnp.dot(
        after(activated, down_sent), down_matrix, preferred_element_type=jnp.float32
    )
    feed_out = feed_out + down_bias
    output_low = (middle + gate_feed * feed_out).astype(jnp.bfloat16)
    d_gate_feed = jnp.sum(upstream * feed_out, axis=0, keepdims=True)
    down_half = over_tokens(pick(after(activated, output_low), ci), d_feed)
    down_half = add_low(down_half, down_received)
    down_scatter = ScatterSum(part_rows, xi, yi, zi)
    down_scatter.corner(down_half)
    output = half_latents(after(output_low, down_half))

    d_activated = times_transposed(after(d_feed, down_half), down_matrix)
    unused_gelu, gelu_pull = jax.vjp(gelu_tanh, before)
    d_before = gelu_pull(d_activated)[0].astype(jnp.bfloat16)
    down_scatter.plane(d_before)
    up_sent = over_tokens(normed_feed, pick(d_before, 1 - ci)).astype(jnp.bfloat16)
    up_received = swap(up_sent, "c")
    d_normed_feed = times_transposed(after(d_before, up_sent), up_matrix)
    up_half = over_tokens(normed_feed, pick(after(d_before, d_normed_feed), ci))
    up_half = add_low(up_half, up_received)
    up_scatter = ScatterSum(part_columns, xi, yi, zi)
    up_scatter.corner(up_half)
    down_scatter.line(up_half)
    unused_norm, norm_pull = jax.vjp(norm_modulate, middle, shift_feed, scale_feed)
    d_middle_part, d_shift_feed, d_scale_feed = norm_pull(after(d_normed_feed, up_half))
    d_middle = upstream + d_middle_part
    d_gate_attention = jnp.sum(d_middle * branch, axis=0, keepdims=True)
    d_branch = (gate_attention * d_middle).astype(jnp.bfloat16)
    d_attended = times_transposed(d_branch, proj_matrix).astype(jnp.bfloat16)
    up_scatter.plane(d_attended)
    log_rows = log_total[:, :H].T
    part_one = attn_bwd(
        queries, keys, values, after(d_attended, up_scatter.half), log_rows, (0, 8)
    )
    up_scatter.line(*part_one)
    d_queries, d_keys, d_values = attn_bwd(
        queries, keys, values, d_attended, log_rows, (8, 8), tuple(part_one)
    )
    proj_grad = over_tokens(attended, d_branch)
    d_projected = jnp.concatenate([d_queries, d_keys, d_values], axis=1)
    qkv_grad = over_tokens(normed, d_projected)
    first_half = qkv_grad[:, : 2 * width]
    second_half = jnp.concatenate([qkv_grad[:, 2 * width :], proj_grad], axis=1)
    sent = jnp.where(ci == 0, second_half, first_half).astype(jnp.bfloat16)
    received = swap(sent, "c")
    d_normed = times_transposed(after(d_projected, sent), qkv_matrix)
    attention_half = add_low(jnp.where(ci == 0, first_half, second_half), received)
    attention_scatter = ScatterSum(part_columns, xi, yi, zi)
    attention_scatter.corner(attention_half)
    unused_first, first_pull = jax.vjp(norm_modulate, tokens, shift_attention, scale_attention)
    d_tokens_part, d_shift_attention, d_scale_attention = first_pull(d_normed)
    grad_low = (d_middle + d_tokens_part).astype(jnp.bfloat16)
    attention_scatter.plane()
    attention_scatter.line()

    d_mods = jnp.concatenate(
        [
            d_shift_attention,
            d_scale_attention,
            d_gate_attention,
            d_shift_feed,
            d_scale_feed,
            d_gate_feed,
        ],
        axis=1,
    ).astype(jnp.bfloat16)
    every_mods = to_all(d_mods[0])
    grad_input = half_latents(grad_low)
    grad_ada = over_tokens(silu_cut, every_mods).reshape(-1)
    d_silu_rows = times_transposed(every_mods, ada_rows)
    d_silu = exchange(jnp.repeat(d_silu_rows.reshape(16, 1, 2, rows), 2, axis=1).reshape(32, 2, rows))
    d_silu = d_silu.transpose(1, 0, 2).reshape(2, width)
    unused_silu, silu_pull = jax.vjp(jax.nn.silu, conditioning.astype(jnp.float32))
    grad_cond = silu_pull(d_silu)[0].astype(jnp.bfloat16)

    up_bias_grad = jnp.sum(d_before, axis=0, dtype=jnp.float32)
    bias_terms = jnp.concatenate(
        [
            d_mods[0].astype(jnp.float32),
            jnp.sum(d_queries, axis=0, dtype=jnp.float32),
            jnp.sum(d_values, axis=0, dtype=jnp.float32),
            jnp.sum(d_branch, axis=0, dtype=jnp.float32),
            up_bias_grad.reshape(4, 8, 144).transpose(1, 0, 2).reshape(-1),
            jnp.sum(d_feed, axis=0, dtype=jnp.float32),
        ]
    )
    grad_bias = jnp.sum(exchange(bias_terms.reshape(32, -1)), axis=0)

    up_sum = up_scatter.total().reshape(4, rows, width)
    up_sum = lax.all_to_all(up_sum, ("c", "y"), 0, 0, tiled=True)
    grad_up = up_sum.reshape(4, rows, 8, 144).transpose(1, 2, 0, 3).reshape(-1)
    grad_down = down_scatter.total().reshape(-1)
    sums = attention_scatter.total().reshape(4, rows, width)
    sums = lax.all_to_all(sums, ("c", "y"), 0, 0, tiled=True)
    grad_qkv = jnp.concatenate([sums[0], sums[1], sums[2]], axis=1).reshape(-1)
    grad_proj = sums[3].reshape(-1)
    return (
        output,
        grad_input,
        grad_cond,
        grad_ada,
        grad_qkv,
        grad_proj,
        grad_up,
        grad_down,
        grad_bias,
    )


def local_any(
    latent_in,
    conditioning,
    ada_weight,
    qkv_weight,
    proj_weight,
    up_weight,
    down_weight,
    bias_pack,
    cotangent,
):
    model_width = latent_in.shape[2]
    every_param = (
        lax.all_gather(ada_weight, ("batch", "seq"), axis=0, tiled=True),
        lax.all_gather(qkv_weight, ("batch", "seq"), axis=0, tiled=True),
        lax.all_gather(proj_weight, ("batch", "seq"), axis=0, tiled=True),
        lax.all_gather(up_weight, ("batch", "seq"), axis=0, tiled=True),
        lax.all_gather(down_weight, ("batch", "seq"), axis=0, tiled=True),
        lax.all_gather(bias_pack, ("batch", "seq"), axis=0, tiled=True),
    )
    ada_matrix, qkv_matrix, proj_matrix, up_matrix, down_matrix, biases = shape_all(
        every_param, model_width
    )
    ada_bias = biases[: 6 * model_width]
    query_bias = biases[6 * model_width : 7 * model_width]
    value_bias = biases[7 * model_width : 8 * model_width]
    proj_bias = biases[8 * model_width : 9 * model_width]
    up_bias = biases[9 * model_width : 9 * model_width + FF]
    down_bias = biases[9 * model_width + FF :]
    tokens = latent_in.astype(jnp.float32)
    conditions = conditioning.astype(jnp.float32)
    silu_cond = jax.nn.silu(conditions).astype(jnp.bfloat16)
    modulations = jnp.dot(silu_cond, ada_matrix, preferred_element_type=jnp.float32) + ada_bias
    shift_attention, scale_attention, gate_attention, shift_feed, scale_feed, gate_feed = jnp.split(
        modulations[:, None, :], 6, axis=2
    )
    normed = norm_modulate(tokens, shift_attention, scale_attention).astype(jnp.bfloat16)
    projected = jnp.einsum("btd,df->btf", normed, qkv_matrix, preferred_element_type=jnp.float32)
    queries = (projected[..., :model_width] + query_bias).astype(jnp.bfloat16)
    own_keys = jnp.concatenate(
        [
            projected[..., model_width : 2 * model_width],
            projected[..., 2 * model_width :] + value_bias,
        ],
        axis=2,
    ).astype(jnp.bfloat16)
    every_keys = lax.all_gather(own_keys, "seq", axis=1, tiled=True)
    attended, log_total = lax.map(attend_latent, (queries, every_keys))
    attended = attended.astype(jnp.bfloat16)
    branch = (
        jnp.einsum("btd,de->bte", attended, proj_matrix, preferred_element_type=jnp.float32)
        + proj_bias
    )
    middle = tokens + gate_attention * branch
    normed_feed = norm_modulate(middle, shift_feed, scale_feed).astype(jnp.bfloat16)
    before = (
        jnp.einsum("btd,df->btf", normed_feed, up_matrix, preferred_element_type=jnp.float32)
        + up_bias
    )
    activated = gelu_tanh(before).astype(jnp.bfloat16)
    feed_out = (
        jnp.einsum("btf,fd->btd", activated, down_matrix, preferred_element_type=jnp.float32)
        + down_bias
    )
    output = (middle + gate_feed * feed_out).astype(jnp.bfloat16)
    param_again = (
        lax.all_gather(ada_weight, ("batch", "seq"), axis=0, tiled=True),
        lax.all_gather(qkv_weight, ("batch", "seq"), axis=0, tiled=True),
        lax.all_gather(proj_weight, ("batch", "seq"), axis=0, tiled=True),
        lax.all_gather(up_weight, ("batch", "seq"), axis=0, tiled=True),
        lax.all_gather(down_weight, ("batch", "seq"), axis=0, tiled=True),
        lax.all_gather(bias_pack, ("batch", "seq"), axis=0, tiled=True),
    )
    ada_matrix, qkv_matrix, proj_matrix, up_matrix, down_matrix, biases = shape_all(
        param_again, model_width
    )
    upstream = cotangent.astype(jnp.float32)
    d_gate_feed = jnp.sum(upstream * feed_out, axis=1, keepdims=True)
    d_feed = (gate_feed * upstream).astype(jnp.bfloat16)
    d_activated = jnp.einsum("btd,fd->btf", d_feed, down_matrix, preferred_element_type=jnp.float32)
    unused_gelu, gelu_pull = jax.vjp(gelu_tanh, before)
    d_before = gelu_pull(d_activated)[0].astype(jnp.bfloat16)
    d_normed_feed = jnp.einsum(
        "btf,df->btd", d_before, up_matrix, preferred_element_type=jnp.float32
    )
    unused_norm, norm_pull = jax.vjp(norm_modulate, middle, shift_feed, scale_feed)
    d_middle_part, d_shift_feed, d_scale_feed = norm_pull(d_normed_feed)
    d_middle = upstream + d_middle_part
    d_gate_attention = jnp.sum(d_middle * branch, axis=1, keepdims=True)
    d_branch = (gate_attention * d_middle).astype(jnp.bfloat16)
    d_attended = jnp.einsum(
        "bte,de->btd", d_branch, proj_matrix, preferred_element_type=jnp.float32
    ).astype(jnp.bfloat16)
    d_queries, d_every = lax.map(attend_back, (queries, every_keys, log_total, d_attended))
    d_queries = d_queries.astype(jnp.bfloat16)
    d_own = lax.psum_scatter(d_every.astype(jnp.bfloat16), "seq", scatter_dimension=1, tiled=True)
    d_projected = jnp.concatenate([d_queries, d_own], axis=2)
    d_normed = jnp.einsum(
        "btf,df->btd", d_projected, qkv_matrix, preferred_element_type=jnp.float32
    )
    unused_first, first_pull = jax.vjp(norm_modulate, tokens, shift_attention, scale_attention)
    d_tokens_part, d_shift_attention, d_scale_attention = first_pull(d_normed)
    grad_input = (d_middle + d_tokens_part).astype(jnp.bfloat16)
    local_mods = jnp.concatenate(
        [
            d_shift_attention,
            d_scale_attention,
            d_gate_attention,
            d_shift_feed,
            d_scale_feed,
            d_gate_feed,
        ],
        axis=2,
    )[:, 0, :]
    d_mods = lax.psum(local_mods.astype(jnp.bfloat16), "seq")
    d_silu = jnp.einsum("bf,df->bd", d_mods, ada_matrix, preferred_element_type=jnp.float32)
    unused_silu, silu_pull = jax.vjp(jax.nn.silu, conditions)
    grad_cond = silu_pull(d_silu)[0].astype(jnp.bfloat16)
    is_owner = lax.axis_index("seq") == 0
    owned_mods = jnp.where(is_owner, d_mods, jnp.zeros_like(d_mods))
    bias_terms = jnp.concatenate(
        [
            jnp.sum(owned_mods, axis=0, dtype=jnp.float32),
            jnp.sum(d_queries, axis=(0, 1), dtype=jnp.float32),
            jnp.sum(d_own[..., model_width:], axis=(0, 1), dtype=jnp.float32),
            jnp.sum(d_branch, axis=(0, 1), dtype=jnp.float32),
            jnp.sum(d_before, axis=(0, 1), dtype=jnp.float32),
            jnp.sum(d_feed, axis=(0, 1), dtype=jnp.float32),
        ]
    )
    matrix_terms = [
        (silu_cond, owned_mods, ada_weight.shape[0]),
        (
            normed.reshape(-1, model_width),
            d_projected.reshape(-1, 3 * model_width),
            qkv_weight.shape[0],
        ),
        (
            attended.reshape(-1, model_width),
            d_branch.reshape(-1, model_width),
            proj_weight.shape[0],
        ),
        (normed_feed.reshape(-1, model_width), d_before.reshape(-1, FF), up_weight.shape[0]),
        (activated.reshape(-1, FF), d_feed.reshape(-1, model_width), down_weight.shape[0]),
    ]
    bias_share = bias_pack.shape[0]
    shard_rows = sum((entry[2] for entry in matrix_terms)) + bias_share
    block_count = shard_rows * lax.axis_size(("batch", "seq")) // shard_rows
    pieces = []
    for left, right, grad_shard_size in matrix_terms:
        pieces.append(flat_term(left, right).reshape(block_count, grad_shard_size))
    pieces.append(bias_terms.reshape(block_count, bias_share))
    owned_grads = lax.psum_scatter(
        jnp.concatenate(pieces, axis=1).reshape(-1),
        ("batch", "seq"),
        scatter_dimension=0,
        tiled=True,
    )
    results = []
    cursor = 0
    for shard_size in [entry[2] for entry in matrix_terms] + [bias_share]:
        results.append(owned_grads[cursor : cursor + shard_size])
        cursor = cursor + shard_size
    grad_ada, grad_qkv, grad_proj, grad_up, grad_down, grad_bias = results
    return (
        output,
        grad_input,
        grad_cond,
        grad_ada,
        grad_qkv,
        grad_proj,
        grad_up,
        grad_down,
        grad_bias,
    )


def solution(mesh):
    batch, seq = mesh.shape["batch"], mesh.shape["seq"]
    if (batch, seq) == (16, 2):
        inner = Mesh(mesh.devices.reshape(4, 2, 2, 2), ALL)
        body, tokens = local_pairs, ("z", "x", "c")
        flat, split = P(ALL), "y"
    else:
        inner, body, tokens, split = mesh, local_any, "batch", "seq"
        flat = P(("batch", "seq"))
    activations = P(tokens, split, None)
    vectors = P(tokens, None)
    in_specs = (activations, vectors) + (flat,) * 6 + (activations,)
    out_specs = (activations, activations, vectors) + (flat,) * 6
    return jax.shard_map(body, mesh=inner, in_specs=in_specs, out_specs=out_specs, check_vma=False)
```

```python
import functools
import itertools

import jax
import jax.numpy as jnp
from jax import lax
from jax.experimental import pallas as pl
from jax.experimental.pallas import tpu as pltpu
from jax.sharding import Mesh
from jax.sharding import PartitionSpec as P

H = 16
HD = 72
FF = 4608


EPS = 1e-06
GELU_COEF = 0.7978845608028654
SCALE = HD ** (-0.5)
LOG2E = 1.4426950408889634
WIN = 256
ALL = ("z", "x", "c", "y")
SWAP = [(0, 1), (1, 0)]


def norm_modulate(inputs, shift_term, scale_term):
    center = inputs - jnp.mean(inputs, axis=-1, keepdims=True)
    spread = jnp.mean(center * center, axis=-1, keepdims=True)
    return center * lax.rsqrt(spread + EPS) * (1.0 + scale_term) + shift_term


def gelu_tanh(values):
    return (
        0.5 * values * (1.0 + jnp.tanh(GELU_COEF * (values + 0.044715 * values * values * values)))
    )


def flat_term(left, right):
    product = jnp.einsum("nd,nf->df", left, right, preferred_element_type=jnp.float32).reshape(-1)
    return product


def split_heads(queries, keys_values):
    query_rows = queries.shape[0]
    key_rows = keys_values.shape[0]
    model_width = queries.shape[1]
    query_heads = queries.reshape(query_rows, H, HD)
    key_heads = keys_values[:, :model_width].reshape(key_rows, H, HD)
    value_heads = keys_values[:, model_width:].reshape(key_rows, H, HD)
    scores = jnp.einsum(
        "qhe,khe->hqk", query_heads, key_heads, preferred_element_type=jnp.float32
    ) * HD ** (-0.5)
    return (query_heads, key_heads, value_heads, scores)


def attend_latent(block_items):
    queries, keys_values = block_items
    query_heads, key_heads, value_heads, scores = split_heads(queries, keys_values)
    top_score = jnp.max(scores, axis=-1, keepdims=True)
    exp_scores = jnp.exp(scores - top_score)
    exp_total = jnp.sum(exp_scores, axis=-1, keepdims=True)
    probs_low = (exp_scores / exp_total).astype(jnp.bfloat16)
    attended = jnp.einsum(
        "hqk,khe->qhe", probs_low, value_heads, preferred_element_type=jnp.float32
    )
    return (
        attended.reshape(queries.shape[0], queries.shape[1]),
        (top_score + jnp.log(exp_total))[..., 0],
    )


def attend_back(block_items):
    queries, keys_values, log_total, d_attended = block_items
    query_rows = queries.shape[0]
    key_rows = keys_values.shape[0]
    model_width = queries.shape[1]
    query_heads, key_heads, value_heads, scores = split_heads(queries, keys_values)
    attention_probs = jnp.exp(scores - log_total[..., None])
    d_heads = d_attended.reshape(query_rows, H, HD)
    d_probs = jnp.einsum("qhe,khe->hqk", d_heads, value_heads, preferred_element_type=jnp.float32)
    centered = d_probs - jnp.sum(attention_probs * d_probs, axis=-1, keepdims=True)
    d_scores = (HD ** (-0.5) * (attention_probs * centered)).astype(jnp.bfloat16)
    d_queries = jnp.einsum("hqk,khe->qhe", d_scores, key_heads, preferred_element_type=jnp.float32)
    d_keys = jnp.einsum("hqk,qhe->khe", d_scores, query_heads, preferred_element_type=jnp.float32)
    d_values = jnp.einsum(
        "hqk,qhe->khe",
        attention_probs.astype(jnp.bfloat16),
        d_heads,
        preferred_element_type=jnp.float32,
    )
    joined = jnp.concatenate(
        [d_keys.reshape(key_rows, model_width), d_values.reshape(key_rows, model_width)], axis=1
    )
    return (d_queries.reshape(query_rows, model_width), joined)


def shape_all(gathered, model_width):
    ada_full, qkv_full, proj_full, up_full, down_full, bias_full = gathered
    return (
        ada_full.reshape(model_width, 6 * model_width),
        qkv_full.reshape(model_width, 3 * model_width),
        proj_full.reshape(model_width, model_width),
        up_full.reshape(model_width, FF),
        down_full.reshape(FF, model_width),
        bias_full.astype(jnp.float32),
    )


def head_window(head, width):
    start = jnp.minimum((head * HD) // 128, width // 128 - 2) * 128
    return pl.multiple_of(start, 128), head * HD - start


def attn_fwd_kernel(q_ref, k_ref, v_ref, *refs, tile, first):
    o_ref, lse_ref = refs[-2:]
    head = pl.program_id(0) + first
    rows, width = q_ref.shape

    if len(refs) > 2:

        @pl.when(pl.program_id(0) == 0)
        def _():
            o_ref[...] = refs[0][...]
            lse_ref[...] = refs[1][...]

    lo, off = head_window(head, width)
    lane = lax.broadcasted_iota(jnp.int32, (1, WIN), 1)
    inside = (lane >= off) & (lane < off + HD)
    keep = inside.astype(jnp.bfloat16)
    kw = k_ref[:, pl.ds(lo, WIN)]
    vw = v_ref[:, pl.ds(lo, WIN)]
    col = lax.broadcasted_iota(jnp.int32, (1, 128), 1) == head
    for t in range(rows // tile):
        r = pl.ds(t * tile, tile)
        qm = q_ref[r, pl.ds(lo, WIN)] * keep
        s = lax.dot_general(qm, kw, (((1,), (1,)), ((), ())), preferred_element_type=jnp.float32)
        top = jnp.max(s, axis=-1, keepdims=True)
        p = jnp.exp2((s - top) * (SCALE * LOG2E))
        total = jnp.sum(p, axis=-1, keepdims=True)
        o = jnp.dot(p.astype(jnp.bfloat16), vw, preferred_element_type=jnp.float32)
        o = o * (1.0 / total)
        old = o_ref[r, pl.ds(lo, WIN)].astype(jnp.float32)
        o_ref[r, pl.ds(lo, WIN)] = jnp.where(inside, o, old).astype(jnp.bfloat16)
        lse_ref[r, :] = jnp.where(col, top * SCALE + jnp.log(total), lse_ref[r, :])


def whole(array_or_shape):
    shape = array_or_shape.shape
    return pl.BlockSpec(shape, lambda h: (0,) * len(shape), pipeline_mode=pl.Buffered(1))


def attn_fwd(q, k, v, heads, into=(), tile=256):
    rows, width = q.shape
    keys = k.shape[0]
    first, count = heads
    outs = [
        jax.ShapeDtypeStruct(q.shape, jnp.bfloat16),
        jax.ShapeDtypeStruct((rows, 128), jnp.float32),
    ]
    ins = (q, k, v, *into)
    return pl.pallas_call(
        functools.partial(attn_fwd_kernel, tile=tile, first=first),
        grid=(count,),
        in_specs=[whole(a) for a in ins],
        out_specs=[whole(a) for a in outs],
        out_shape=outs,
        compiler_params=pltpu.CompilerParams(vmem_limit_bytes=40 << 20),
        cost_estimate=pl.CostEstimate(
            flops=4 * count * rows * keys * WIN,
            bytes_accessed=8 * rows * width,
            transcendentals=count * rows * keys,
        ),
        name="attention_forward",
    )(*ins)


def attn_bwd_kernel(q_ref, k_ref, v_ref, g_ref, lse_ref, *refs, tile, first):
    dq_ref, dk_ref, dv_ref = refs[-3:]
    head = pl.program_id(0) + first
    rows, width = q_ref.shape
    keys = k_ref.shape[0]

    if len(refs) > 3:

        @pl.when(pl.program_id(0) == 0)
        def _():
            dq_ref[...] = refs[0][...]
            dk_ref[...] = refs[1][...]
            dv_ref[...] = refs[2][...]

    lo, off = head_window(head, width)
    lane = lax.broadcasted_iota(jnp.int32, (1, WIN), 1)
    inside = (lane >= off) & (lane < off + HD)
    keep = inside.astype(jnp.bfloat16)
    kw = k_ref[:, pl.ds(lo, WIN)]
    vw = v_ref[:, pl.ds(lo, WIN)]
    ktw = kw.T
    dk = jnp.zeros((keys, WIN), jnp.float32)
    dv = jnp.zeros((keys, WIN), jnp.float32)
    for t in range(rows // tile):
        r = pl.ds(t * tile, tile)
        lse = lse_ref[pl.ds(head, 1), r]
        qw = q_ref[r, pl.ds(lo, WIN)]
        gw = g_ref[r, pl.ds(lo, WIN)]
        st = jnp.dot(kw, (qw * keep).T, preferred_element_type=jnp.float32)
        pt = jnp.exp2(st * (SCALE * LOG2E) - lse * LOG2E)
        dpt = jnp.dot(vw, (gw * keep).T, preferred_element_type=jnp.float32)
        delta = jnp.sum(pt * dpt, axis=0, keepdims=True)
        dst = (pt * (dpt - delta) * SCALE).astype(jnp.bfloat16)
        dv = dv + jnp.dot(pt.astype(jnp.bfloat16), gw, preferred_element_type=jnp.float32)
        dk = dk + jnp.dot(dst, qw, preferred_element_type=jnp.float32)
        dq = jnp.dot(ktw, dst, preferred_element_type=jnp.float32).T
        old = dq_ref[r, pl.ds(lo, WIN)].astype(jnp.float32)
        dq_ref[r, pl.ds(lo, WIN)] = jnp.where(inside, dq, old).astype(jnp.bfloat16)
    old = dk_ref[:, pl.ds(lo, WIN)].astype(jnp.float32)
    dk_ref[:, pl.ds(lo, WIN)] = jnp.where(inside, dk, old).astype(jnp.bfloat16)
    old = dv_ref[:, pl.ds(lo, WIN)].astype(jnp.float32)
    dv_ref[:, pl.ds(lo, WIN)] = jnp.where(inside, dv, old).astype(jnp.bfloat16)


def attn_bwd(q, k, v, g, lse_rows, heads, into=(), tile=512):
    rows, width = q.shape
    keys = k.shape[0]
    first, count = heads
    outs = [jax.ShapeDtypeStruct(a.shape, jnp.bfloat16) for a in (q, k, v)]
    ins = (q, k, v, g, lse_rows, *into)
    return pl.pallas_call(
        functools.partial(attn_bwd_kernel, tile=tile, first=first),
        grid=(count,),
        in_specs=[whole(a) for a in ins],
        out_specs=[whole(a) for a in outs],
        out_shape=outs,
        compiler_params=pltpu.CompilerParams(vmem_limit_bytes=52 << 20),
        cost_estimate=pl.CostEstimate(
            flops=10 * count * rows * keys * WIN,
            bytes_accessed=14 * rows * width,
            transcendentals=count * rows * keys,
        ),
        name="attention_backward",
    )(*ins)


def after(array, *earlier):
    if not earlier:
        return array
    return lax.optimization_barrier((array, earlier))[0]


def assemble(pieces, places, where, kind, height):
    width = pieces[0].shape[-1]
    blocks = [(i, b) for i, piece in enumerate(pieces) for b in range(piece.shape[0])]

    def body(where_ref, *refs):
        ins, out = refs[: len(pieces)], refs[len(pieces)]
        held, arrived, left = refs[len(pieces) + 1 :]
        zi = where_ref[0]
        loads, stores = [], []
        start = 0
        for piece, (first, x_bit, c_bit, y_bit, offset) in zip(ins, places):
            xi = where_ref[1] if x_bit == 0 else 1 - where_ref[1]
            ci = where_ref[2] if c_bit == 0 else 1 - where_ref[2]
            yi = where_ref[3] if y_bit == 0 else 1 - where_ref[3]
            size = piece.shape[1]
            for block in range(piece.shape[0]):
                slot = start + block
                row = ((zi ^ (first + block)) * 2 + xi) * height + offset
                quarter = (ci * 2 + yi) * (8 * height)
                if kind == "columns":
                    rows = pl.ds(pl.multiple_of(row, 16), size)
                    quarter = (ci * 2 + yi) * width
                    target = out.at[rows, pl.ds(pl.multiple_of(quarter, 128), width)]
                else:
                    target = out.at[pl.ds(pl.multiple_of(quarter + row, 16), size), :]
                here = held.at[slot, pl.ds(0, size)]
                loads.append(pltpu.make_async_copy(piece.at[block], here, arrived.at[slot]))
                stores.append(pltpu.make_async_copy(here, target, left.at[slot]))
            start += piece.shape[0]
        for load in loads:
            load.start()
        for load, store in zip(loads, stores):
            load.wait()
            store.start()
        for store in stores:
            store.wait()

    shape = (8 * height, 4 * width) if kind == "columns" else (32 * height, width)
    tallest = max(piece.shape[1] for piece in pieces)
    return pl.pallas_call(
        body,
        grid_spec=pltpu.PrefetchScalarGridSpec(
            num_scalar_prefetch=1,
            grid=(1,),
            in_specs=[pl.BlockSpec(memory_space=pl.ANY)] * len(pieces),
            out_specs=pl.BlockSpec(memory_space=pl.ANY),
            scratch_shapes=[
                pltpu.VMEM((len(blocks), tallest, width), pieces[0].dtype),
                pltpu.SemaphoreType.DMA((len(blocks),)),
                pltpu.SemaphoreType.DMA((len(blocks),)),
            ],
        ),
        out_shape=jax.ShapeDtypeStruct(shape, pieces[0].dtype),
        compiler_params=pltpu.CompilerParams(vmem_limit_bytes=56 << 20),
        cost_estimate=pl.CostEstimate(
            flops=0, bytes_accessed=4 * shape[0] * shape[1], transcendentals=0
        ),
        name="assemble_" + kind,
    )(where, *pieces)


def swap(array, axis):
    return lax.ppermute(array, axis, SWAP)


def line_hops(block_of):
    return [
        lax.ppermute(block_of(step), "z", [(i, i ^ step) for i in range(4)]) for step in range(1, 4)
    ]


def plane_gather(line):
    return swap(line, "x"), swap(line, "y")


def corner_swap(array, first):
    pairs = []
    for x, c, y in itertools.product(range(2), repeat=3):
        along_x = c == first
        target = (1 - x, c, y) if along_x else (x, c, 1 - y)
        pairs.append((x * 4 + c * 2 + y, target[0] * 4 + target[1] * 2 + target[2]))
    return lax.ppermute(array, ("x", "c", "y"), pairs)


def corner_gather(from_x, from_y):
    return corner_swap(jnp.where(lax.axis_index("c") == 0, from_x, from_y), 1)


PLACES = [(0, 0, 0), (1, 0, 0), (0, 0, 1), (1, 0, 1)]


def with_core(pieces, others):
    places = [(0, x, c, y, 0) for x, c, y in PLACES] + [(0, x, 1 - c, y, 0) for x, c, y in PLACES]
    return list(pieces) + list(others), places


def add_low(*terms):
    total = terms[0].astype(jnp.float32)
    for term in terms[1:]:
        total = total + term.astype(jnp.float32)
    return total.astype(jnp.bfloat16)


def part_columns(half, yy, xx):
    width = half.shape[1] // 2
    cut = lax.dynamic_slice(
        half.reshape(4, 2, 144, 2 * width), (0, xx, 0, yy * width), (4, 1, 144, width)
    )
    return cut.reshape(4, 144, width)


def part_rows(half, yy, xx):
    width = half.shape[1]
    cut = lax.dynamic_slice(
        half.reshape(2, 4, 2, 144, width), (yy, 0, xx, 0, 0), (1, 4, 1, 144, width)
    )
    return cut.reshape(4, 144, width)


class ScatterSum:
    def __init__(self, part, half):
        self.part, self.half = part, half
        self.zi, self.xi, self.yi = [lax.axis_index(name) for name in ("z", "x", "y")]

    def corner(self):
        self.sent = (self.part(self.half, 1 - self.yi, 1 - self.xi),)
        self.got = (corner_swap(self.sent[0], 0),)

    def plane(self, *earlier):
        half, got = after(self.half, *earlier), self.got[0]
        to_y, to_x = self.part(half, 1 - self.yi, self.xi), self.part(half, self.yi, 1 - self.xi)
        even = lax.axis_index("c") == 0
        to_y = jnp.where(even, add_low(to_y, got), to_y)
        to_x = jnp.where(even, to_x, add_low(to_x, got))
        self.sent = to_y, to_x
        self.got = swap(to_y, "y"), swap(to_x, "x")

    def line(self, *earlier):
        half = after(self.half, *earlier)
        own = add_low(self.part(half, self.yi, self.xi), *self.got)
        blocks = [lax.dynamic_index_in_dim(own, self.zi ^ step, 0, False) for step in range(4)]
        self.own, self.sent = blocks[0], blocks[1:]
        self.got = line_hops(lambda step: blocks[step])

    def total(self, *earlier):
        total = after(self.own, *earlier).astype(jnp.float32)
        for hop in self.got:
            total = total + hop.astype(jnp.float32)
        return total


def local_pairs(
    latent_in,
    conditioning,
    ada_weight,
    qkv_weight,
    proj_weight,
    up_weight,
    down_weight,
    bias_pack,
    cotangent,
):
    width = latent_in.shape[2]
    half_rows = latent_in.shape[1]
    zi, xi, ci, yi = [lax.axis_index(name) for name in ALL]
    device = ((zi * 2 + xi) * 2 + ci) * 2 + yi
    where = jnp.stack([zi, xi, ci, yi]).astype(jnp.int32)
    rows = width // 32

    def exchange(array):
        return lax.all_to_all(array, ALL, 0, 0, tiled=True)

    def to_all(vector):
        return exchange(jnp.broadcast_to(vector, (32,) + vector.shape))

    def over_tokens(left, right):
        return lax.dot_general(
            left, right, (((0,), (0,)), ((), ())), preferred_element_type=jnp.float32
        )

    def times_transposed(left, right):
        return lax.dot_general(
            left, right, (((1,), (1,)), ((), ())), preferred_element_type=jnp.float32
        )

    qkv_rows = qkv_weight.reshape(rows, 3 * width)
    quarters = jnp.stack(
        [qkv_rows[:, i * width : (i + 1) * width] for i in range(3)]
        + [proj_weight.reshape(rows, width)]
    )
    up_quarters = up_weight.reshape(rows, 8, 4, 144).transpose(2, 0, 1, 3).reshape(4, rows, width)
    units = lax.all_to_all(
        jnp.concatenate([quarters, up_quarters], axis=1), ("c", "y"), 0, 0, tiled=True
    )
    unit_a = units[:, :rows].reshape(4 * rows, width)
    unit_u = units[:, rows:].reshape(4 * rows, width)
    unit_d = down_weight.reshape(4 * rows, width)
    hops_a = line_hops(lambda step: unit_a)
    other_half = after(lax.dynamic_index_in_dim(latent_in, 1 - yi, 0, False), unit_a)
    half_received = swap(other_half, "y")
    line_a = jnp.stack([after(unit_a, half_received), *hops_a])
    plane_a = plane_gather(line_a)
    unit_u = after(unit_u, line_a)
    hops_u = line_hops(lambda step: unit_u)
    own_condition = lax.dynamic_index_in_dim(conditioning, yi, 0, False)
    small = to_all(after(jnp.concatenate([bias_pack, own_condition]), line_a))
    bias_share = bias_pack.shape[0]
    biases = small[:, :bias_share].reshape(-1).astype(jnp.float32)
    conditions = small[:, bias_share:].astype(jnp.float32)
    silu_all = jax.nn.silu(conditions).astype(jnp.bfloat16)
    silu_cut = lax.dynamic_slice(silu_all, (0, device * rows), (32, rows))
    ada_rows = ada_weight.reshape(rows, 6 * width)
    shares = jnp.dot(silu_cut, ada_rows, preferred_element_type=jnp.float32)
    first_shares, later_shares = shares[:, : 2 * width], shares[:, 2 * width :]
    modulations = jnp.sum(exchange(first_shares), axis=0, keepdims=True)
    modulations = modulations + biases[: 2 * width]
    shift_attention, scale_attention = jnp.split(modulations, 2, axis=1)
    own_half = lax.dynamic_index_in_dim(latent_in, yi, 0, False)
    tokens_low = jnp.concatenate([own_half, half_received])
    tokens = tokens_low.astype(jnp.float32)
    normed = norm_modulate(tokens, shift_attention, scale_attention).astype(jnp.bfloat16)
    line_a, plane_a, hops_u = lax.optimization_barrier((line_a, plane_a, hops_u))
    corner_a = corner_gather(*plane_a)
    core_a = [swap(p, "c") for p in (line_a, *plane_a)]
    line_u = jnp.stack([unit_u, *hops_u])
    unit_d = after(unit_d, line_u, *core_a)
    hops_d = line_hops(lambda step: unit_d)
    corner_a = after(corner_a, unit_d)
    core_a.append(swap(corner_a, "c"))
    line_u = after(line_u, core_a[3])
    plane_u = plane_gather(line_u)
    pieces, places = with_core((line_a, *plane_a, corner_a), core_a)
    attention_matrix = assemble(after(pieces, line_u, unit_d), places, where, "columns", 4 * rows)
    qkv_matrix = attention_matrix[:, : 3 * width]
    proj_matrix = attention_matrix[:, 3 * width :]

    query_bias = biases[6 * width : 7 * width]
    value_bias = biases[7 * width : 8 * width]
    proj_bias = biases[8 * width : 9 * width]
    up_bias = biases[9 * width : 9 * width + FF].reshape(8, 4, 144).transpose(1, 0, 2).reshape(-1)
    down_bias = biases[9 * width + FF :]

    later_modulations = jnp.sum(
        exchange(after(later_shares, attention_matrix)), axis=0, keepdims=True
    )
    later_modulations = later_modulations + biases[2 * width : 6 * width]
    gate_attention, shift_feed, scale_feed, gate_feed = jnp.split(later_modulations, 4, axis=1)
    projected = jnp.dot(normed, qkv_matrix, preferred_element_type=jnp.float32)
    queries = (projected[:, :width] + query_bias).astype(jnp.bfloat16)
    keys = projected[:, width : 2 * width].astype(jnp.bfloat16)
    values = (projected[:, 2 * width :] + value_bias).astype(jnp.bfloat16)
    line_d = jnp.stack([after(unit_d, values), *hops_d])
    plane_u = after(plane_u, line_d)
    corner_u = corner_gather(*plane_u)
    core_u = [swap(p, "c") for p in (after(line_u, line_d), *plane_u)]
    part_one = attn_fwd(after(queries, *plane_u, line_d), keys, values, (0, 8))
    line_d, corner_u, core_u = after((line_d, corner_u, core_u), *part_one)
    core_u.append(swap(corner_u, "c"))
    plane_d = plane_gather(line_d)
    attended, log_total = attn_fwd(
        after(queries, line_d, *core_u[:3]), keys, values, (8, 8), tuple(part_one)
    )
    branch = (
        jnp.dot(attended, proj_matrix, preferred_element_type=jnp.float32)
        + proj_bias
    )
    middle = tokens + gate_attention * branch
    normed_feed = norm_modulate(middle, shift_feed, scale_feed).astype(jnp.bfloat16)
    pieces, places = with_core((line_u, *plane_u, corner_u), core_u)
    plane_d = after(plane_d, normed_feed)
    corner_d = corner_gather(*plane_d)
    core_d = [swap(p, "c") for p in (after(line_d, normed_feed), *plane_d)]
    up_matrix = assemble(
        after(pieces, normed_feed, *plane_d), places, where, "columns", 4 * rows
    )
    other_cotangent = after(lax.dynamic_index_in_dim(cotangent, 1 - yi, 0, False), corner_d)
    cotangent_received = swap(other_cotangent, "y")
    core_d.append(swap(corner_d, "c"))
    up_matrix = after(up_matrix, *core_d[:3], corner_d, other_cotangent)
    before = jnp.dot(normed_feed, up_matrix, preferred_element_type=jnp.float32) + up_bias
    activated = gelu_tanh(before).astype(jnp.bfloat16)
    activated, core_d[3] = lax.optimization_barrier((activated, core_d[3]))
    own_cotangent = lax.dynamic_index_in_dim(cotangent, yi, 0, False)
    def pick(array, core):
        return lax.dynamic_slice_in_dim(array, core * 2 * width, 2 * width, 1)

    pieces, places = with_core((line_d, *plane_d, corner_d), core_d)
    down_matrix = assemble(after(pieces, activated), places, where, "rows", 4 * rows)
    feed_out = jnp.dot(activated, down_matrix, preferred_element_type=jnp.float32) + down_bias
    output_low = (middle + gate_feed * feed_out).astype(jnp.bfloat16)
    cotangent_received, output_low = lax.optimization_barrier((cotangent_received, output_low))
    upstream = jnp.concatenate([own_cotangent, cotangent_received]).astype(jnp.float32)
    d_feed = (gate_feed * upstream).astype(jnp.bfloat16)
    down_sent = over_tokens(pick(after(activated, output_low), 1 - ci), d_feed)
    down_sent = down_sent.astype(jnp.bfloat16)
    down_received = swap(down_sent, "c")
    output_received = swap(output_low[half_rows:], "y")
    d_gate_feed = jnp.sum(upstream * feed_out, axis=0, keepdims=True)

    d_activated = times_transposed(after(d_feed, down_sent), down_matrix)
    unused_gelu, gelu_pull = jax.vjp(gelu_tanh, before)
    d_before = gelu_pull(d_activated)[0].astype(jnp.bfloat16)
    up_sent = over_tokens(
        after(normed_feed, output_received, down_received), pick(d_before, 1 - ci)
    ).astype(jnp.bfloat16)
    up_received = swap(up_sent, "c")
    down_half = over_tokens(pick(after(activated, up_sent), ci), d_feed)
    down = ScatterSum(part_rows, add_low(down_half, down_received))
    down.corner()
    d_normed_feed = times_transposed(after(d_before, *down.sent, up_received), up_matrix)
    down.plane(d_normed_feed)
    up_half = over_tokens(after(normed_feed, *down.sent), pick(d_before, ci))
    up = ScatterSum(part_columns, add_low(up_half, up_received))
    up.corner()
    unused_norm, norm_pull = jax.vjp(norm_modulate, middle, shift_feed, scale_feed)
    d_middle_part, d_shift_feed, d_scale_feed = norm_pull(
        after(d_normed_feed, *up.sent)
    )
    d_middle = upstream + d_middle_part
    d_gate_attention = jnp.sum(d_middle * branch, axis=0, keepdims=True)
    d_branch = (gate_attention * d_middle).astype(jnp.bfloat16)
    d_attended = times_transposed(after(d_branch, down.got[0]), proj_matrix).astype(jnp.bfloat16)
    mods_early = jnp.concatenate([d_gate_attention, d_shift_feed, d_scale_feed, d_gate_feed], 1)
    mods_early = mods_early.astype(jnp.bfloat16)
    early_every = to_all(mods_early[0])
    down.line(d_attended)
    up.plane(d_attended)
    log_rows = log_total[:, :H].T
    gradients = attn_bwd(
        queries,
        keys,
        values,
        after(d_attended, *up.sent, *down.sent, mods_early),
        log_rows,
        (0, 8),
    )

    def attention_terms(start, stop, core, *earlier):
        d_q, d_k, d_v, d_b = [a[:, start:stop] for a in (*gradients, d_branch)]
        left = after(normed, *earlier)
        first = over_tokens(left, jnp.where(core == 0, d_q, d_v))
        second = over_tokens(
            jnp.where(core == 0, left, attended), jnp.where(core == 0, d_k, d_b)
        )
        return jnp.concatenate([first, second])

    left_sent = attention_terms(
        0, 512, 1 - ci, *gradients, *down.got, *up.got, early_every
    ).astype(jnp.bfloat16)
    left_received = swap(left_sent, "c")
    up.line(left_sent)
    left_half = attention_terms(0, 512, ci, left_sent, *up.sent)
    left = ScatterSum(part_rows, add_low(left_half, left_received))
    left.corner()
    down_sum = down.total(left_half)
    gradients = attn_bwd(
        queries,
        keys,
        values,
        after(d_attended, *left.sent, down_sum),
        log_rows,
        (8, 4),
        tuple(gradients),
    )
    gradients = after(tuple(gradients), *left.got, *up.got)
    left.plane(*gradients)
    up_terms = up.total(*gradients).reshape(4, rows, width)
    up_sum = lax.all_to_all(up_terms, ("c", "y"), 0, 0, tiled=True)
    gradients = attn_bwd(
        queries,
        keys,
        values,
        after(d_attended, *left.sent, up_terms),
        log_rows,
        (12, 4),
        tuple(gradients),
    )
    gradients = after(tuple(gradients), *left.got, up_sum)
    d_queries, d_keys, d_values = gradients
    left.line(*gradients)
    right_sent = attention_terms(512, width, 1 - ci, *left.sent).astype(jnp.bfloat16)
    right_received = swap(right_sent, "c")
    right_half = attention_terms(512, width, ci, right_sent)
    right = ScatterSum(part_rows, add_low(right_half, right_received))
    right.corner()
    d_projected = jnp.concatenate(after((d_queries, d_keys, d_values), *right.sent), axis=1)
    d_normed = times_transposed(d_projected, qkv_matrix)
    right.plane(d_normed)
    unused_first, first_pull = jax.vjp(norm_modulate, tokens, shift_attention, scale_attention)
    d_tokens_part, d_shift_attention, d_scale_attention = first_pull(after(d_normed, *right.sent))
    grad_low = (d_middle + d_tokens_part).astype(jnp.bfloat16)
    quarter_rows = half_rows // 2
    grad_first = swap(grad_low[half_rows : half_rows + quarter_rows], "y")
    mods_late = jnp.concatenate([d_shift_attention, d_scale_attention], axis=1)
    mods_late = mods_late.astype(jnp.bfloat16)
    left_terms = left.total(grad_low)
    right.line(grad_low, mods_late, left_terms)
    late_every = to_all(after(mods_late, *right.sent)[0])
    bias_terms = jnp.concatenate(
        [
            mods_late[0].astype(jnp.float32),
            mods_early[0].astype(jnp.float32),
            jnp.sum(after(d_queries, *right.sent), axis=0, dtype=jnp.float32),
            jnp.sum(after(d_values, *right.sent), axis=0, dtype=jnp.float32),
            jnp.sum(after(d_branch, *right.sent), axis=0, dtype=jnp.float32),
            jnp.sum(after(d_before, *right.sent), axis=0, dtype=jnp.float32)
            .reshape(4, 8, 144)
            .transpose(1, 0, 2)
            .reshape(-1),
            jnp.sum(after(d_feed, *right.sent), axis=0, dtype=jnp.float32),
        ]
    )
    grad_last = swap(after(grad_low, grad_first)[half_rows + quarter_rows :], "y")
    late_every, early_every = after((late_every, early_every), *right.sent)

    late_width = late_every.shape[1]
    grad_ada = jnp.concatenate(
        [over_tokens(silu_cut, late_every), over_tokens(silu_cut, early_every)], axis=1
    ).reshape(-1)
    d_silu_rows = times_transposed(late_every, ada_rows[:, :late_width])
    d_silu_rows = d_silu_rows + times_transposed(early_every, ada_rows[:, late_width:])
    d_silu_parts = jnp.repeat(d_silu_rows.reshape(16, 1, 2, rows), 2, axis=1)
    parts = exchange(
        jnp.concatenate([d_silu_parts.reshape(32, 2 * rows), bias_terms.reshape(32, -1)], axis=1)
    )
    d_silu = parts[:, : 2 * rows].reshape(32, 2, rows).transpose(1, 0, 2).reshape(2, width)
    grad_bias = jnp.sum(parts[:, 2 * rows :], axis=0)
    unused_silu, silu_pull = jax.vjp(jax.nn.silu, conditioning.astype(jnp.float32))
    grad_cond = silu_pull(d_silu)[0].astype(jnp.bfloat16)

    right_terms = right.total(d_silu_rows, grad_first)
    sums = jnp.concatenate([left_terms, right_terms], axis=1).reshape(4, rows, width)
    sums = lax.all_to_all(sums, ("c", "y"), 0, 0, tiled=True)
    down_sum, output_low, output_received, grad_last = after(
        (down_sum, output_low, output_received, grad_last), right_terms
    )
    grad_received = jnp.concatenate([grad_first, grad_last])
    grad_up = after(up_sum, right_terms).reshape(4, rows, 8, 144).transpose(1, 2, 0, 3).reshape(-1)
    def both_halves(own_rows, received):
        first = jnp.where(yi == 0, own_rows, received)
        second = jnp.where(yi == 0, received, own_rows)
        return jnp.stack([first, second])

    output = both_halves(output_low[:half_rows], output_received)
    grad_input = both_halves(grad_low[:half_rows], grad_received)

    grad_down = down_sum.reshape(-1)
    grad_qkv = jnp.concatenate([sums[0], sums[1], sums[2]], axis=1).reshape(-1)
    grad_proj = sums[3].reshape(-1)
    return (
        output,
        grad_input,
        grad_cond,
        grad_ada,
        grad_qkv,
        grad_proj,
        grad_up,
        grad_down,
        grad_bias,
    )


def local_any(
    latent_in,
    conditioning,
    ada_weight,
    qkv_weight,
    proj_weight,
    up_weight,
    down_weight,
    bias_pack,
    cotangent,
):
    model_width = latent_in.shape[2]
    every_param = (
        lax.all_gather(ada_weight, ("batch", "seq"), axis=0, tiled=True),
        lax.all_gather(qkv_weight, ("batch", "seq"), axis=0, tiled=True),
        lax.all_gather(proj_weight, ("batch", "seq"), axis=0, tiled=True),
        lax.all_gather(up_weight, ("batch", "seq"), axis=0, tiled=True),
        lax.all_gather(down_weight, ("batch", "seq"), axis=0, tiled=True),
        lax.all_gather(bias_pack, ("batch", "seq"), axis=0, tiled=True),
    )
    ada_matrix, qkv_matrix, proj_matrix, up_matrix, down_matrix, biases = shape_all(
        every_param, model_width
    )
    ada_bias = biases[: 6 * model_width]
    query_bias = biases[6 * model_width : 7 * model_width]
    value_bias = biases[7 * model_width : 8 * model_width]
    proj_bias = biases[8 * model_width : 9 * model_width]
    up_bias = biases[9 * model_width : 9 * model_width + FF]
    down_bias = biases[9 * model_width + FF :]
    tokens = latent_in.astype(jnp.float32)
    conditions = conditioning.astype(jnp.float32)
    silu_cond = jax.nn.silu(conditions).astype(jnp.bfloat16)
    modulations = jnp.dot(silu_cond, ada_matrix, preferred_element_type=jnp.float32) + ada_bias
    shift_attention, scale_attention, gate_attention, shift_feed, scale_feed, gate_feed = jnp.split(
        modulations[:, None, :], 6, axis=2
    )
    normed = norm_modulate(tokens, shift_attention, scale_attention).astype(jnp.bfloat16)
    projected = jnp.einsum("btd,df->btf", normed, qkv_matrix, preferred_element_type=jnp.float32)
    queries = (projected[..., :model_width] + query_bias).astype(jnp.bfloat16)
    own_keys = jnp.concatenate(
        [
            projected[..., model_width : 2 * model_width],
            projected[..., 2 * model_width :] + value_bias,
        ],
        axis=2,
    ).astype(jnp.bfloat16)
    every_keys = lax.all_gather(own_keys, "seq", axis=1, tiled=True)
    attended, log_total = lax.map(attend_latent, (queries, every_keys))
    attended = attended.astype(jnp.bfloat16)
    branch = (
        jnp.einsum("btd,de->bte", attended, proj_matrix, preferred_element_type=jnp.float32)
        + proj_bias
    )
    middle = tokens + gate_attention * branch
    normed_feed = norm_modulate(middle, shift_feed, scale_feed).astype(jnp.bfloat16)
    before = (
        jnp.einsum("btd,df->btf", normed_feed, up_matrix, preferred_element_type=jnp.float32)
        + up_bias
    )
    activated = gelu_tanh(before).astype(jnp.bfloat16)
    feed_out = (
        jnp.einsum("btf,fd->btd", activated, down_matrix, preferred_element_type=jnp.float32)
        + down_bias
    )
    output = (middle + gate_feed * feed_out).astype(jnp.bfloat16)
    param_again = (
        lax.all_gather(ada_weight, ("batch", "seq"), axis=0, tiled=True),
        lax.all_gather(qkv_weight, ("batch", "seq"), axis=0, tiled=True),
        lax.all_gather(proj_weight, ("batch", "seq"), axis=0, tiled=True),
        lax.all_gather(up_weight, ("batch", "seq"), axis=0, tiled=True),
        lax.all_gather(down_weight, ("batch", "seq"), axis=0, tiled=True),
        lax.all_gather(bias_pack, ("batch", "seq"), axis=0, tiled=True),
    )
    ada_matrix, qkv_matrix, proj_matrix, up_matrix, down_matrix, biases = shape_all(
        param_again, model_width
    )
    upstream = cotangent.astype(jnp.float32)
    d_gate_feed = jnp.sum(upstream * feed_out, axis=1, keepdims=True)
    d_feed = (gate_feed * upstream).astype(jnp.bfloat16)
    d_activated = jnp.einsum("btd,fd->btf", d_feed, down_matrix, preferred_element_type=jnp.float32)
    unused_gelu, gelu_pull = jax.vjp(gelu_tanh, before)
    d_before = gelu_pull(d_activated)[0].astype(jnp.bfloat16)
    d_normed_feed = jnp.einsum(
        "btf,df->btd", d_before, up_matrix, preferred_element_type=jnp.float32
    )
    unused_norm, norm_pull = jax.vjp(norm_modulate, middle, shift_feed, scale_feed)
    d_middle_part, d_shift_feed, d_scale_feed = norm_pull(d_normed_feed)
    d_middle = upstream + d_middle_part
    d_gate_attention = jnp.sum(d_middle * branch, axis=1, keepdims=True)
    d_branch = (gate_attention * d_middle).astype(jnp.bfloat16)
    d_attended = jnp.einsum(
        "bte,de->btd", d_branch, proj_matrix, preferred_element_type=jnp.float32
    ).astype(jnp.bfloat16)
    d_queries, d_every = lax.map(attend_back, (queries, every_keys, log_total, d_attended))
    d_queries = d_queries.astype(jnp.bfloat16)
    d_own = lax.psum_scatter(d_every.astype(jnp.bfloat16), "seq", scatter_dimension=1, tiled=True)
    d_projected = jnp.concatenate([d_queries, d_own], axis=2)
    d_normed = jnp.einsum(
        "btf,df->btd", d_projected, qkv_matrix, preferred_element_type=jnp.float32
    )
    unused_first, first_pull = jax.vjp(norm_modulate, tokens, shift_attention, scale_attention)
    d_tokens_part, d_shift_attention, d_scale_attention = first_pull(d_normed)
    grad_input = (d_middle + d_tokens_part).astype(jnp.bfloat16)
    local_mods = jnp.concatenate(
        [
            d_shift_attention,
            d_scale_attention,
            d_gate_attention,
            d_shift_feed,
            d_scale_feed,
            d_gate_feed,
        ],
        axis=2,
    )[:, 0, :]
    d_mods = lax.psum(local_mods.astype(jnp.bfloat16), "seq")
    d_silu = jnp.einsum("bf,df->bd", d_mods, ada_matrix, preferred_element_type=jnp.float32)
    unused_silu, silu_pull = jax.vjp(jax.nn.silu, conditions)
    grad_cond = silu_pull(d_silu)[0].astype(jnp.bfloat16)
    is_owner = lax.axis_index("seq") == 0
    owned_mods = jnp.where(is_owner, d_mods, jnp.zeros_like(d_mods))
    bias_terms = jnp.concatenate(
        [
            jnp.sum(owned_mods, axis=0, dtype=jnp.float32),
            jnp.sum(d_queries, axis=(0, 1), dtype=jnp.float32),
            jnp.sum(d_own[..., model_width:], axis=(0, 1), dtype=jnp.float32),
            jnp.sum(d_branch, axis=(0, 1), dtype=jnp.float32),
            jnp.sum(d_before, axis=(0, 1), dtype=jnp.float32),
            jnp.sum(d_feed, axis=(0, 1), dtype=jnp.float32),
        ]
    )
    matrix_terms = [
        (silu_cond, owned_mods, ada_weight.shape[0]),
        (
            normed.reshape(-1, model_width),
            d_projected.reshape(-1, 3 * model_width),
            qkv_weight.shape[0],
        ),
        (
            attended.reshape(-1, model_width),
            d_branch.reshape(-1, model_width),
            proj_weight.shape[0],
        ),
        (normed_feed.reshape(-1, model_width), d_before.reshape(-1, FF), up_weight.shape[0]),
        (activated.reshape(-1, FF), d_feed.reshape(-1, model_width), down_weight.shape[0]),
    ]
    bias_share = bias_pack.shape[0]
    shard_rows = sum((entry[2] for entry in matrix_terms)) + bias_share
    block_count = shard_rows * lax.axis_size(("batch", "seq")) // shard_rows
    pieces = []
    for left, right, grad_shard_size in matrix_terms:
        pieces.append(flat_term(left, right).reshape(block_count, grad_shard_size))
    pieces.append(bias_terms.reshape(block_count, bias_share))
    owned_grads = lax.psum_scatter(
        jnp.concatenate(pieces, axis=1).reshape(-1),
        ("batch", "seq"),
        scatter_dimension=0,
        tiled=True,
    )
    results = []
    cursor = 0
    for shard_size in [entry[2] for entry in matrix_terms] + [bias_share]:
        results.append(owned_grads[cursor : cursor + shard_size])
        cursor = cursor + shard_size
    grad_ada, grad_qkv, grad_proj, grad_up, grad_down, grad_bias = results
    return (
        output,
        grad_input,
        grad_cond,
        grad_ada,
        grad_qkv,
        grad_proj,
        grad_up,
        grad_down,
        grad_bias,
    )


def solution(mesh):
    batch, seq = mesh.shape["batch"], mesh.shape["seq"]
    if (batch, seq) == (16, 2):
        inner = Mesh(mesh.devices.reshape(4, 2, 2, 2), ALL)
        body, tokens = local_pairs, ("z", "x", "c")
        flat, split = P(ALL), "y"
    else:
        inner, body, tokens, split = mesh, local_any, "batch", "seq"
        flat = P(("batch", "seq"))
    activations = P(tokens, split, None)
    vectors = P(tokens, None)
    in_specs = (activations, vectors) + (flat,) * 6 + (activations,)
    out_specs = (activations, activations, vectors) + (flat,) * 6
    return jax.shard_map(body, mesh=inner, in_specs=in_specs, out_specs=out_specs, check_vma=False)
```

```python
import functools
import itertools

import jax
import jax.numpy as jnp
from jax import lax
from jax.experimental import pallas as pl
from jax.experimental.pallas import tpu as pltpu
from jax.sharding import Mesh
from jax.sharding import PartitionSpec as P

H = 16
HD = 72
FF = 4608


EPS = 1e-06
GELU_COEF = 0.7978845608028654
SCALE = HD ** (-0.5)
LOG2E = 1.4426950408889634
WIN = 256
ALL = ("z", "x", "c", "y")
SWAP = [(0, 1), (1, 0)]


def norm_modulate(inputs, shift_term, scale_term):
    center = inputs - jnp.mean(inputs, axis=-1, keepdims=True)
    spread = jnp.mean(center * center, axis=-1, keepdims=True)
    return center * lax.rsqrt(spread + EPS) * (1.0 + scale_term) + shift_term


def gelu_tanh(values):
    return (
        0.5 * values * (1.0 + jnp.tanh(GELU_COEF * (values + 0.044715 * values * values * values)))
    )


def flat_term(left, right):
    product = jnp.einsum("nd,nf->df", left, right, preferred_element_type=jnp.float32).reshape(-1)
    return product


def split_heads(queries, keys_values):
    query_rows = queries.shape[0]
    key_rows = keys_values.shape[0]
    model_width = queries.shape[1]
    query_heads = queries.reshape(query_rows, H, HD)
    key_heads = keys_values[:, :model_width].reshape(key_rows, H, HD)
    value_heads = keys_values[:, model_width:].reshape(key_rows, H, HD)
    scores = jnp.einsum(
        "qhe,khe->hqk", query_heads, key_heads, preferred_element_type=jnp.float32
    ) * HD ** (-0.5)
    return (query_heads, key_heads, value_heads, scores)


def attend_latent(block_items):
    queries, keys_values = block_items
    query_heads, key_heads, value_heads, scores = split_heads(queries, keys_values)
    top_score = jnp.max(scores, axis=-1, keepdims=True)
    exp_scores = jnp.exp(scores - top_score)
    exp_total = jnp.sum(exp_scores, axis=-1, keepdims=True)
    probs_low = (exp_scores / exp_total).astype(jnp.bfloat16)
    attended = jnp.einsum(
        "hqk,khe->qhe", probs_low, value_heads, preferred_element_type=jnp.float32
    )
    return (
        attended.reshape(queries.shape[0], queries.shape[1]),
        (top_score + jnp.log(exp_total))[..., 0],
    )


def attend_back(block_items):
    queries, keys_values, log_total, d_attended = block_items
    query_rows = queries.shape[0]
    key_rows = keys_values.shape[0]
    model_width = queries.shape[1]
    query_heads, key_heads, value_heads, scores = split_heads(queries, keys_values)
    attention_probs = jnp.exp(scores - log_total[..., None])
    d_heads = d_attended.reshape(query_rows, H, HD)
    d_probs = jnp.einsum("qhe,khe->hqk", d_heads, value_heads, preferred_element_type=jnp.float32)
    centered = d_probs - jnp.sum(attention_probs * d_probs, axis=-1, keepdims=True)
    d_scores = (HD ** (-0.5) * (attention_probs * centered)).astype(jnp.bfloat16)
    d_queries = jnp.einsum("hqk,khe->qhe", d_scores, key_heads, preferred_element_type=jnp.float32)
    d_keys = jnp.einsum("hqk,qhe->khe", d_scores, query_heads, preferred_element_type=jnp.float32)
    d_values = jnp.einsum(
        "hqk,qhe->khe",
        attention_probs.astype(jnp.bfloat16),
        d_heads,
        preferred_element_type=jnp.float32,
    )
    joined = jnp.concatenate(
        [d_keys.reshape(key_rows, model_width), d_values.reshape(key_rows, model_width)], axis=1
    )
    return (d_queries.reshape(query_rows, model_width), joined)


def shape_all(gathered, model_width):
    ada_full, qkv_full, proj_full, up_full, down_full, bias_full = gathered
    return (
        ada_full.reshape(model_width, 6 * model_width),
        qkv_full.reshape(model_width, 3 * model_width),
        proj_full.reshape(model_width, model_width),
        up_full.reshape(model_width, FF),
        down_full.reshape(FF, model_width),
        bias_full.astype(jnp.float32),
    )


def head_window(head, width):
    start = jnp.minimum((head * HD) // 128, width // 128 - 2) * 128
    return pl.multiple_of(start, 128), head * HD - start


def attn_fwd_kernel(q_ref, k_ref, v_ref, *refs, tile, first):
    o_ref, lse_ref = refs[-2:]
    head = pl.program_id(0) + first
    rows, width = q_ref.shape

    if len(refs) > 2:

        @pl.when(pl.program_id(0) == 0)
        def _():
            o_ref[...] = refs[0][...]
            lse_ref[...] = refs[1][...]

    lo, off = head_window(head, width)
    lane = lax.broadcasted_iota(jnp.int32, (1, WIN), 1)
    inside = (lane >= off) & (lane < off + HD)
    keep = inside.astype(jnp.bfloat16)
    kw = k_ref[:, pl.ds(lo, WIN)]
    vw = v_ref[:, pl.ds(lo, WIN)]
    col = lax.broadcasted_iota(jnp.int32, (1, 128), 1) == head
    for t in range(rows // tile):
        r = pl.ds(t * tile, tile)
        qm = q_ref[r, pl.ds(lo, WIN)] * keep
        s = lax.dot_general(qm, kw, (((1,), (1,)), ((), ())), preferred_element_type=jnp.float32)
        top = jnp.max(s, axis=-1, keepdims=True)
        p = jnp.exp2((s - top) * (SCALE * LOG2E))
        total = jnp.sum(p, axis=-1, keepdims=True)
        o = jnp.dot(p.astype(jnp.bfloat16), vw, preferred_element_type=jnp.float32)
        o = o * (1.0 / total)
        old = o_ref[r, pl.ds(lo, WIN)].astype(jnp.float32)
        o_ref[r, pl.ds(lo, WIN)] = jnp.where(inside, o, old).astype(jnp.bfloat16)
        lse_ref[r, :] = jnp.where(col, top * SCALE + jnp.log(total), lse_ref[r, :])


def whole(array_or_shape):
    shape = array_or_shape.shape
    return pl.BlockSpec(shape, lambda h: (0,) * len(shape), pipeline_mode=pl.Buffered(1))


def attn_fwd(q, k, v, heads, into=(), tile=256):
    rows, width = q.shape
    keys = k.shape[0]
    first, count = heads
    outs = [
        jax.ShapeDtypeStruct(q.shape, jnp.bfloat16),
        jax.ShapeDtypeStruct((rows, 128), jnp.float32),
    ]
    ins = (q, k, v, *into)
    return pl.pallas_call(
        functools.partial(attn_fwd_kernel, tile=tile, first=first),
        grid=(count,),
        in_specs=[whole(a) for a in ins],
        out_specs=[whole(a) for a in outs],
        out_shape=outs,
        compiler_params=pltpu.CompilerParams(vmem_limit_bytes=40 << 20),
        cost_estimate=pl.CostEstimate(
            flops=4 * count * rows * keys * WIN,
            bytes_accessed=8 * rows * width,
            transcendentals=count * rows * keys,
        ),
        name="attention_forward",
    )(*ins)


def attn_bwd_kernel(q_ref, k_ref, v_ref, g_ref, lse_ref, *refs, tile, first, origin):
    dq_ref, dk_ref, dv_ref = refs[-3:]
    head = pl.program_id(0) + first
    rows, width = q_ref.shape
    keys = k_ref.shape[0]

    if len(refs) > 3:

        @pl.when(pl.program_id(0) == 0)
        def _():
            dq_ref[:, :128] = refs[0][...]
            dk_ref[:, :128] = refs[1][...]
            dv_ref[:, :128] = refs[2][...]

    lo, off = head_window(head, origin + dq_ref.shape[1])
    there = pl.ds(pl.multiple_of(lo - origin, 128), WIN)
    lane = lax.broadcasted_iota(jnp.int32, (1, WIN), 1)
    inside = (lane >= off) & (lane < off + HD)
    keep = inside.astype(jnp.bfloat16)
    kw = k_ref[:, pl.ds(lo, WIN)]
    vw = v_ref[:, pl.ds(lo, WIN)]
    ktw = kw.T
    dk = jnp.zeros((keys, WIN), jnp.float32)
    dv = jnp.zeros((keys, WIN), jnp.float32)
    for t in range(rows // tile):
        r = pl.ds(t * tile, tile)
        lse = lse_ref[pl.ds(head, 1), r]
        qw = q_ref[r, pl.ds(lo, WIN)]
        gw = g_ref[r, pl.ds(lo, WIN)]
        st = jnp.dot(kw, (qw * keep).T, preferred_element_type=jnp.float32)
        pt = jnp.exp2(st * (SCALE * LOG2E) - lse * LOG2E)
        dpt = jnp.dot(vw, (gw * keep).T, preferred_element_type=jnp.float32)
        delta = jnp.sum(pt * dpt, axis=0, keepdims=True)
        dst = (pt * (dpt - delta) * SCALE).astype(jnp.bfloat16)
        dv = dv + jnp.dot(pt.astype(jnp.bfloat16), gw, preferred_element_type=jnp.float32)
        dk = dk + jnp.dot(dst, qw, preferred_element_type=jnp.float32)
        dq = jnp.dot(ktw, dst, preferred_element_type=jnp.float32).T
        old = dq_ref[r, there].astype(jnp.float32)
        dq_ref[r, there] = jnp.where(inside, dq, old).astype(jnp.bfloat16)
    old = dk_ref[:, there].astype(jnp.float32)
    dk_ref[:, there] = jnp.where(inside, dk, old).astype(jnp.bfloat16)
    old = dv_ref[:, there].astype(jnp.float32)
    dv_ref[:, there] = jnp.where(inside, dv, old).astype(jnp.bfloat16)


def head_columns(heads):
    first, count = heads
    return (first * HD) // 128 * 128, -(-((first + count) * HD) // 128) * 128


def attn_bwd(q, k, v, g, lse_rows, heads, before=(), tile=512):
    rows, width = q.shape
    keys = k.shape[0]
    first, count = heads
    start, stop = head_columns(heads)
    outs = [jax.ShapeDtypeStruct((a.shape[0], stop - start), jnp.bfloat16) for a in (q, k, v)]
    ins = (q, k, v, g, lse_rows, *before)
    specs = [whole(a) for a in ins[:5]]
    for array in before:
        last = array.shape[1] // 128 - 1
        specs.append(pl.BlockSpec((array.shape[0], 128), lambda h, last=last: (0, last)))
    return pl.pallas_call(
        functools.partial(attn_bwd_kernel, tile=tile, first=first, origin=start),
        grid=(count,),
        in_specs=specs,
        out_specs=[whole(a) for a in outs],
        out_shape=outs,
        compiler_params=pltpu.CompilerParams(vmem_limit_bytes=52 << 20),
        cost_estimate=pl.CostEstimate(
            flops=10 * count * rows * keys * WIN,
            bytes_accessed=14 * rows * width,
            transcendentals=count * rows * keys,
        ),
        name="attention_backward",
    )(*ins)


def after(array, *earlier):
    if not earlier:
        return array
    return lax.optimization_barrier((array, earlier))[0]


def swap(array, axis):
    return lax.ppermute(array, axis, SWAP)


def line_hops(block_of):
    return [
        lax.ppermute(block_of(step), "z", [(i, i ^ step) for i in range(4)]) for step in range(1, 4)
    ]


def plane_gather(line):
    return swap(line, "x"), swap(line, "y")


def corner_swap(array, first):
    pairs = []
    for x, c, y in itertools.product(range(2), repeat=3):
        along_x = c == first
        target = (1 - x, c, y) if along_x else (x, c, 1 - y)
        pairs.append((x * 4 + c * 2 + y, target[0] * 4 + target[1] * 2 + target[2]))
    return lax.ppermute(array, ("x", "c", "y"), pairs)


def corner_gather(from_x, from_y):
    return corner_swap(jnp.where(lax.axis_index("c") == 0, from_x, from_y), 1)


def add_low(*terms):
    total = terms[0].astype(jnp.float32)
    for term in terms[1:]:
        total = total + term.astype(jnp.float32)
    return total.astype(jnp.bfloat16)


def rows_of(half, yy, xx):
    width = half.shape[1]
    cut = lax.dynamic_slice(
        half.reshape(2, 4, 2, 144, width), (yy, 0, xx, 0, 0), (1, 4, 1, 144, width)
    )
    return cut.reshape(4, 144, width)


def columns_of(half, yy, xx):
    width = half.shape[1] // 2
    cut = lax.dynamic_slice(
        half.reshape(4, 2, 144, 2 * width), (0, xx, 0, yy * width), (4, 1, 144, width)
    )
    return cut.reshape(4, 144, width)


class ScatterSum:
    def __init__(self, part, half, quarters):
        self.part, self.half = part, half
        self.mine, self.theirs = quarters
        self.zi, self.xi = lax.axis_index("z"), lax.axis_index("x")

    def corner(self):
        self.sent = (self.part(self.half, self.theirs, 1 - self.xi),)
        self.got = (corner_swap(self.sent[0], 0),)

    def plane(self, *earlier):
        half, got = after(self.half, *earlier), self.got[0]
        to_y, to_x = self.part(half, self.theirs, self.xi), self.part(half, self.mine, 1 - self.xi)
        even = lax.axis_index("c") == 0
        to_y = jnp.where(even, add_low(to_y, got), to_y)
        to_x = jnp.where(even, to_x, add_low(to_x, got))
        self.sent = to_y, to_x
        self.got = swap(to_y, "y"), swap(to_x, "x")

    def line(self, *earlier):
        half = after(self.half, *earlier)
        own = add_low(self.part(half, self.mine, self.xi), *self.got)
        blocks = [lax.dynamic_index_in_dim(own, self.zi ^ step, 0, False) for step in range(4)]
        self.own, self.sent = blocks[0], blocks[1:]
        self.got = line_hops(lambda step: blocks[step])

    def total(self, *earlier):
        total = after(self.own, *earlier).astype(jnp.float32)
        for hop in self.got:
            total = total + hop.astype(jnp.float32)
        return total


def load_quarter(where_ref, pieces, quarter, buf, sems):
    copies = []
    for x_bit in range(2):
        piece = pieces[quarter * 2 + x_bit]
        xi = where_ref[1] if x_bit == 0 else 1 - where_ref[1]
        height = piece.shape[1]
        for block in range(4):
            row = pl.multiple_of(((where_ref[0] ^ block) * 2 + xi) * height, 16)
            copies.append(
                pltpu.make_async_copy(
                    piece.at[block], buf.at[pl.ds(row, height), :], sems.at[len(copies)]
                )
            )
    return copies


def stream_quarters(where_ref, pieces, buf, sems):
    step = pl.program_id(0)
    for i in range(4):

        @pl.when(step == i)
        def _(i=i):
            quarter = load_quarter(where_ref, pieces, i, buf.at[i % 2], sems.at[i % 2])
            if i == 0:
                for copy in quarter:
                    copy.start()
            if i < 3:
                other = (i + 1) % 2
                for copy in load_quarter(
                    where_ref, pieces, i + 1, buf.at[other], sems.at[other]
                ):
                    copy.start()
            for copy in quarter:
                copy.wait()

    return lax.rem(step, 2)


def quarter_scratch(width):
    return [pltpu.VMEM((2, width, width), jnp.bfloat16), pltpu.SemaphoreType.DMA((2, 8))]


def times_t(left, right):
    return lax.dot_general(
        left, right, (((1,), (1,)), ((), ())), preferred_element_type=jnp.float32
    )


def quarter_call(body, where, ins, in_specs, pieces, outs, out_specs, scratch, flops, name):
    return pl.pallas_call(
        body,
        grid_spec=pltpu.PrefetchScalarGridSpec(
            num_scalar_prefetch=1,
            grid=(4,),
            in_specs=in_specs + [pl.BlockSpec(memory_space=pl.ANY)] * len(pieces),
            out_specs=out_specs,
            scratch_shapes=scratch,
        ),
        out_shape=outs,
        compiler_params=pltpu.CompilerParams(vmem_limit_bytes=58 << 20),
        cost_estimate=pl.CostEstimate(
            flops=flops, bytes_accessed=30 << 20, transcendentals=0
        ),
        name=name,
    )(where, *ins, *pieces)


def fixed(array):
    shape = array.shape
    return pl.BlockSpec(shape, lambda i, w: (0,) * len(shape), pipeline_mode=pl.Buffered(1))


def moving(rows, width):
    return pl.BlockSpec((rows, width), lambda i, w: (0, i))


TILE = 512


def feed_up(where, inputs, bias, pieces):
    rows, width = inputs.shape

    def body(where_ref, x_ref, bias_ref, *refs):
        ins, (act_ref, slope_ref, buf, sems) = refs[:8], refs[8:]
        slot = stream_quarters(where_ref, ins, buf, sems)
        weights = buf.at[slot]
        for t in range(rows // TILE):
            r = pl.ds(t * TILE, TILE)
            u = jnp.dot(x_ref[r, :], weights[...], preferred_element_type=jnp.float32)
            u = u + bias_ref[...]
            square = u * u
            bend = jnp.tanh(u * (GELU_COEF + (GELU_COEF * 0.044715) * square))
            half = 0.5 + 0.5 * bend
            slope = (0.5 * GELU_COEF) + (1.5 * GELU_COEF * 0.044715) * square
            act_ref[r, :] = (u * half).astype(jnp.bfloat16)
            slope_ref[r, :] = (half + u * (1.0 - bend * bend) * slope).astype(jnp.bfloat16)

    out = jax.ShapeDtypeStruct((rows, 4 * width), jnp.bfloat16)
    return quarter_call(
        body,
        where,
        (inputs, bias),
        [fixed(inputs), moving(1, width)],
        pieces,
        [out, out],
        [moving(rows, width)] * 2,
        quarter_scratch(width),
        8 * rows * width * width,
        "feed_up",
    )


def feed_down(where, activated, middle, gate, bias, pieces):
    rows, width = middle.shape

    def body(where_ref, act_ref, middle_ref, gate_ref, bias_ref, *refs):
        ins, (feed_ref, out_ref, buf, sems) = refs[:8], refs[8:]
        slot = stream_quarters(where_ref, ins, buf, sems)
        weights = buf.at[slot]
        step = pl.program_id(0)
        for t in range(rows // TILE):
            r = pl.ds(t * TILE, TILE)
            term = jnp.dot(act_ref[r, :], weights[...], preferred_element_type=jnp.float32)

            @pl.when(step == 0)
            def _():
                feed_ref[r, :] = term + bias_ref[...]

            @pl.when((step > 0) & (step < 3))
            def _():
                feed_ref[r, :] += term

            @pl.when(step == 3)
            def _():
                feed = feed_ref[r, :] + term
                feed_ref[r, :] = feed
                out_ref[r, :] = (middle_ref[r, :] + gate_ref[...] * feed).astype(jnp.bfloat16)

    outs = [
        jax.ShapeDtypeStruct((rows, width), jnp.float32),
        jax.ShapeDtypeStruct((rows, width), jnp.bfloat16),
    ]
    return quarter_call(
        body,
        where,
        (activated, middle, gate, bias),
        [moving(rows, width), fixed(middle), fixed(gate), fixed(bias)],
        pieces,
        outs,
        [fixed(a) for a in outs],
        quarter_scratch(width),
        8 * rows * width * width,
        "feed_down",
    )


def feed_back(where, d_feed, slope, down_pieces, up_pieces):
    rows, width = d_feed.shape

    def body(where_ref, d_ref, slope_ref, *refs):
        down_ins, up_ins = refs[:8], refs[8:16]
        before_ref, normed_ref, sum_ref, down_buf, down_sems, up_buf, up_sems = refs[16:]
        slot = stream_quarters(where_ref, down_ins, down_buf, down_sems)
        stream_quarters(where_ref, up_ins, up_buf, up_sems)
        down_weights, up_weights = down_buf.at[slot], up_buf.at[slot]
        step = pl.program_id(0)
        total = jnp.zeros((1, width), jnp.float32)
        for t in range(rows // TILE):
            r = pl.ds(t * TILE, TILE)
            d_act = times_t(d_ref[r, :], down_weights[...])
            d_before = (d_act * slope_ref[r, :].astype(jnp.float32)).astype(jnp.bfloat16)
            before_ref[r, :] = d_before
            total = total + jnp.sum(d_before.astype(jnp.float32), axis=0, keepdims=True)
            term = times_t(d_before, up_weights[...])

            @pl.when(step == 0)
            def _():
                normed_ref[r, :] = term

            @pl.when(step > 0)
            def _():
                normed_ref[r, :] += term

        sum_ref[...] = total

    outs = [
        jax.ShapeDtypeStruct((rows, 4 * width), jnp.bfloat16),
        jax.ShapeDtypeStruct((rows, width), jnp.float32),
        jax.ShapeDtypeStruct((1, 4 * width), jnp.float32),
    ]
    return quarter_call(
        body,
        where,
        (d_feed, slope),
        [fixed(d_feed), moving(rows, width)],
        list(down_pieces) + list(up_pieces),
        outs,
        [moving(rows, width), fixed(outs[1]), moving(1, width)],
        quarter_scratch(width) * 2,
        16 * rows * width * width,
        "feed_back",
    )


def project(where, inputs, query_bias, value_bias, pieces):
    rows, width = inputs.shape

    def body(where_ref, x_ref, query_ref, value_ref, *refs):
        ins, (q_ref, k_ref, v_ref, all_ref, buf, sems, out_sems) = refs[:8], refs[8:]
        base = where_ref[2] * 2 + where_ref[3]

        def loads(quarter, place):
            return load_quarter(where_ref, ins, quarter, buf.at[place], sems.at[place])

        for place in range(4):
            for quarter in range(4):

                @pl.when((base ^ place) == quarter)
                def _(place=place, quarter=quarter):
                    for copy in loads(quarter, place):
                        copy.start()

        stores = []
        biases = (query_ref, None, value_ref, None)
        for place, out_ref in enumerate((q_ref, k_ref, v_ref, None)):
            for copy in loads(0, place):
                copy.wait()
            stores.append(
                pltpu.make_async_copy(buf.at[place], all_ref.at[place], out_sems.at[place])
            )
            stores[-1].start()
            if out_ref is None:
                continue
            for t in range(rows // TILE):
                r = pl.ds(t * TILE, TILE)
                term = jnp.dot(x_ref[r, :], buf[place], preferred_element_type=jnp.float32)
                if biases[place] is not None:
                    term = term + biases[place][...]
                out_ref[r, :] = term.astype(jnp.bfloat16)
        for store in stores:
            store.wait()

    low = jax.ShapeDtypeStruct((rows, width), jnp.bfloat16)
    every = jax.ShapeDtypeStruct((4, width, width), jnp.bfloat16)
    spec = pl.BlockSpec((rows, width), lambda i, w: (0, 0), pipeline_mode=pl.Buffered(1))
    return pl.pallas_call(
        body,
        grid_spec=pltpu.PrefetchScalarGridSpec(
            num_scalar_prefetch=1,
            grid=(1,),
            in_specs=[spec, fixed(query_bias), fixed(value_bias)]
            + [pl.BlockSpec(memory_space=pl.ANY)] * 8,
            out_specs=[spec] * 3 + [pl.BlockSpec(memory_space=pl.ANY)],
            scratch_shapes=[
                pltpu.VMEM((4, width, width), jnp.bfloat16),
                pltpu.SemaphoreType.DMA((4, 8)),
                pltpu.SemaphoreType.DMA((4,)),
            ],
        ),
        out_shape=[low, low, low, every],
        compiler_params=pltpu.CompilerParams(vmem_limit_bytes=58 << 20),
        cost_estimate=pl.CostEstimate(
            flops=6 * rows * width * width, bytes_accessed=30 << 20, transcendentals=0
        ),
        name="project",
    )(where, inputs, query_bias, value_bias, *pieces)


def project_back(parts, matrices):
    rows = parts[0].shape[0]
    width = matrices.shape[1]
    cut = width - parts[1].shape[1]

    def body(*refs):
        ins, (w_ref, out_ref) = refs[:6], refs[6:]
        total = None
        for i in range(3):
            for ref, start, stop in ((ins[2 * i], 0, cut), (ins[2 * i + 1], cut, width)):
                term = times_t(ref[:, : stop - start], w_ref[i, :, start:stop])
                total = term if total is None else total + term
        out_ref[...] = total

    return pl.pallas_call(
        body,
        grid=(rows // TILE,),
        in_specs=[pl.BlockSpec((TILE, a.shape[1]), lambda i: (i, 0)) for a in parts]
        + [
            pl.BlockSpec(
                (3, width, width), lambda i: (0, 0, 0), pipeline_mode=pl.Buffered(1)
            )
        ],
        out_specs=pl.BlockSpec((TILE, width), lambda i: (i, 0)),
        out_shape=jax.ShapeDtypeStruct((rows, width), jnp.float32),
        compiler_params=pltpu.CompilerParams(vmem_limit_bytes=40 << 20),
        cost_estimate=pl.CostEstimate(
            flops=6 * rows * width * width, bytes_accessed=20 << 20, transcendentals=0
        ),
        name="project_back",
    )(*parts, matrices)


def bias_sums(mods, parts, d_branch, up_sums, d_feed):
    width = d_feed.shape[1]
    cut = width - parts[1].shape[1]

    def body(mods_ref, qa_ref, qb_ref, va_ref, vb_ref, branch_ref, up_ref, feed_ref, out_ref):
        @pl.when(pl.program_id(0) == 0)
        def _():
            out_ref[...] = jnp.zeros_like(out_ref)
            out_ref[0:6, :] = mods_ref[...].astype(jnp.float32)
            out_ref[9:13, :] = up_ref[...]

        for row, ref, start, stop in (
            (6, qa_ref, 0, cut),
            (6, qb_ref, cut, width),
            (7, va_ref, 0, cut),
            (7, vb_ref, cut, width),
            (8, branch_ref, 0, width),
            (13, feed_ref, 0, width),
        ):
            terms = ref[:, : stop - start].astype(jnp.float32)
            out_ref[row : row + 1, start:stop] += jnp.sum(terms, axis=0, keepdims=True)

    def tile(array):
        return pl.BlockSpec((256, array.shape[1]), lambda i: (i, 0))

    def held(array):
        return pl.BlockSpec(array.shape, lambda i: (0, 0))

    out = jax.ShapeDtypeStruct((14, width), jnp.float32)
    return pl.pallas_call(
        body,
        grid=(d_feed.shape[0] // 256,),
        in_specs=[held(mods)]
        + [tile(a) for a in parts]
        + [tile(d_branch), held(up_sums), tile(d_feed)],
        out_specs=held(out),
        out_shape=out,
        compiler_params=pltpu.CompilerParams(vmem_limit_bytes=16 << 20),
        cost_estimate=pl.CostEstimate(flops=8 << 20, bytes_accessed=10 << 20, transcendentals=0),
        name="bias_sums",
    )(mods, *parts, d_branch, up_sums, d_feed)


def local_pairs(
    latent_in,
    conditioning,
    ada_weight,
    qkv_weight,
    proj_weight,
    up_weight,
    down_weight,
    bias_pack,
    cotangent,
):
    width = latent_in.shape[2]
    half_rows = latent_in.shape[1]
    zi, xi, ci, yi = [lax.axis_index(name) for name in ALL]
    device = ((zi * 2 + xi) * 2 + ci) * 2 + yi
    where = jnp.stack([zi, xi, ci, yi]).astype(jnp.int32)
    rows = width // 32

    quarter = ci * 2 + yi

    def in_order(array):
        return jnp.stack(
            [lax.dynamic_index_in_dim(array, quarter ^ step, 0, False) for step in range(4)]
        )

    def exchange(array):
        return lax.all_to_all(array, ALL, 0, 0, tiled=True)

    def exchange_quarters(array):
        got = [lax.dynamic_index_in_dim(array, quarter, 0, False)]
        for step, axes in ((1, "y"), (2, "c"), (3, ("c", "y"))):
            entry = lax.dynamic_index_in_dim(array, quarter ^ step, 0, False)
            got.append(
                swap(entry, axes)
                if step < 3
                else lax.ppermute(entry, axes, [(i, i ^ 3) for i in range(4)])
            )
        return in_order(jnp.stack(got))

    def to_all(vector):
        return exchange(jnp.broadcast_to(vector, (32,) + vector.shape))

    def over_tokens(left, right):
        return lax.dot_general(
            left, right, (((0,), (0,)), ((), ())), preferred_element_type=jnp.float32
        )

    def times_transposed(left, right):
        return lax.dot_general(
            left, right, (((1,), (1,)), ((), ())), preferred_element_type=jnp.float32
        )

    qkv_rows = qkv_weight.reshape(rows, 3 * width)
    quarters = jnp.stack(
        [qkv_rows[:, i * width : (i + 1) * width] for i in range(3)]
        + [proj_weight.reshape(rows, width)]
    )
    up_quarters = up_weight.reshape(rows, 8, 4, 144).transpose(2, 0, 1, 3).reshape(4, rows, width)
    units = exchange_quarters(jnp.concatenate([quarters, up_quarters], axis=1))
    unit_a = units[:, :rows].reshape(4 * rows, width)
    unit_u = units[:, rows:].reshape(4 * rows, width)
    unit_d = down_weight.reshape(4 * rows, width)
    hops_a = line_hops(lambda step: unit_a)
    other_half = after(lax.dynamic_index_in_dim(latent_in, 1 - yi, 0, False), unit_a)
    half_received = swap(other_half, "y")
    line_a = jnp.stack([after(unit_a, half_received), *hops_a])
    plane_a = plane_gather(line_a)
    unit_u = after(unit_u, line_a)
    hops_u = line_hops(lambda step: unit_u)
    own_condition = lax.dynamic_index_in_dim(conditioning, yi, 0, False)
    small = to_all(after(jnp.concatenate([bias_pack, own_condition]), line_a))
    bias_share = bias_pack.shape[0]
    biases = small[:, :bias_share].reshape(-1).astype(jnp.float32)
    conditions = small[:, bias_share:].astype(jnp.float32)
    silu_all = jax.nn.silu(conditions).astype(jnp.bfloat16)
    silu_cut = lax.dynamic_slice(silu_all, (0, device * rows), (32, rows))
    ada_rows = ada_weight.reshape(rows, 6 * width)
    shares = jnp.dot(silu_cut, ada_rows, preferred_element_type=jnp.float32)
    first_shares, later_shares = shares[:, : 2 * width], shares[:, 2 * width :]
    line_a, plane_a, hops_u, first_shares = lax.optimization_barrier(
        (line_a, plane_a, hops_u, first_shares)
    )
    corner_a = corner_gather(*plane_a)
    core_a = [swap(p, "c") for p in (line_a, *plane_a)]
    first_shares = after(first_shares, *core_a)
    modulations = jnp.sum(exchange(first_shares), axis=0, keepdims=True)
    modulations = modulations + biases[: 2 * width]
    shift_attention, scale_attention = jnp.split(modulations, 2, axis=1)
    own_half = lax.dynamic_index_in_dim(latent_in, yi, 0, False)
    tokens_low = jnp.concatenate([own_half, half_received])
    tokens = tokens_low.astype(jnp.float32)
    normed = norm_modulate(tokens, shift_attention, scale_attention).astype(jnp.bfloat16)
    line_u = jnp.stack([unit_u, *hops_u])
    unit_d = after(unit_d, line_u, *core_a)
    hops_d = line_hops(lambda step: unit_d)
    corner_a = after(corner_a, unit_d, modulations)
    core_a.append(swap(corner_a, "c"))
    line_u = after(line_u, core_a[3])
    plane_u = plane_gather(line_u)
    query_bias = biases[None, 6 * width : 7 * width]
    value_bias = biases[None, 7 * width : 8 * width]
    proj_bias = biases[8 * width : 9 * width]
    up_bias = biases[9 * width : 9 * width + FF].reshape(8, 4, 144).transpose(1, 0, 2)
    up_bias = in_order(up_bias.reshape(4, width)).reshape(1, FF)
    down_bias = biases[None, 9 * width + FF :]
    queries, keys, values, matrices = project(
        where,
        normed,
        query_bias,
        value_bias,
        after([line_a, *plane_a, corner_a, *core_a], line_u, unit_d),
    )
    proj_matrix = matrices[3]
    line_d = jnp.stack([after(unit_d, values), *hops_d])
    plane_u = after(plane_u, line_d)
    corner_u = corner_gather(*plane_u)
    core_u = [swap(p, "c") for p in (after(line_u, line_d), *plane_u)]
    part_one = attn_fwd(after(queries, *plane_u, line_d), keys, values, (0, 8))
    line_d, corner_u, core_u = after((line_d, corner_u, core_u), *part_one)
    core_u.append(swap(corner_u, "c"))
    plane_d = plane_gather(line_d)
    attended, log_total = attn_fwd(
        after(queries, line_d, *core_u[:3]), keys, values, (8, 8), tuple(part_one)
    )
    later_modulations = jnp.sum(after(exchange(after(later_shares, line_u)), *part_one), axis=0, keepdims=True)
    later_modulations = later_modulations + biases[2 * width : 6 * width]
    gate_attention, shift_feed, scale_feed, gate_feed = jnp.split(later_modulations, 4, axis=1)
    branch = (
        jnp.dot(attended, proj_matrix, preferred_element_type=jnp.float32)
        + proj_bias
    )
    middle = tokens + gate_attention * branch
    normed_feed = norm_modulate(middle, shift_feed, scale_feed).astype(jnp.bfloat16)
    pieces_u = after([line_u, *plane_u, corner_u, *core_u], normed_feed)
    plane_d = after(plane_d, normed_feed)
    corner_d = corner_gather(*plane_d)
    core_d = [swap(p, "c") for p in (after(line_d, normed_feed), *plane_d)]
    other_cotangent = after(lax.dynamic_index_in_dim(cotangent, 1 - yi, 0, False), *plane_d)
    cotangent_received = swap(other_cotangent, "y")
    activated, slope = feed_up(
        where,
        after(normed_feed, *core_d[:3], other_cotangent),
        up_bias,
        pieces_u,
    )
    activated, corner_d = lax.optimization_barrier((activated, corner_d))
    core_d.append(swap(corner_d, "c"))
    pieces_d = after([line_d, *plane_d, corner_d, *core_d], activated)
    feed_out, output_low = feed_down(where, activated, middle, gate_feed, down_bias, pieces_d)
    cotangent_received, output_low = lax.optimization_barrier((cotangent_received, output_low))
    own_cotangent = lax.dynamic_index_in_dim(cotangent, yi, 0, False)
    upstream = jnp.concatenate([own_cotangent, cotangent_received]).astype(jnp.float32)
    d_feed = (gate_feed * upstream).astype(jnp.bfloat16)
    ours, others = slice(None, 2 * width), slice(2 * width, None)
    down_sent = over_tokens(activated[:, others], d_feed).astype(jnp.bfloat16)
    down_received = swap(down_sent, "c")
    output_received = swap(after(output_low, down_sent)[half_rows:], "y")
    d_gate_feed = jnp.sum(upstream * feed_out, axis=0, keepdims=True)
    down_half = over_tokens(after(activated, down_sent)[:, ours], d_feed)
    down = ScatterSum(rows_of, add_low(down_half, down_received), (0, 1))
    down.corner()
    d_before, d_normed_feed, before_sums = feed_back(
        where, after(d_feed, *down.sent), slope, pieces_d, pieces_u
    )
    output_received, d_before = lax.optimization_barrier((output_received, d_before))
    down.plane(d_normed_feed)
    up_sent = over_tokens(after(normed_feed, *down.sent), d_before[:, others])
    up_sent = up_sent.astype(jnp.bfloat16)
    up_received = swap(up_sent, "c")
    unused_norm, norm_pull = jax.vjp(norm_modulate, middle, shift_feed, scale_feed)
    d_middle_part, d_shift_feed, d_scale_feed = norm_pull(
        after(d_normed_feed, up_sent)
    )
    d_middle = upstream + d_middle_part
    d_gate_attention = jnp.sum(d_middle * branch, axis=0, keepdims=True)
    d_branch = (gate_attention * d_middle).astype(jnp.bfloat16)
    d_attended = times_transposed(d_branch, proj_matrix).astype(jnp.bfloat16)
    mods_early = jnp.concatenate([d_gate_attention, d_shift_feed, d_scale_feed, d_gate_feed], 1)
    mods_early = mods_early.astype(jnp.bfloat16)
    up_half = over_tokens(after(normed_feed, d_attended), d_before[:, ours])
    up = ScatterSum(columns_of, add_low(up_half, up_received), (0, 1))
    down.line(up.half)
    up.corner()
    log_rows = log_total[:, :H].T
    part_a = attn_bwd(
        queries,
        keys,
        values,
        after(d_attended, *up.sent, *down.sent, mods_early),
        log_rows,
        (0, 8),
    )

    def attention_terms(gradients, d_b, core, *earlier):
        d_q, d_k, d_v = gradients
        left = after(normed, *earlier)
        first = over_tokens(left, jnp.where(core == 0, d_q, d_v))
        second = over_tokens(
            jnp.where(core == 0, left, attended), jnp.where(core == 0, d_k, d_b)
        )
        return jnp.concatenate([first, second])

    left_terms = [a[:, :512] for a in part_a], d_branch[:, :512]
    left_sent = attention_terms(*left_terms, 1 - ci, *part_a, *down.got, *up.got)
    left_sent = left_sent.astype(jnp.bfloat16)
    left_received = swap(left_sent, "c")
    up.plane(left_sent)
    left_half = attention_terms(*left_terms, ci, left_sent, *up.sent)
    left = ScatterSum(rows_of, add_low(left_half, left_received), (yi, 1 - yi))
    left.corner()
    down_sum = down.total(left_half)
    part_b = attn_bwd(
        queries,
        keys,
        values,
        after(d_attended, *left.sent, down_sum),
        log_rows,
        (8, 4),
        part_a,
    )
    part_b = after(tuple(part_b), *left.got, *up.got)
    left.plane(*part_b)
    up.line(*part_b)
    part_c = attn_bwd(
        queries,
        keys,
        values,
        after(d_attended, *left.sent, *up.sent),
        log_rows,
        (12, 4),
        part_b,
    )
    part_c = after(tuple(part_c), *left.got, *up.got)
    right_parts = [
        jnp.concatenate([b[:, :256], c], axis=1) for b, c in zip(part_b, part_c)
    ]
    right_terms = right_parts, d_branch[:, 512:]
    left.line(*part_c)
    right_sent = attention_terms(*right_terms, 1 - ci, *left.sent).astype(jnp.bfloat16)
    right_received = swap(right_sent, "c")
    right_half = attention_terms(*right_terms, ci, right_sent)
    right = ScatterSum(rows_of, add_low(right_half, right_received), (yi, 1 - yi))
    right.corner()
    parts = [array for pair in zip(part_a, right_parts) for array in pair]
    d_normed = project_back(after(parts, *right.sent, *left.got), matrices)
    right.plane(d_normed)
    up_sum = exchange_quarters(up.total(*right.sent).reshape(4, rows, width))
    unused_first, first_pull = jax.vjp(norm_modulate, tokens, shift_attention, scale_attention)
    d_tokens_part, d_shift_attention, d_scale_attention = first_pull(after(d_normed, *right.sent))
    grad_low = (d_middle + d_tokens_part).astype(jnp.bfloat16)
    grad_low, up_sum = lax.optimization_barrier((grad_low, up_sum))
    mods = jnp.concatenate([d_shift_attention, d_scale_attention], axis=1).astype(jnp.bfloat16)
    mods = jnp.concatenate([mods, mods_early], axis=1)
    every_mods = to_all(mods.reshape(2, 3 * width)).reshape(32, 6 * width)
    right.line(grad_low, mods)
    quarter_rows = half_rows // 2
    grad_first = swap(grad_low[half_rows : half_rows + quarter_rows], "y")

    def both_halves(own_rows, *received):
        both = jnp.stack([own_rows, own_rows])
        row = 0
        for piece in received:
            both = lax.dynamic_update_slice(both, piece[None], (1 - yi, row, 0))
            row += piece.shape[0]
        return both

    left_totals = left.total(*right.sent)
    down_sum, output_low, output_received, up_sum = after(
        (down_sum, output_low, output_received, up_sum), *right.sent
    )
    output = both_halves(output_low[:half_rows], output_received)
    grad_down = down_sum.reshape(-1)
    grad_up = up_sum.reshape(4, rows, 8, 144).transpose(1, 2, 0, 3).reshape(-1)
    up_sums = in_order(before_sums.reshape(4, width)).reshape(4, 8, 144).transpose(1, 0, 2)
    bias_terms = bias_sums(
        mods.reshape(6, width),
        after((part_a[0], right_parts[0], part_a[2], right_parts[2]), *right.sent),
        d_branch,
        up_sums.reshape(4, width),
        d_feed,
    ).reshape(32, -1)
    right_totals = right.total(left_totals, output, grad_down, grad_up, bias_terms)
    sums = jnp.concatenate([left_totals, right_totals], axis=1).reshape(4, rows, width)
    sums = exchange_quarters(sums)
    every_mods, grad_first = lax.optimization_barrier((every_mods, grad_first))
    grad_last = swap(after(grad_low, grad_first)[half_rows + quarter_rows :], "y")
    d_silu_rows = times_transposed(every_mods, ada_rows)
    d_silu_parts = jnp.repeat(d_silu_rows.reshape(16, 1, 2, rows), 2, axis=1)
    parts = exchange(
        jnp.concatenate([d_silu_parts.reshape(32, 2 * rows), bias_terms], axis=1)
    )
    grad_ada = over_tokens(silu_cut, every_mods).reshape(-1)
    parts, grad_last = lax.optimization_barrier((parts, grad_last))
    d_silu = parts[:, : 2 * rows].reshape(32, 2, rows).transpose(1, 0, 2).reshape(2, width)
    grad_bias = jnp.sum(parts[:, 2 * rows :], axis=0)
    unused_silu, silu_pull = jax.vjp(jax.nn.silu, conditioning.astype(jnp.float32))
    grad_cond = silu_pull(d_silu)[0].astype(jnp.bfloat16)
    grad_input = both_halves(grad_low[:half_rows], grad_first, grad_last)
    grad_qkv = jnp.concatenate([sums[0], sums[1], sums[2]], axis=1).reshape(-1)
    grad_proj = sums[3].reshape(-1)
    return (
        output,
        grad_input,
        grad_cond,
        grad_ada,
        grad_qkv,
        grad_proj,
        grad_up,
        grad_down,
        grad_bias,
    )


def local_any(
    latent_in,
    conditioning,
    ada_weight,
    qkv_weight,
    proj_weight,
    up_weight,
    down_weight,
    bias_pack,
    cotangent,
):
    model_width = latent_in.shape[2]
    every_param = (
        lax.all_gather(ada_weight, ("batch", "seq"), axis=0, tiled=True),
        lax.all_gather(qkv_weight, ("batch", "seq"), axis=0, tiled=True),
        lax.all_gather(proj_weight, ("batch", "seq"), axis=0, tiled=True),
        lax.all_gather(up_weight, ("batch", "seq"), axis=0, tiled=True),
        lax.all_gather(down_weight, ("batch", "seq"), axis=0, tiled=True),
        lax.all_gather(bias_pack, ("batch", "seq"), axis=0, tiled=True),
    )
    ada_matrix, qkv_matrix, proj_matrix, up_matrix, down_matrix, biases = shape_all(
        every_param, model_width
    )
    ada_bias = biases[: 6 * model_width]
    query_bias = biases[6 * model_width : 7 * model_width]
    value_bias = biases[7 * model_width : 8 * model_width]
    proj_bias = biases[8 * model_width : 9 * model_width]
    up_bias = biases[9 * model_width : 9 * model_width + FF]
    down_bias = biases[9 * model_width + FF :]
    tokens = latent_in.astype(jnp.float32)
    conditions = conditioning.astype(jnp.float32)
    silu_cond = jax.nn.silu(conditions).astype(jnp.bfloat16)
    modulations = jnp.dot(silu_cond, ada_matrix, preferred_element_type=jnp.float32) + ada_bias
    shift_attention, scale_attention, gate_attention, shift_feed, scale_feed, gate_feed = jnp.split(
        modulations[:, None, :], 6, axis=2
    )
    normed = norm_modulate(tokens, shift_attention, scale_attention).astype(jnp.bfloat16)
    projected = jnp.einsum("btd,df->btf", normed, qkv_matrix, preferred_element_type=jnp.float32)
    queries = (projected[..., :model_width] + query_bias).astype(jnp.bfloat16)
    own_keys = jnp.concatenate(
        [
            projected[..., model_width : 2 * model_width],
            projected[..., 2 * model_width :] + value_bias,
        ],
        axis=2,
    ).astype(jnp.bfloat16)
    every_keys = lax.all_gather(own_keys, "seq", axis=1, tiled=True)
    attended, log_total = lax.map(attend_latent, (queries, every_keys))
    attended = attended.astype(jnp.bfloat16)
    branch = (
        jnp.einsum("btd,de->bte", attended, proj_matrix, preferred_element_type=jnp.float32)
        + proj_bias
    )
    middle = tokens + gate_attention * branch
    normed_feed = norm_modulate(middle, shift_feed, scale_feed).astype(jnp.bfloat16)
    before = (
        jnp.einsum("btd,df->btf", normed_feed, up_matrix, preferred_element_type=jnp.float32)
        + up_bias
    )
    activated = gelu_tanh(before).astype(jnp.bfloat16)
    feed_out = (
        jnp.einsum("btf,fd->btd", activated, down_matrix, preferred_element_type=jnp.float32)
        + down_bias
    )
    output = (middle + gate_feed * feed_out).astype(jnp.bfloat16)
    param_again = (
        lax.all_gather(ada_weight, ("batch", "seq"), axis=0, tiled=True),
        lax.all_gather(qkv_weight, ("batch", "seq"), axis=0, tiled=True),
        lax.all_gather(proj_weight, ("batch", "seq"), axis=0, tiled=True),
        lax.all_gather(up_weight, ("batch", "seq"), axis=0, tiled=True),
        lax.all_gather(down_weight, ("batch", "seq"), axis=0, tiled=True),
        lax.all_gather(bias_pack, ("batch", "seq"), axis=0, tiled=True),
    )
    ada_matrix, qkv_matrix, proj_matrix, up_matrix, down_matrix, biases = shape_all(
        param_again, model_width
    )
    upstream = cotangent.astype(jnp.float32)
    d_gate_feed = jnp.sum(upstream * feed_out, axis=1, keepdims=True)
    d_feed = (gate_feed * upstream).astype(jnp.bfloat16)
    d_activated = jnp.einsum("btd,fd->btf", d_feed, down_matrix, preferred_element_type=jnp.float32)
    unused_gelu, gelu_pull = jax.vjp(gelu_tanh, before)
    d_before = gelu_pull(d_activated)[0].astype(jnp.bfloat16)
    d_normed_feed = jnp.einsum(
        "btf,df->btd", d_before, up_matrix, preferred_element_type=jnp.float32
    )
    unused_norm, norm_pull = jax.vjp(norm_modulate, middle, shift_feed, scale_feed)
    d_middle_part, d_shift_feed, d_scale_feed = norm_pull(d_normed_feed)
    d_middle = upstream + d_middle_part
    d_gate_attention = jnp.sum(d_middle * branch, axis=1, keepdims=True)
    d_branch = (gate_attention * d_middle).astype(jnp.bfloat16)
    d_attended = jnp.einsum(
        "bte,de->btd", d_branch, proj_matrix, preferred_element_type=jnp.float32
    ).astype(jnp.bfloat16)
    d_queries, d_every = lax.map(attend_back, (queries, every_keys, log_total, d_attended))
    d_queries = d_queries.astype(jnp.bfloat16)
    d_own = lax.psum_scatter(d_every.astype(jnp.bfloat16), "seq", scatter_dimension=1, tiled=True)
    d_projected = jnp.concatenate([d_queries, d_own], axis=2)
    d_normed = jnp.einsum(
        "btf,df->btd", d_projected, qkv_matrix, preferred_element_type=jnp.float32
    )
    unused_first, first_pull = jax.vjp(norm_modulate, tokens, shift_attention, scale_attention)
    d_tokens_part, d_shift_attention, d_scale_attention = first_pull(d_normed)
    grad_input = (d_middle + d_tokens_part).astype(jnp.bfloat16)
    local_mods = jnp.concatenate(
        [
            d_shift_attention,
            d_scale_attention,
            d_gate_attention,
            d_shift_feed,
            d_scale_feed,
            d_gate_feed,
        ],
        axis=2,
    )[:, 0, :]
    d_mods = lax.psum(local_mods.astype(jnp.bfloat16), "seq")
    d_silu = jnp.einsum("bf,df->bd", d_mods, ada_matrix, preferred_element_type=jnp.float32)
    unused_silu, silu_pull = jax.vjp(jax.nn.silu, conditions)
    grad_cond = silu_pull(d_silu)[0].astype(jnp.bfloat16)
    is_owner = lax.axis_index("seq") == 0
    owned_mods = jnp.where(is_owner, d_mods, jnp.zeros_like(d_mods))
    bias_terms = jnp.concatenate(
        [
            jnp.sum(owned_mods, axis=0, dtype=jnp.float32),
            jnp.sum(d_queries, axis=(0, 1), dtype=jnp.float32),
            jnp.sum(d_own[..., model_width:], axis=(0, 1), dtype=jnp.float32),
            jnp.sum(d_branch, axis=(0, 1), dtype=jnp.float32),
            jnp.sum(d_before, axis=(0, 1), dtype=jnp.float32),
            jnp.sum(d_feed, axis=(0, 1), dtype=jnp.float32),
        ]
    )
    matrix_terms = [
        (silu_cond, owned_mods, ada_weight.shape[0]),
        (
            normed.reshape(-1, model_width),
            d_projected.reshape(-1, 3 * model_width),
            qkv_weight.shape[0],
        ),
        (
            attended.reshape(-1, model_width),
            d_branch.reshape(-1, model_width),
            proj_weight.shape[0],
        ),
        (normed_feed.reshape(-1, model_width), d_before.reshape(-1, FF), up_weight.shape[0]),
        (activated.reshape(-1, FF), d_feed.reshape(-1, model_width), down_weight.shape[0]),
    ]
    bias_share = bias_pack.shape[0]
    shard_rows = sum((entry[2] for entry in matrix_terms)) + bias_share
    block_count = shard_rows * lax.axis_size(("batch", "seq")) // shard_rows
    pieces = []
    for left, right, grad_shard_size in matrix_terms:
        pieces.append(flat_term(left, right).reshape(block_count, grad_shard_size))
    pieces.append(bias_terms.reshape(block_count, bias_share))
    owned_grads = lax.psum_scatter(
        jnp.concatenate(pieces, axis=1).reshape(-1),
        ("batch", "seq"),
        scatter_dimension=0,
        tiled=True,
    )
    results = []
    cursor = 0
    for shard_size in [entry[2] for entry in matrix_terms] + [bias_share]:
        results.append(owned_grads[cursor : cursor + shard_size])
        cursor = cursor + shard_size
    grad_ada, grad_qkv, grad_proj, grad_up, grad_down, grad_bias = results
    return (
        output,
        grad_input,
        grad_cond,
        grad_ada,
        grad_qkv,
        grad_proj,
        grad_up,
        grad_down,
        grad_bias,
    )


def solution(mesh):
    batch, seq = mesh.shape["batch"], mesh.shape["seq"]
    if (batch, seq) == (16, 2):
        inner = Mesh(mesh.devices.reshape(4, 2, 2, 2), ALL)
        body, tokens = local_pairs, ("z", "x", "c")
        flat, split = P(ALL), "y"
    else:
        inner, body, tokens, split = mesh, local_any, "batch", "seq"
        flat = P(("batch", "seq"))
    activations = P(tokens, split, None)
    vectors = P(tokens, None)
    in_specs = (activations, vectors) + (flat,) * 6 + (activations,)
    out_specs = (activations, activations, vectors) + (flat,) * 6
    return jax.shard_map(body, mesh=inner, in_specs=in_specs, out_specs=out_specs, check_vma=False)
```

```python
import functools
import itertools

import jax
import jax.numpy as jnp
from jax import lax
from jax.experimental import pallas as pl
from jax.experimental.pallas import tpu as pltpu
from jax.sharding import Mesh
from jax.sharding import PartitionSpec as P

H = 16
HD = 72
FF = 4608


EPS = 1e-06
GELU_COEF = 0.7978845608028654
SCALE = HD ** (-0.5)
LOG2E = 1.4426950408889634
WIN = 256
ALL = ("z", "x", "c", "y")
SWAP = [(0, 1), (1, 0)]


def norm_modulate(inputs, shift_term, scale_term):
    center = inputs - jnp.mean(inputs, axis=-1, keepdims=True)
    spread = jnp.mean(center * center, axis=-1, keepdims=True)
    return center * lax.rsqrt(spread + EPS) * (1.0 + scale_term) + shift_term


def gelu_tanh(values):
    return (
        0.5 * values * (1.0 + jnp.tanh(GELU_COEF * (values + 0.044715 * values * values * values)))
    )


def flat_term(left, right):
    product = jnp.einsum("nd,nf->df", left, right, preferred_element_type=jnp.float32).reshape(-1)
    return product


def split_heads(queries, keys_values):
    query_rows = queries.shape[0]
    key_rows = keys_values.shape[0]
    model_width = queries.shape[1]
    query_heads = queries.reshape(query_rows, H, HD)
    key_heads = keys_values[:, :model_width].reshape(key_rows, H, HD)
    value_heads = keys_values[:, model_width:].reshape(key_rows, H, HD)
    scores = jnp.einsum(
        "qhe,khe->hqk", query_heads, key_heads, preferred_element_type=jnp.float32
    ) * HD ** (-0.5)
    return (query_heads, key_heads, value_heads, scores)


def attend_latent(block_items):
    queries, keys_values = block_items
    query_heads, key_heads, value_heads, scores = split_heads(queries, keys_values)
    top_score = jnp.max(scores, axis=-1, keepdims=True)
    exp_scores = jnp.exp(scores - top_score)
    exp_total = jnp.sum(exp_scores, axis=-1, keepdims=True)
    probs_low = (exp_scores / exp_total).astype(jnp.bfloat16)
    attended = jnp.einsum(
        "hqk,khe->qhe", probs_low, value_heads, preferred_element_type=jnp.float32
    )
    return (
        attended.reshape(queries.shape[0], queries.shape[1]),
        (top_score + jnp.log(exp_total))[..., 0],
    )


def attend_back(block_items):
    queries, keys_values, log_total, d_attended = block_items
    query_rows = queries.shape[0]
    key_rows = keys_values.shape[0]
    model_width = queries.shape[1]
    query_heads, key_heads, value_heads, scores = split_heads(queries, keys_values)
    attention_probs = jnp.exp(scores - log_total[..., None])
    d_heads = d_attended.reshape(query_rows, H, HD)
    d_probs = jnp.einsum("qhe,khe->hqk", d_heads, value_heads, preferred_element_type=jnp.float32)
    centered = d_probs - jnp.sum(attention_probs * d_probs, axis=-1, keepdims=True)
    d_scores = (HD ** (-0.5) * (attention_probs * centered)).astype(jnp.bfloat16)
    d_queries = jnp.einsum("hqk,khe->qhe", d_scores, key_heads, preferred_element_type=jnp.float32)
    d_keys = jnp.einsum("hqk,qhe->khe", d_scores, query_heads, preferred_element_type=jnp.float32)
    d_values = jnp.einsum(
        "hqk,qhe->khe",
        attention_probs.astype(jnp.bfloat16),
        d_heads,
        preferred_element_type=jnp.float32,
    )
    joined = jnp.concatenate(
        [d_keys.reshape(key_rows, model_width), d_values.reshape(key_rows, model_width)], axis=1
    )
    return (d_queries.reshape(query_rows, model_width), joined)


def shape_all(gathered, model_width):
    ada_full, qkv_full, proj_full, up_full, down_full, bias_full = gathered
    return (
        ada_full.reshape(model_width, 6 * model_width),
        qkv_full.reshape(model_width, 3 * model_width),
        proj_full.reshape(model_width, model_width),
        up_full.reshape(model_width, FF),
        down_full.reshape(FF, model_width),
        bias_full.astype(jnp.float32),
    )


def head_window(head, width):
    start = jnp.minimum((head * HD) // 128, width // 128 - 2) * 128
    return pl.multiple_of(start, 128), head * HD - start


def attn_fwd_kernel(q_ref, k_ref, v_ref, *refs, tile, first):
    o_ref, lse_ref = refs[-2:]
    head = pl.program_id(0) + first
    rows, width = q_ref.shape

    if len(refs) > 2:

        @pl.when(pl.program_id(0) == 0)
        def _():
            o_ref[...] = refs[0][...]
            lse_ref[...] = refs[1][...]

    lo, off = head_window(head, width)
    lane = lax.broadcasted_iota(jnp.int32, (1, WIN), 1)
    inside = (lane >= off) & (lane < off + HD)
    keep = inside.astype(jnp.bfloat16)
    kw = k_ref[:, pl.ds(lo, WIN)]
    vw = v_ref[:, pl.ds(lo, WIN)]
    col = lax.broadcasted_iota(jnp.int32, (1, 128), 1) == head
    for t in range(rows // tile):
        r = pl.ds(t * tile, tile)
        qm = q_ref[r, pl.ds(lo, WIN)] * keep
        s = lax.dot_general(qm, kw, (((1,), (1,)), ((), ())), preferred_element_type=jnp.float32)
        top = jnp.max(s, axis=-1, keepdims=True)
        p = jnp.exp2((s - top) * (SCALE * LOG2E))
        total = jnp.sum(p, axis=-1, keepdims=True)
        o = jnp.dot(p.astype(jnp.bfloat16), vw, preferred_element_type=jnp.float32)
        o = o * (1.0 / total)
        old = o_ref[r, pl.ds(lo, WIN)].astype(jnp.float32)
        o_ref[r, pl.ds(lo, WIN)] = jnp.where(inside, o, old).astype(jnp.bfloat16)
        lse_ref[r, :] = jnp.where(col, top * SCALE + jnp.log(total), lse_ref[r, :])


def whole(array_or_shape):
    shape = array_or_shape.shape
    return pl.BlockSpec(shape, lambda h: (0,) * len(shape), pipeline_mode=pl.Buffered(1))


def attn_fwd(q, k, v, heads, into=(), tile=256):
    rows, width = q.shape
    keys = k.shape[0]
    first, count = heads
    outs = [
        jax.ShapeDtypeStruct(q.shape, jnp.bfloat16),
        jax.ShapeDtypeStruct((rows, 128), jnp.float32),
    ]
    ins = (q, k, v, *into)
    return pl.pallas_call(
        functools.partial(attn_fwd_kernel, tile=tile, first=first),
        grid=(count,),
        in_specs=[whole(a) for a in ins],
        out_specs=[whole(a) for a in outs],
        out_shape=outs,
        compiler_params=pltpu.CompilerParams(vmem_limit_bytes=60 << 20),
        cost_estimate=pl.CostEstimate(
            flops=4 * count * rows * keys * WIN,
            bytes_accessed=8 * rows * width,
            transcendentals=count * rows * keys,
        ),
        name="attention_forward",
    )(*ins)


def attn_bwd_kernel(q_ref, k_ref, v_ref, g_ref, lse_ref, *refs, tile, first, origin):
    dq_ref, dk_ref, dv_ref = refs[-3:]
    head = pl.program_id(0) + first
    rows, width = q_ref.shape
    keys = k_ref.shape[0]

    if len(refs) > 3:

        @pl.when(pl.program_id(0) == 0)
        def _():
            dq_ref[:, :128] = refs[0][...]
            dk_ref[:, :128] = refs[1][...]
            dv_ref[:, :128] = refs[2][...]

    lo, off = head_window(head, origin + dq_ref.shape[1])
    there = pl.ds(pl.multiple_of(lo - origin, 128), WIN)
    lane = lax.broadcasted_iota(jnp.int32, (1, WIN), 1)
    inside = (lane >= off) & (lane < off + HD)
    keep = inside.astype(jnp.bfloat16)
    kw = k_ref[:, pl.ds(lo, WIN)]
    vw = v_ref[:, pl.ds(lo, WIN)]
    ktw = kw.T
    dk = jnp.zeros((keys, WIN), jnp.float32)
    dv = jnp.zeros((keys, WIN), jnp.float32)
    for t in range(rows // tile):
        r = pl.ds(t * tile, tile)
        lse = lse_ref[pl.ds(head, 1), r]
        qw = q_ref[r, pl.ds(lo, WIN)]
        gw = g_ref[r, pl.ds(lo, WIN)]
        st = jnp.dot(kw, (qw * keep).T, preferred_element_type=jnp.float32)
        pt = jnp.exp2(st * (SCALE * LOG2E) - lse * LOG2E)
        dpt = jnp.dot(vw, (gw * keep).T, preferred_element_type=jnp.float32)
        delta = jnp.sum(pt * dpt, axis=0, keepdims=True)
        dst = (pt * (dpt - delta) * SCALE).astype(jnp.bfloat16)
        dv = dv + jnp.dot(pt.astype(jnp.bfloat16), gw, preferred_element_type=jnp.float32)
        dk = dk + jnp.dot(dst, qw, preferred_element_type=jnp.float32)
        dq = jnp.dot(ktw, dst, preferred_element_type=jnp.float32).T
        old = dq_ref[r, there].astype(jnp.float32)
        dq_ref[r, there] = jnp.where(inside, dq, old).astype(jnp.bfloat16)
    old = dk_ref[:, there].astype(jnp.float32)
    dk_ref[:, there] = jnp.where(inside, dk, old).astype(jnp.bfloat16)
    old = dv_ref[:, there].astype(jnp.float32)
    dv_ref[:, there] = jnp.where(inside, dv, old).astype(jnp.bfloat16)


def head_columns(heads):
    first, count = heads
    return (first * HD) // 128 * 128, -(-((first + count) * HD) // 128) * 128


def attn_bwd(q, k, v, g, lse_rows, heads, before=(), tile=512):
    rows, width = q.shape
    keys = k.shape[0]
    first, count = heads
    start, stop = head_columns(heads)
    outs = [jax.ShapeDtypeStruct((a.shape[0], stop - start), jnp.bfloat16) for a in (q, k, v)]
    ins = (q, k, v, g, lse_rows, *before)
    specs = [whole(a) for a in ins[:5]]
    for array in before:
        last = array.shape[1] // 128 - 1
        specs.append(pl.BlockSpec((array.shape[0], 128), lambda h, last=last: (0, last)))
    return pl.pallas_call(
        functools.partial(attn_bwd_kernel, tile=tile, first=first, origin=start),
        grid=(count,),
        in_specs=specs,
        out_specs=[whole(a) for a in outs],
        out_shape=outs,
        compiler_params=pltpu.CompilerParams(vmem_limit_bytes=60 << 20),
        cost_estimate=pl.CostEstimate(
            flops=10 * count * rows * keys * WIN,
            bytes_accessed=14 * rows * width,
            transcendentals=count * rows * keys,
        ),
        name="attention_backward",
    )(*ins)


def after(array, *earlier):
    if not earlier:
        return array
    return lax.optimization_barrier((array, earlier))[0]


def swap(array, axis):
    return lax.ppermute(array, axis, SWAP)


def line_hops(block_of):
    return [
        lax.ppermute(block_of(step), "z", [(i, i ^ step) for i in range(4)]) for step in range(1, 4)
    ]


def plane_gather(line):
    return swap(line, "x"), swap(line, "y")


def corner_swap(array, first):
    pairs = []
    for x, c, y in itertools.product(range(2), repeat=3):
        along_x = c == first
        target = (1 - x, c, y) if along_x else (x, c, 1 - y)
        pairs.append((x * 4 + c * 2 + y, target[0] * 4 + target[1] * 2 + target[2]))
    return lax.ppermute(array, ("x", "c", "y"), pairs)


def corner_gather(from_x, from_y):
    return corner_swap(jnp.where(lax.axis_index("c") == 0, from_x, from_y), 1)


def add_low(*terms):
    total = terms[0].astype(jnp.float32)
    for term in terms[1:]:
        total = total + term.astype(jnp.float32)
    return total.astype(jnp.bfloat16)


def rows_of(half, yy, xx):
    width = half.shape[1]
    cut = lax.dynamic_slice(
        half.reshape(2, 4, 2, 144, width), (yy, 0, xx, 0, 0), (1, 4, 1, 144, width)
    )
    return cut.reshape(4, 144, width)


def columns_of(half, yy, xx):
    width = half.shape[1] // 2
    cut = lax.dynamic_slice(
        half.reshape(4, 2, 144, 2 * width), (0, xx, 0, yy * width), (4, 1, 144, width)
    )
    return cut.reshape(4, 144, width)


class ScatterSum:
    def __init__(self, part, half, quarters):
        self.part, self.half = part, half
        self.mine, self.theirs = quarters
        self.zi, self.xi = lax.axis_index("z"), lax.axis_index("x")

    def corner(self):
        self.sent = (self.part(self.half, self.theirs, 1 - self.xi),)
        self.got = (corner_swap(self.sent[0], 0),)

    def plane(self, *earlier):
        half, got = after(self.half, *earlier), self.got[0]
        to_y, to_x = self.part(half, self.theirs, self.xi), self.part(half, self.mine, 1 - self.xi)
        even = lax.axis_index("c") == 0
        to_y = jnp.where(even, add_low(to_y, got), to_y)
        to_x = jnp.where(even, to_x, add_low(to_x, got))
        self.sent = to_y, to_x
        self.got = swap(to_y, "y"), swap(to_x, "x")

    def line(self, *earlier):
        half = after(self.half, *earlier)
        own = add_low(self.part(half, self.mine, self.xi), *self.got)
        blocks = [lax.dynamic_index_in_dim(own, self.zi ^ step, 0, False) for step in range(4)]
        self.own, self.sent = blocks[0], blocks[1:]
        self.got = line_hops(lambda step: blocks[step])

    def total(self, *earlier):
        total = after(self.own, *earlier).astype(jnp.float32)
        for hop in self.got:
            total = total + hop.astype(jnp.float32)
        return total


def load_quarter(where_ref, pieces, quarter, buf, sems):
    copies = []
    for x_bit in range(2):
        piece = pieces[quarter * 2 + x_bit]
        xi = where_ref[1] if x_bit == 0 else 1 - where_ref[1]
        height = piece.shape[1]
        for block in range(4):
            row = pl.multiple_of(((where_ref[0] ^ block) * 2 + xi) * height, 16)
            copies.append(
                pltpu.make_async_copy(
                    piece.at[block], buf.at[pl.ds(row, height), :], sems.at[len(copies)]
                )
            )
    return copies


class Quarters:
    def __init__(self, where_ref, pieces, buf, sems):
        self.buf, self.first = buf, pl.program_id(0) == 0
        self.loads = [
            load_quarter(where_ref, pieces, i, buf.at[i], sems.at[i]) for i in range(4)
        ]

    def start(self, i):
        @pl.when(self.first)
        def _():
            for copy in self.loads[i]:
                copy.start()

    def wait(self, i):
        @pl.when(self.first)
        def _():
            for copy in self.loads[i]:
                copy.wait()

        return self.buf.at[i]


def stream_quarters(where_ref, pieces, buf, sems):
    step = pl.program_id(0)
    for i in range(4):

        @pl.when(step == i)
        def _(i=i):
            quarter = load_quarter(where_ref, pieces, i, buf.at[i % 2], sems.at[i % 2])
            if i == 0:
                for copy in quarter:
                    copy.start()
            if i < 3:
                other = (i + 1) % 2
                for copy in load_quarter(
                    where_ref, pieces, i + 1, buf.at[other], sems.at[other]
                ):
                    copy.start()
            for copy in quarter:
                copy.wait()

    return lax.rem(step, 2)


def quarter_scratch(width):
    return [pltpu.VMEM((2, width, width), jnp.bfloat16), pltpu.SemaphoreType.DMA((2, 8))]


def times_t(left, right):
    return lax.dot_general(
        left, right, (((1,), (1,)), ((), ())), preferred_element_type=jnp.float32
    )


def quarter_call(body, where, ins, in_specs, pieces, outs, out_specs, scratch, flops, name):
    return pl.pallas_call(
        body,
        grid_spec=pltpu.PrefetchScalarGridSpec(
            num_scalar_prefetch=1,
            grid=(4,),
            in_specs=in_specs + [pl.BlockSpec(memory_space=pl.ANY)] * len(pieces),
            out_specs=out_specs,
            scratch_shapes=scratch,
        ),
        out_shape=outs,
        compiler_params=pltpu.CompilerParams(vmem_limit_bytes=58 << 20),
        cost_estimate=pl.CostEstimate(
            flops=flops, bytes_accessed=30 << 20, transcendentals=0
        ),
        name=name,
    )(where, *ins, *pieces)


def fixed(array):
    shape = array.shape
    return pl.BlockSpec(shape, lambda i, w: (0,) * len(shape), pipeline_mode=pl.Buffered(1))


def moving(rows, width):
    return pl.BlockSpec((rows, width), lambda i, w: (0, i))


TILE = 512


def feed_up(where, inputs, bias, pieces):
    rows, width = inputs.shape

    def body(where_ref, x_ref, bias_ref, *refs):
        ins, (act_ref, slope_ref, buf, sems) = refs[:8], refs[8:]
        slot = stream_quarters(where_ref, ins, buf, sems)
        weights = buf.at[slot]
        for t in range(rows // TILE):
            r = pl.ds(t * TILE, TILE)
            u = jnp.dot(x_ref[r, :], weights[...], preferred_element_type=jnp.float32)
            u = u + bias_ref[...]
            square = u * u
            bend = jnp.tanh(u * (GELU_COEF + (GELU_COEF * 0.044715) * square))
            half = 0.5 + 0.5 * bend
            slope = (0.5 * GELU_COEF) + (1.5 * GELU_COEF * 0.044715) * square
            act_ref[r, :] = (u * half).astype(jnp.bfloat16)
            slope_ref[r, :] = (half + u * (1.0 - bend * bend) * slope).astype(jnp.bfloat16)

    out = jax.ShapeDtypeStruct((rows, 4 * width), jnp.bfloat16)
    return quarter_call(
        body,
        where,
        (inputs, bias),
        [fixed(inputs), moving(1, width)],
        pieces,
        [out, out],
        [moving(rows, width)] * 2,
        quarter_scratch(width),
        8 * rows * width * width,
        "feed_up",
    )


def feed_down(where, activated, middle, gate, bias, pieces):
    rows, width = middle.shape

    def body(where_ref, act_ref, middle_ref, gate_ref, bias_ref, *refs):
        ins, (feed_ref, out_ref, buf, sems) = refs[:8], refs[8:]
        quarters = Quarters(where_ref, ins, buf, sems)
        for i in range(4):
            quarters.start(i)
        feed = None
        for i in range(4):
            weights = quarters.wait(i)
            term = jnp.dot(
                act_ref[:, i * width : (i + 1) * width],
                weights[...],
                preferred_element_type=jnp.float32,
            )
            feed = term if feed is None else feed + term
        feed = feed + bias_ref[...]
        feed_ref[...] = feed
        out_ref[...] = (middle_ref[...] + gate_ref[...] * feed).astype(jnp.bfloat16)

    outs = [
        jax.ShapeDtypeStruct((rows, width), jnp.float32),
        jax.ShapeDtypeStruct((rows, width), jnp.bfloat16),
    ]
    def tiles(array):
        return pl.BlockSpec((256, array.shape[1]), lambda i, w: (i, 0))

    return pl.pallas_call(
        body,
        grid_spec=pltpu.PrefetchScalarGridSpec(
            num_scalar_prefetch=1,
            grid=(rows // 256,),
            in_specs=[tiles(activated), tiles(middle), fixed(gate), fixed(bias)]
            + [pl.BlockSpec(memory_space=pl.ANY)] * 8,
            out_specs=[tiles(a) for a in outs],
            scratch_shapes=[
                pltpu.VMEM((4, width, width), jnp.bfloat16),
                pltpu.SemaphoreType.DMA((4, 8)),
            ],
        ),
        out_shape=outs,
        compiler_params=pltpu.CompilerParams(vmem_limit_bytes=58 << 20),
        cost_estimate=pl.CostEstimate(
            flops=8 * rows * width * width, bytes_accessed=30 << 20, transcendentals=0
        ),
        name="feed_down",
    )(where, activated, middle, gate, bias, *pieces)


def feed_back(where, d_feed, slope, down_pieces, up_pieces):
    rows, width = d_feed.shape

    def body(where_ref, d_ref, slope_ref, *refs):
        down_ins, up_ins = refs[:8], refs[8:16]
        before_ref, normed_ref, sum_ref, down_buf, down_sems, up_buf, up_sems = refs[16:]
        slot = stream_quarters(where_ref, down_ins, down_buf, down_sems)
        stream_quarters(where_ref, up_ins, up_buf, up_sems)
        down_weights, up_weights = down_buf.at[slot], up_buf.at[slot]
        step = pl.program_id(0)
        total = jnp.zeros((1, width), jnp.float32)
        for t in range(rows // TILE):
            r = pl.ds(t * TILE, TILE)
            d_act = times_t(d_ref[r, :], down_weights[...])
            d_before = (d_act * slope_ref[r, :].astype(jnp.float32)).astype(jnp.bfloat16)
            before_ref[r, :] = d_before
            total = total + jnp.sum(d_before.astype(jnp.float32), axis=0, keepdims=True)
            term = times_t(d_before, up_weights[...])

            @pl.when(step == 0)
            def _():
                normed_ref[r, :] = term

            @pl.when(step > 0)
            def _():
                normed_ref[r, :] += term

        sum_ref[...] = total

    outs = [
        jax.ShapeDtypeStruct((rows, 4 * width), jnp.bfloat16),
        jax.ShapeDtypeStruct((rows, width), jnp.float32),
        jax.ShapeDtypeStruct((1, 4 * width), jnp.float32),
    ]
    return quarter_call(
        body,
        where,
        (d_feed, slope),
        [fixed(d_feed), moving(rows, width)],
        list(down_pieces) + list(up_pieces),
        outs,
        [moving(rows, width), fixed(outs[1]), moving(1, width)],
        quarter_scratch(width) * 2,
        16 * rows * width * width,
        "feed_back",
    )


def project(where, inputs, query_bias, value_bias, pieces):
    rows, width = inputs.shape

    def body(where_ref, x_ref, query_ref, value_ref, *refs):
        ins, (q_ref, k_ref, v_ref, all_ref, buf, sems, out_sems) = refs[:8], refs[8:]
        base = where_ref[2] * 2 + where_ref[3]

        def loads(quarter, place):
            return load_quarter(where_ref, ins, quarter, buf.at[place], sems.at[place])

        for place in range(4):
            for quarter in range(4):

                @pl.when((base ^ place) == quarter)
                def _(place=place, quarter=quarter):
                    for copy in loads(quarter, place):
                        copy.start()

        stores = []
        biases = (query_ref, None, value_ref, None)
        for place, out_ref in enumerate((q_ref, k_ref, v_ref, None)):
            for copy in loads(0, place):
                copy.wait()
            stores.append(
                pltpu.make_async_copy(buf.at[place], all_ref.at[place], out_sems.at[place])
            )
            stores[-1].start()
            if out_ref is None:
                continue
            for t in range(rows // TILE):
                r = pl.ds(t * TILE, TILE)
                term = jnp.dot(x_ref[r, :], buf[place], preferred_element_type=jnp.float32)
                if biases[place] is not None:
                    term = term + biases[place][...]
                out_ref[r, :] = term.astype(jnp.bfloat16)
        for store in stores:
            store.wait()

    low = jax.ShapeDtypeStruct((rows, width), jnp.bfloat16)
    every = jax.ShapeDtypeStruct((4, width, width), jnp.bfloat16)
    spec = pl.BlockSpec((rows, width), lambda i, w: (0, 0), pipeline_mode=pl.Buffered(1))
    return pl.pallas_call(
        body,
        grid_spec=pltpu.PrefetchScalarGridSpec(
            num_scalar_prefetch=1,
            grid=(1,),
            in_specs=[spec, fixed(query_bias), fixed(value_bias)]
            + [pl.BlockSpec(memory_space=pl.ANY)] * 8,
            out_specs=[spec] * 3 + [pl.BlockSpec(memory_space=pl.ANY)],
            scratch_shapes=[
                pltpu.VMEM((4, width, width), jnp.bfloat16),
                pltpu.SemaphoreType.DMA((4, 8)),
                pltpu.SemaphoreType.DMA((4,)),
            ],
        ),
        out_shape=[low, low, low, every],
        compiler_params=pltpu.CompilerParams(vmem_limit_bytes=58 << 20),
        cost_estimate=pl.CostEstimate(
            flops=6 * rows * width * width, bytes_accessed=30 << 20, transcendentals=0
        ),
        name="project",
    )(where, inputs, query_bias, value_bias, *pieces)


def project_back(parts, matrices):
    rows = parts[0].shape[0]
    width = matrices.shape[1]
    cut = width - parts[1].shape[1]

    def body(*refs):
        ins, (w_ref, out_ref) = refs[:6], refs[6:]
        total = None
        for i in range(3):
            for ref, start, stop in ((ins[2 * i], 0, cut), (ins[2 * i + 1], cut, width)):
                term = times_t(ref[:, : stop - start], w_ref[i, :, start:stop])
                total = term if total is None else total + term
        out_ref[...] = total

    return pl.pallas_call(
        body,
        grid=(rows // TILE,),
        in_specs=[pl.BlockSpec((TILE, a.shape[1]), lambda i: (i, 0)) for a in parts]
        + [
            pl.BlockSpec(
                (3, width, width), lambda i: (0, 0, 0), pipeline_mode=pl.Buffered(1)
            )
        ],
        out_specs=pl.BlockSpec((TILE, width), lambda i: (i, 0)),
        out_shape=jax.ShapeDtypeStruct((rows, width), jnp.float32),
        compiler_params=pltpu.CompilerParams(vmem_limit_bytes=40 << 20),
        cost_estimate=pl.CostEstimate(
            flops=6 * rows * width * width, bytes_accessed=20 << 20, transcendentals=0
        ),
        name="project_back",
    )(*parts, matrices)


def bias_sums(mods, parts, d_branch, up_sums, d_feed):
    width = d_feed.shape[1]
    cut = width - parts[1].shape[1]

    def body(mods_ref, qa_ref, qb_ref, va_ref, vb_ref, branch_ref, up_ref, feed_ref, out_ref):
        @pl.when(pl.program_id(0) == 0)
        def _():
            out_ref[...] = jnp.zeros_like(out_ref)
            out_ref[0:6, :] = mods_ref[...].astype(jnp.float32)
            out_ref[9:13, :] = up_ref[...]

        for row, ref, start, stop in (
            (6, qa_ref, 0, cut),
            (6, qb_ref, cut, width),
            (7, va_ref, 0, cut),
            (7, vb_ref, cut, width),
            (8, branch_ref, 0, width),
            (13, feed_ref, 0, width),
        ):
            terms = ref[:, : stop - start].astype(jnp.float32)
            out_ref[row : row + 1, start:stop] += jnp.sum(terms, axis=0, keepdims=True)

    def tile(array):
        return pl.BlockSpec((256, array.shape[1]), lambda i: (i, 0))

    def held(array):
        return pl.BlockSpec(array.shape, lambda i: (0, 0))

    out = jax.ShapeDtypeStruct((14, width), jnp.float32)
    return pl.pallas_call(
        body,
        grid=(d_feed.shape[0] // 256,),
        in_specs=[held(mods)]
        + [tile(a) for a in parts]
        + [tile(d_branch), held(up_sums), tile(d_feed)],
        out_specs=held(out),
        out_shape=out,
        compiler_params=pltpu.CompilerParams(vmem_limit_bytes=16 << 20),
        cost_estimate=pl.CostEstimate(flops=8 << 20, bytes_accessed=10 << 20, transcendentals=0),
        name="bias_sums",
    )(mods, *parts, d_branch, up_sums, d_feed)


def local_pairs(
    latent_in,
    conditioning,
    ada_weight,
    qkv_weight,
    proj_weight,
    up_weight,
    down_weight,
    bias_pack,
    cotangent,
):
    width = latent_in.shape[2]
    half_rows = latent_in.shape[1]
    zi, xi, ci, yi = [lax.axis_index(name) for name in ALL]
    device = ((zi * 2 + xi) * 2 + ci) * 2 + yi
    where = jnp.stack([zi, xi, ci, yi]).astype(jnp.int32)
    rows = width // 32

    quarter = ci * 2 + yi

    def in_order(array):
        return jnp.stack(
            [lax.dynamic_index_in_dim(array, quarter ^ step, 0, False) for step in range(4)]
        )

    def exchange(array):
        return lax.all_to_all(array, ALL, 0, 0, tiled=True)

    def exchange_quarters(array):
        got = [lax.dynamic_index_in_dim(array, quarter, 0, False)]
        for step, axes in ((1, "y"), (2, "c"), (3, ("c", "y"))):
            entry = lax.dynamic_index_in_dim(array, quarter ^ step, 0, False)
            got.append(
                swap(entry, axes)
                if step < 3
                else lax.ppermute(entry, axes, [(i, i ^ 3) for i in range(4)])
            )
        return in_order(jnp.stack(got))

    def to_all(vector):
        return exchange(jnp.broadcast_to(vector, (32,) + vector.shape))

    def over_tokens(left, right):
        return lax.dot_general(
            left, right, (((0,), (0,)), ((), ())), preferred_element_type=jnp.float32
        )

    def times_transposed(left, right):
        return lax.dot_general(
            left, right, (((1,), (1,)), ((), ())), preferred_element_type=jnp.float32
        )

    qkv_rows = qkv_weight.reshape(rows, 3 * width)
    quarters = jnp.stack(
        [qkv_rows[:, i * width : (i + 1) * width] for i in range(3)]
        + [proj_weight.reshape(rows, width)]
    )
    up_quarters = up_weight.reshape(rows, 8, 4, 144).transpose(2, 0, 1, 3).reshape(4, rows, width)
    units = exchange_quarters(jnp.concatenate([quarters, up_quarters], axis=1))
    unit_a = units[:, :rows].reshape(4 * rows, width)
    unit_u = units[:, rows:].reshape(4 * rows, width)
    unit_d = down_weight.reshape(4 * rows, width)
    hops_a = line_hops(lambda step: unit_a)
    other_half = after(lax.dynamic_index_in_dim(latent_in, 1 - yi, 0, False), unit_a)
    half_received = swap(other_half, "y")
    line_a = jnp.stack([after(unit_a, half_received), *hops_a])
    plane_a = plane_gather(line_a)
    unit_u = after(unit_u, line_a)
    hops_u = line_hops(lambda step: unit_u)
    own_condition = lax.dynamic_index_in_dim(conditioning, yi, 0, False)
    small = to_all(after(jnp.concatenate([bias_pack, own_condition]), line_a))
    bias_share = bias_pack.shape[0]
    biases = small[:, :bias_share].reshape(-1).astype(jnp.float32)
    conditions = small[:, bias_share:].astype(jnp.float32)
    silu_all = jax.nn.silu(conditions).astype(jnp.bfloat16)
    silu_cut = lax.dynamic_slice(silu_all, (0, device * rows), (32, rows))
    ada_rows = ada_weight.reshape(rows, 6 * width)
    shares = jnp.dot(silu_cut, ada_rows, preferred_element_type=jnp.float32)
    first_shares, later_shares = shares[:, : 2 * width], shares[:, 2 * width :]
    line_a, plane_a, hops_u, first_shares = lax.optimization_barrier(
        (line_a, plane_a, hops_u, first_shares)
    )
    corner_a = corner_gather(*plane_a)
    core_a = [swap(p, "c") for p in (line_a, *plane_a)]
    first_shares = after(first_shares, *core_a)
    modulations = jnp.sum(exchange(first_shares), axis=0, keepdims=True)
    modulations = modulations + biases[: 2 * width]
    shift_attention, scale_attention = jnp.split(modulations, 2, axis=1)
    own_half = lax.dynamic_index_in_dim(latent_in, yi, 0, False)
    tokens_low = jnp.concatenate([own_half, half_received])
    tokens = tokens_low.astype(jnp.float32)
    normed = norm_modulate(tokens, shift_attention, scale_attention).astype(jnp.bfloat16)
    line_u = jnp.stack([unit_u, *hops_u])
    unit_d = after(unit_d, line_u, *core_a)
    hops_d = line_hops(lambda step: unit_d)
    corner_a = after(corner_a, unit_d, modulations)
    core_a.append(swap(corner_a, "c"))
    line_u = after(line_u, core_a[3])
    plane_u = plane_gather(line_u)
    query_bias = biases[None, 6 * width : 7 * width]
    value_bias = biases[None, 7 * width : 8 * width]
    proj_bias = biases[8 * width : 9 * width]
    up_bias = biases[9 * width : 9 * width + FF].reshape(8, 4, 144).transpose(1, 0, 2)
    up_bias = in_order(up_bias.reshape(4, width)).reshape(1, FF)
    down_bias = biases[None, 9 * width + FF :]
    queries, keys, values, matrices = project(
        where,
        normed,
        query_bias,
        value_bias,
        after([line_a, *plane_a, corner_a, *core_a], line_u, unit_d),
    )
    proj_matrix = matrices[3]
    line_d = jnp.stack([after(unit_d, values), *hops_d])
    plane_u = after(plane_u, line_d)
    corner_u = corner_gather(*plane_u)
    core_u = [swap(p, "c") for p in (after(line_u, line_d), *plane_u)]
    part_one = attn_fwd(after(queries, *plane_u, line_d), keys, values, (0, 8))
    line_d, corner_u, core_u = after((line_d, corner_u, core_u), *part_one)
    core_u.append(swap(corner_u, "c"))
    plane_d = plane_gather(line_d)
    attended, log_total = attn_fwd(
        after(queries, line_d, *core_u[:3]), keys, values, (8, 8), tuple(part_one)
    )
    later_modulations = jnp.sum(after(exchange(after(later_shares, line_u)), *part_one), axis=0, keepdims=True)
    later_modulations = later_modulations + biases[2 * width : 6 * width]
    gate_attention, shift_feed, scale_feed, gate_feed = jnp.split(later_modulations, 4, axis=1)
    branch = (
        jnp.dot(attended, proj_matrix, preferred_element_type=jnp.float32)
        + proj_bias
    )
    middle = tokens + gate_attention * branch
    normed_feed = norm_modulate(middle, shift_feed, scale_feed).astype(jnp.bfloat16)
    pieces_u = after([line_u, *plane_u, corner_u, *core_u], normed_feed)
    plane_d = after(plane_d, normed_feed)
    corner_d = corner_gather(*plane_d)
    core_d = [swap(p, "c") for p in (after(line_d, normed_feed), *plane_d)]
    other_cotangent = after(lax.dynamic_index_in_dim(cotangent, 1 - yi, 0, False), *plane_d)
    cotangent_received = swap(other_cotangent, "y")
    activated, slope = feed_up(
        where,
        after(normed_feed, *core_d[:3], other_cotangent),
        up_bias,
        pieces_u,
    )
    activated, corner_d = lax.optimization_barrier((activated, corner_d))
    core_d.append(swap(corner_d, "c"))
    pieces_d = after([line_d, *plane_d, corner_d, *core_d], activated)
    feed_out, output_low = feed_down(where, activated, middle, gate_feed, down_bias, pieces_d)
    cotangent_received, output_low = lax.optimization_barrier((cotangent_received, output_low))
    own_cotangent = lax.dynamic_index_in_dim(cotangent, yi, 0, False)
    upstream = jnp.concatenate([own_cotangent, cotangent_received]).astype(jnp.float32)
    d_feed = (gate_feed * upstream).astype(jnp.bfloat16)
    ours, others = slice(None, 2 * width), slice(2 * width, None)
    down_sent = over_tokens(activated[:, others], d_feed).astype(jnp.bfloat16)
    down_received = swap(down_sent, "c")
    output_received = swap(after(output_low, down_sent)[half_rows:], "y")
    d_gate_feed = jnp.sum(upstream * feed_out, axis=0, keepdims=True)
    down_half = over_tokens(after(activated, down_sent)[:, ours], d_feed)
    down = ScatterSum(rows_of, add_low(down_half, down_received), (0, 1))
    down.corner()
    d_before, d_normed_feed, before_sums = feed_back(
        where, after(d_feed, *down.sent), slope, pieces_d, pieces_u
    )
    output_received, d_before = lax.optimization_barrier((output_received, d_before))
    down.plane(d_normed_feed)
    up_sent = over_tokens(after(normed_feed, *down.sent), d_before[:, others])
    up_sent = up_sent.astype(jnp.bfloat16)
    up_received = swap(up_sent, "c")
    unused_norm, norm_pull = jax.vjp(norm_modulate, middle, shift_feed, scale_feed)
    d_middle_part, d_shift_feed, d_scale_feed = norm_pull(
        after(d_normed_feed, up_sent)
    )
    d_middle = upstream + d_middle_part
    d_gate_attention = jnp.sum(d_middle * branch, axis=0, keepdims=True)
    d_branch = (gate_attention * d_middle).astype(jnp.bfloat16)
    d_attended = times_transposed(d_branch, proj_matrix).astype(jnp.bfloat16)
    mods_early = jnp.concatenate([d_gate_attention, d_shift_feed, d_scale_feed, d_gate_feed], 1)
    mods_early = mods_early.astype(jnp.bfloat16)
    up_half = over_tokens(after(normed_feed, d_attended), d_before[:, ours])
    up = ScatterSum(columns_of, add_low(up_half, up_received), (0, 1))
    down.line(up.half)
    up.corner()
    log_rows = log_total[:, :H].T
    part_a = attn_bwd(
        queries,
        keys,
        values,
        after(d_attended, *up.sent, *down.sent, mods_early),
        log_rows,
        (0, 8),
    )

    def attention_terms(gradients, d_b, core, received, *earlier):
        d_q, d_k, d_v = gradients
        left = after(normed, *earlier)
        first = over_tokens(left, jnp.where(core == 0, d_q, d_v))
        second = over_tokens(
            jnp.where(core == 0, left, attended), jnp.where(core == 0, d_k, d_b)
        )
        if received is not None:
            first, second = first + received[:width], second + received[width:]
        return jnp.concatenate([first.astype(jnp.bfloat16), second.astype(jnp.bfloat16)])

    left_terms = [a[:, :512] for a in part_a], d_branch[:, :512]
    left_sent = attention_terms(*left_terms, 1 - ci, None, *part_a, *down.got, *up.got)
    left_received = swap(left_sent, "c")
    up.plane(left_sent)
    left_half = attention_terms(*left_terms, ci, left_received, left_sent, *up.sent)
    left = ScatterSum(rows_of, left_half, (yi, 1 - yi))
    left.corner()
    down_sum = down.total(left_half)
    part_b = attn_bwd(
        queries,
        keys,
        values,
        after(d_attended, *left.sent, down_sum),
        log_rows,
        (8, 4),
        part_a,
    )
    part_b = after(tuple(part_b), *left.got, *up.got)
    left.plane(*part_b)
    up.line(*part_b)
    part_c = attn_bwd(
        queries,
        keys,
        values,
        after(d_attended, *left.sent, *up.sent),
        log_rows,
        (12, 4),
        part_b,
    )
    part_c = after(tuple(part_c), *left.got, *up.got)
    right_parts = [
        jnp.concatenate([b[:, :256], c], axis=1) for b, c in zip(part_b, part_c)
    ]
    right_terms = right_parts, d_branch[:, 512:]
    left.line(*part_c)
    right_sent = attention_terms(*right_terms, 1 - ci, None, *left.sent)
    right_received = swap(right_sent, "c")
    right_half = attention_terms(*right_terms, ci, right_received, right_sent)
    right = ScatterSum(rows_of, right_half, (yi, 1 - yi))
    right.corner()
    parts = [array for pair in zip(part_a, right_parts) for array in pair]
    d_normed = project_back(after(parts, *right.sent, *left.got), matrices)
    right.plane(d_normed)
    up_sum = exchange_quarters(up.total(*right.sent).reshape(4, rows, width))
    unused_first, first_pull = jax.vjp(norm_modulate, tokens, shift_attention, scale_attention)
    d_tokens_part, d_shift_attention, d_scale_attention = first_pull(after(d_normed, *right.sent))
    grad_low = (d_middle + d_tokens_part).astype(jnp.bfloat16)
    grad_low, up_sum = lax.optimization_barrier((grad_low, up_sum))
    mods = jnp.concatenate([d_shift_attention, d_scale_attention], axis=1).astype(jnp.bfloat16)
    mods = jnp.concatenate([mods, mods_early], axis=1)
    every_mods = to_all(mods.reshape(2, 3 * width)).reshape(32, 6 * width)
    right.line(grad_low, mods)
    quarter_rows = half_rows // 2
    grad_first = swap(grad_low[half_rows : half_rows + quarter_rows], "y")

    def both_halves(own_rows, *received):
        both = jnp.stack([own_rows, own_rows])
        row = 0
        for piece in received:
            both = lax.dynamic_update_slice(both, piece[None], (1 - yi, row, 0))
            row += piece.shape[0]
        return both

    left_totals = left.total(*right.sent)
    down_sum, output_low, output_received, up_sum = after(
        (down_sum, output_low, output_received, up_sum), *right.sent
    )
    output = both_halves(output_low[:half_rows], output_received)
    grad_down = down_sum.reshape(-1)
    grad_up = up_sum.reshape(4, rows, 8, 144).transpose(1, 2, 0, 3).reshape(-1)
    up_sums = in_order(before_sums.reshape(4, width)).reshape(4, 8, 144).transpose(1, 0, 2)
    bias_terms = bias_sums(
        mods.reshape(6, width),
        after((part_a[0], right_parts[0], part_a[2], right_parts[2]), *right.sent),
        d_branch,
        up_sums.reshape(4, width),
        d_feed,
    ).reshape(32, -1)
    right_totals = right.total(left_totals, output, grad_down, grad_up, bias_terms)
    sums = jnp.concatenate([left_totals, right_totals], axis=1).reshape(4, rows, width)
    sums = exchange_quarters(sums)
    every_mods, grad_first = lax.optimization_barrier((every_mods, grad_first))
    grad_last = swap(after(grad_low, grad_first)[half_rows + quarter_rows :], "y")
    d_silu_rows = times_transposed(every_mods, ada_rows)
    d_silu_parts = jnp.repeat(d_silu_rows.reshape(16, 1, 2, rows), 2, axis=1)
    parts = exchange(
        jnp.concatenate([d_silu_parts.reshape(32, 2 * rows), bias_terms], axis=1)
    )
    grad_ada = over_tokens(silu_cut, every_mods).reshape(-1)
    parts, grad_last = lax.optimization_barrier((parts, grad_last))
    d_silu = parts[:, : 2 * rows].reshape(32, 2, rows).transpose(1, 0, 2).reshape(2, width)
    grad_bias = jnp.sum(parts[:, 2 * rows :], axis=0)
    unused_silu, silu_pull = jax.vjp(jax.nn.silu, conditioning.astype(jnp.float32))
    grad_cond = silu_pull(d_silu)[0].astype(jnp.bfloat16)
    grad_input = both_halves(grad_low[:half_rows], grad_first, grad_last)
    grad_qkv = jnp.concatenate([sums[0], sums[1], sums[2]], axis=1).reshape(-1)
    grad_proj = sums[3].reshape(-1)
    return (
        output,
        grad_input,
        grad_cond,
        grad_ada,
        grad_qkv,
        grad_proj,
        grad_up,
        grad_down,
        grad_bias,
    )


def local_any(
    latent_in,
    conditioning,
    ada_weight,
    qkv_weight,
    proj_weight,
    up_weight,
    down_weight,
    bias_pack,
    cotangent,
):
    model_width = latent_in.shape[2]
    every_param = (
        lax.all_gather(ada_weight, ("batch", "seq"), axis=0, tiled=True),
        lax.all_gather(qkv_weight, ("batch", "seq"), axis=0, tiled=True),
        lax.all_gather(proj_weight, ("batch", "seq"), axis=0, tiled=True),
        lax.all_gather(up_weight, ("batch", "seq"), axis=0, tiled=True),
        lax.all_gather(down_weight, ("batch", "seq"), axis=0, tiled=True),
        lax.all_gather(bias_pack, ("batch", "seq"), axis=0, tiled=True),
    )
    ada_matrix, qkv_matrix, proj_matrix, up_matrix, down_matrix, biases = shape_all(
        every_param, model_width
    )
    ada_bias = biases[: 6 * model_width]
    query_bias = biases[6 * model_width : 7 * model_width]
    value_bias = biases[7 * model_width : 8 * model_width]
    proj_bias = biases[8 * model_width : 9 * model_width]
    up_bias = biases[9 * model_width : 9 * model_width + FF]
    down_bias = biases[9 * model_width + FF :]
    tokens = latent_in.astype(jnp.float32)
    conditions = conditioning.astype(jnp.float32)
    silu_cond = jax.nn.silu(conditions).astype(jnp.bfloat16)
    modulations = jnp.dot(silu_cond, ada_matrix, preferred_element_type=jnp.float32) + ada_bias
    shift_attention, scale_attention, gate_attention, shift_feed, scale_feed, gate_feed = jnp.split(
        modulations[:, None, :], 6, axis=2
    )
    normed = norm_modulate(tokens, shift_attention, scale_attention).astype(jnp.bfloat16)
    projected = jnp.einsum("btd,df->btf", normed, qkv_matrix, preferred_element_type=jnp.float32)
    queries = (projected[..., :model_width] + query_bias).astype(jnp.bfloat16)
    own_keys = jnp.concatenate(
        [
            projected[..., model_width : 2 * model_width],
            projected[..., 2 * model_width :] + value_bias,
        ],
        axis=2,
    ).astype(jnp.bfloat16)
    every_keys = lax.all_gather(own_keys, "seq", axis=1, tiled=True)
    attended, log_total = lax.map(attend_latent, (queries, every_keys))
    attended = attended.astype(jnp.bfloat16)
    branch = (
        jnp.einsum("btd,de->bte", attended, proj_matrix, preferred_element_type=jnp.float32)
        + proj_bias
    )
    middle = tokens + gate_attention * branch
    normed_feed = norm_modulate(middle, shift_feed, scale_feed).astype(jnp.bfloat16)
    before = (
        jnp.einsum("btd,df->btf", normed_feed, up_matrix, preferred_element_type=jnp.float32)
        + up_bias
    )
    activated = gelu_tanh(before).astype(jnp.bfloat16)
    feed_out = (
        jnp.einsum("btf,fd->btd", activated, down_matrix, preferred_element_type=jnp.float32)
        + down_bias
    )
    output = (middle + gate_feed * feed_out).astype(jnp.bfloat16)
    param_again = (
        lax.all_gather(ada_weight, ("batch", "seq"), axis=0, tiled=True),
        lax.all_gather(qkv_weight, ("batch", "seq"), axis=0, tiled=True),
        lax.all_gather(proj_weight, ("batch", "seq"), axis=0, tiled=True),
        lax.all_gather(up_weight, ("batch", "seq"), axis=0, tiled=True),
        lax.all_gather(down_weight, ("batch", "seq"), axis=0, tiled=True),
        lax.all_gather(bias_pack, ("batch", "seq"), axis=0, tiled=True),
    )
    ada_matrix, qkv_matrix, proj_matrix, up_matrix, down_matrix, biases = shape_all(
        param_again, model_width
    )
    upstream = cotangent.astype(jnp.float32)
    d_gate_feed = jnp.sum(upstream * feed_out, axis=1, keepdims=True)
    d_feed = (gate_feed * upstream).astype(jnp.bfloat16)
    d_activated = jnp.einsum("btd,fd->btf", d_feed, down_matrix, preferred_element_type=jnp.float32)
    unused_gelu, gelu_pull = jax.vjp(gelu_tanh, before)
    d_before = gelu_pull(d_activated)[0].astype(jnp.bfloat16)
    d_normed_feed = jnp.einsum(
        "btf,df->btd", d_before, up_matrix, preferred_element_type=jnp.float32
    )
    unused_norm, norm_pull = jax.vjp(norm_modulate, middle, shift_feed, scale_feed)
    d_middle_part, d_shift_feed, d_scale_feed = norm_pull(d_normed_feed)
    d_middle = upstream + d_middle_part
    d_gate_attention = jnp.sum(d_middle * branch, axis=1, keepdims=True)
    d_branch = (gate_attention * d_middle).astype(jnp.bfloat16)
    d_attended = jnp.einsum(
        "bte,de->btd", d_branch, proj_matrix, preferred_element_type=jnp.float32
    ).astype(jnp.bfloat16)
    d_queries, d_every = lax.map(attend_back, (queries, every_keys, log_total, d_attended))
    d_queries = d_queries.astype(jnp.bfloat16)
    d_own = lax.psum_scatter(d_every.astype(jnp.bfloat16), "seq", scatter_dimension=1, tiled=True)
    d_projected = jnp.concatenate([d_queries, d_own], axis=2)
    d_normed = jnp.einsum(
        "btf,df->btd", d_projected, qkv_matrix, preferred_element_type=jnp.float32
    )
    unused_first, first_pull = jax.vjp(norm_modulate, tokens, shift_attention, scale_attention)
    d_tokens_part, d_shift_attention, d_scale_attention = first_pull(d_normed)
    grad_input = (d_middle + d_tokens_part).astype(jnp.bfloat16)
    local_mods = jnp.concatenate(
        [
            d_shift_attention,
            d_scale_attention,
            d_gate_attention,
            d_shift_feed,
            d_scale_feed,
            d_gate_feed,
        ],
        axis=2,
    )[:, 0, :]
    d_mods = lax.psum(local_mods.astype(jnp.bfloat16), "seq")
    d_silu = jnp.einsum("bf,df->bd", d_mods, ada_matrix, preferred_element_type=jnp.float32)
    unused_silu, silu_pull = jax.vjp(jax.nn.silu, conditions)
    grad_cond = silu_pull(d_silu)[0].astype(jnp.bfloat16)
    is_owner = lax.axis_index("seq") == 0
    owned_mods = jnp.where(is_owner, d_mods, jnp.zeros_like(d_mods))
    bias_terms = jnp.concatenate(
        [
            jnp.sum(owned_mods, axis=0, dtype=jnp.float32),
            jnp.sum(d_queries, axis=(0, 1), dtype=jnp.float32),
            jnp.sum(d_own[..., model_width:], axis=(0, 1), dtype=jnp.float32),
            jnp.sum(d_branch, axis=(0, 1), dtype=jnp.float32),
            jnp.sum(d_before, axis=(0, 1), dtype=jnp.float32),
            jnp.sum(d_feed, axis=(0, 1), dtype=jnp.float32),
        ]
    )
    matrix_terms = [
        (silu_cond, owned_mods, ada_weight.shape[0]),
        (
            normed.reshape(-1, model_width),
            d_projected.reshape(-1, 3 * model_width),
            qkv_weight.shape[0],
        ),
        (
            attended.reshape(-1, model_width),
            d_branch.reshape(-1, model_width),
            proj_weight.shape[0],
        ),
        (normed_feed.reshape(-1, model_width), d_before.reshape(-1, FF), up_weight.shape[0]),
        (activated.reshape(-1, FF), d_feed.reshape(-1, model_width), down_weight.shape[0]),
    ]
    bias_share = bias_pack.shape[0]
    shard_rows = sum((entry[2] for entry in matrix_terms)) + bias_share
    block_count = shard_rows * lax.axis_size(("batch", "seq")) // shard_rows
    pieces = []
    for left, right, grad_shard_size in matrix_terms:
        pieces.append(flat_term(left, right).reshape(block_count, grad_shard_size))
    pieces.append(bias_terms.reshape(block_count, bias_share))
    owned_grads = lax.psum_scatter(
        jnp.concatenate(pieces, axis=1).reshape(-1),
        ("batch", "seq"),
        scatter_dimension=0,
        tiled=True,
    )
    results = []
    cursor = 0
    for shard_size in [entry[2] for entry in matrix_terms] + [bias_share]:
        results.append(owned_grads[cursor : cursor + shard_size])
        cursor = cursor + shard_size
    grad_ada, grad_qkv, grad_proj, grad_up, grad_down, grad_bias = results
    return (
        output,
        grad_input,
        grad_cond,
        grad_ada,
        grad_qkv,
        grad_proj,
        grad_up,
        grad_down,
        grad_bias,
    )


def solution(mesh):
    batch, seq = mesh.shape["batch"], mesh.shape["seq"]
    if (batch, seq) == (16, 2):
        inner = Mesh(mesh.devices.reshape(4, 2, 2, 2), ALL)
        body, tokens = local_pairs, ("z", "x", "c")
        flat, split = P(ALL), "y"
    else:
        inner, body, tokens, split = mesh, local_any, "batch", "seq"
        flat = P(("batch", "seq"))
    activations = P(tokens, split, None)
    vectors = P(tokens, None)
    in_specs = (activations, vectors) + (flat,) * 6 + (activations,)
    out_specs = (activations, activations, vectors) + (flat,) * 6
    return jax.shard_map(body, mesh=inner, in_specs=in_specs, out_specs=out_specs, check_vma=False)
```

```python
import functools
import itertools

import jax
import jax.numpy as jnp
from jax import lax
from jax.experimental import pallas as pl
from jax.experimental.pallas import tpu as pltpu
from jax.sharding import Mesh
from jax.sharding import PartitionSpec as P

H = 16
HD = 72
FF = 4608


EPS = 1e-06
GELU_COEF = 0.7978845608028654
SCALE = HD ** (-0.5)
LOG2E = 1.4426950408889634
WIN = 256
ALL = ("z", "x", "c", "y")
SWAP = [(0, 1), (1, 0)]


def norm_modulate(inputs, shift_term, scale_term):
    center = inputs - jnp.mean(inputs, axis=-1, keepdims=True)
    spread = jnp.mean(center * center, axis=-1, keepdims=True)
    return center * lax.rsqrt(spread + EPS) * (1.0 + scale_term) + shift_term


def gelu_tanh(values):
    return (
        0.5 * values * (1.0 + jnp.tanh(GELU_COEF * (values + 0.044715 * values * values * values)))
    )


def flat_term(left, right):
    product = jnp.einsum("nd,nf->df", left, right, preferred_element_type=jnp.float32).reshape(-1)
    return product


def split_heads(queries, keys_values):
    query_rows = queries.shape[0]
    key_rows = keys_values.shape[0]
    model_width = queries.shape[1]
    query_heads = queries.reshape(query_rows, H, HD)
    key_heads = keys_values[:, :model_width].reshape(key_rows, H, HD)
    value_heads = keys_values[:, model_width:].reshape(key_rows, H, HD)
    scores = jnp.einsum(
        "qhe,khe->hqk", query_heads, key_heads, preferred_element_type=jnp.float32
    ) * HD ** (-0.5)
    return (query_heads, key_heads, value_heads, scores)


def attend_latent(block_items):
    queries, keys_values = block_items
    query_heads, key_heads, value_heads, scores = split_heads(queries, keys_values)
    top_score = jnp.max(scores, axis=-1, keepdims=True)
    exp_scores = jnp.exp(scores - top_score)
    exp_total = jnp.sum(exp_scores, axis=-1, keepdims=True)
    probs_low = (exp_scores / exp_total).astype(jnp.bfloat16)
    attended = jnp.einsum(
        "hqk,khe->qhe", probs_low, value_heads, preferred_element_type=jnp.float32
    )
    return (
        attended.reshape(queries.shape[0], queries.shape[1]),
        (top_score + jnp.log(exp_total))[..., 0],
    )


def attend_back(block_items):
    queries, keys_values, log_total, d_attended = block_items
    query_rows = queries.shape[0]
    key_rows = keys_values.shape[0]
    model_width = queries.shape[1]
    query_heads, key_heads, value_heads, scores = split_heads(queries, keys_values)
    attention_probs = jnp.exp(scores - log_total[..., None])
    d_heads = d_attended.reshape(query_rows, H, HD)
    d_probs = jnp.einsum("qhe,khe->hqk", d_heads, value_heads, preferred_element_type=jnp.float32)
    centered = d_probs - jnp.sum(attention_probs * d_probs, axis=-1, keepdims=True)
    d_scores = (HD ** (-0.5) * (attention_probs * centered)).astype(jnp.bfloat16)
    d_queries = jnp.einsum("hqk,khe->qhe", d_scores, key_heads, preferred_element_type=jnp.float32)
    d_keys = jnp.einsum("hqk,qhe->khe", d_scores, query_heads, preferred_element_type=jnp.float32)
    d_values = jnp.einsum(
        "hqk,qhe->khe",
        attention_probs.astype(jnp.bfloat16),
        d_heads,
        preferred_element_type=jnp.float32,
    )
    joined = jnp.concatenate(
        [d_keys.reshape(key_rows, model_width), d_values.reshape(key_rows, model_width)], axis=1
    )
    return (d_queries.reshape(query_rows, model_width), joined)


def shape_all(gathered, model_width):
    ada_full, qkv_full, proj_full, up_full, down_full, bias_full = gathered
    return (
        ada_full.reshape(model_width, 6 * model_width),
        qkv_full.reshape(model_width, 3 * model_width),
        proj_full.reshape(model_width, model_width),
        up_full.reshape(model_width, FF),
        down_full.reshape(FF, model_width),
        bias_full.astype(jnp.float32),
    )


def head_window(head, width):
    start = jnp.minimum((head * HD) // 128, width // 128 - 2) * 128
    return pl.multiple_of(start, 128), head * HD - start


def attn_fwd_kernel(q_ref, k_ref, v_ref, *refs, tile, first):
    o_ref, lse_ref = refs[-2:]
    head = pl.program_id(0) + first
    rows, width = q_ref.shape

    if len(refs) > 2:

        @pl.when(pl.program_id(0) == 0)
        def _():
            o_ref[...] = refs[0][...]
            lse_ref[...] = refs[1][...]

    lo, off = head_window(head, width)
    lane = lax.broadcasted_iota(jnp.int32, (1, WIN), 1)
    inside = (lane >= off) & (lane < off + HD)
    keep = inside.astype(jnp.bfloat16)
    kw = k_ref[:, pl.ds(lo, WIN)]
    vw = v_ref[:, pl.ds(lo, WIN)]
    col = lax.broadcasted_iota(jnp.int32, (1, 128), 1) == head
    for t in range(rows // tile):
        r = pl.ds(t * tile, tile)
        qm = q_ref[r, pl.ds(lo, WIN)] * keep
        s = lax.dot_general(qm, kw, (((1,), (1,)), ((), ())), preferred_element_type=jnp.float32)
        top = jnp.max(s, axis=-1, keepdims=True)
        p = jnp.exp2((s - top) * (SCALE * LOG2E))
        total = jnp.sum(p, axis=-1, keepdims=True)
        o = jnp.dot(p.astype(jnp.bfloat16), vw, preferred_element_type=jnp.float32)
        o = o * (1.0 / total)
        old = o_ref[r, pl.ds(lo, WIN)].astype(jnp.float32)
        o_ref[r, pl.ds(lo, WIN)] = jnp.where(inside, o, old).astype(jnp.bfloat16)
        lse_ref[r, :] = jnp.where(col, top * SCALE + jnp.log(total), lse_ref[r, :])


def whole(array_or_shape):
    shape = array_or_shape.shape
    return pl.BlockSpec(shape, lambda h: (0,) * len(shape), pipeline_mode=pl.Buffered(1))


def attn_fwd(q, k, v, heads, into=(), tile=256):
    rows, width = q.shape
    keys = k.shape[0]
    first, count = heads
    outs = [
        jax.ShapeDtypeStruct(q.shape, jnp.bfloat16),
        jax.ShapeDtypeStruct((rows, 128), jnp.float32),
    ]
    ins = (q, k, v, *into)
    return pl.pallas_call(
        functools.partial(attn_fwd_kernel, tile=tile, first=first),
        grid=(count,),
        in_specs=[whole(a) for a in ins],
        out_specs=[whole(a) for a in outs],
        out_shape=outs,
        compiler_params=pltpu.CompilerParams(vmem_limit_bytes=60 << 20),
        cost_estimate=pl.CostEstimate(
            flops=4 * count * rows * keys * WIN,
            bytes_accessed=8 * rows * width,
            transcendentals=count * rows * keys,
        ),
        name="attention_forward",
    )(*ins)


def attn_bwd_kernel(q_ref, k_ref, v_ref, g_ref, lse_ref, *refs, tile, first, origin):
    dq_ref, dk_ref, dv_ref = refs[-3:]
    head = pl.program_id(0) + first
    rows, width = q_ref.shape
    keys = k_ref.shape[0]

    if len(refs) > 3:

        @pl.when(pl.program_id(0) == 0)
        def _():
            dq_ref[:, :128] = refs[0][...]
            dk_ref[:, :128] = refs[1][...]
            dv_ref[:, :128] = refs[2][...]

    lo, off = head_window(head, origin + dq_ref.shape[1])
    there = pl.ds(pl.multiple_of(lo - origin, 128), WIN)
    lane = lax.broadcasted_iota(jnp.int32, (1, WIN), 1)
    inside = (lane >= off) & (lane < off + HD)
    keep = inside.astype(jnp.bfloat16)
    kw = k_ref[:, pl.ds(lo, WIN)]
    vw = v_ref[:, pl.ds(lo, WIN)]
    ktw = kw.T
    dk = jnp.zeros((keys, WIN), jnp.float32)
    dv = jnp.zeros((keys, WIN), jnp.float32)
    for t in range(rows // tile):
        r = pl.ds(t * tile, tile)
        lse = lse_ref[pl.ds(head, 1), r]
        qw = q_ref[r, pl.ds(lo, WIN)]
        gw = g_ref[r, pl.ds(lo, WIN)]
        st = jnp.dot(kw, (qw * keep).T, preferred_element_type=jnp.float32)
        pt = jnp.exp2(st * (SCALE * LOG2E) - lse * LOG2E)
        dpt = jnp.dot(vw, (gw * keep).T, preferred_element_type=jnp.float32)
        delta = jnp.sum(pt * dpt, axis=0, keepdims=True)
        dst = (pt * (dpt - delta) * SCALE).astype(jnp.bfloat16)
        dv = dv + jnp.dot(pt.astype(jnp.bfloat16), gw, preferred_element_type=jnp.float32)
        dk = dk + jnp.dot(dst, qw, preferred_element_type=jnp.float32)
        dq = jnp.dot(ktw, dst, preferred_element_type=jnp.float32).T
        old = dq_ref[r, there].astype(jnp.float32)
        dq_ref[r, there] = jnp.where(inside, dq, old).astype(jnp.bfloat16)
    old = dk_ref[:, there].astype(jnp.float32)
    dk_ref[:, there] = jnp.where(inside, dk, old).astype(jnp.bfloat16)
    old = dv_ref[:, there].astype(jnp.float32)
    dv_ref[:, there] = jnp.where(inside, dv, old).astype(jnp.bfloat16)


def head_columns(heads):
    first, count = heads
    return (first * HD) // 128 * 128, -(-((first + count) * HD) // 128) * 128


def attn_bwd(q, k, v, g, lse_rows, heads, before=(), tile=512):
    rows, width = q.shape
    keys = k.shape[0]
    first, count = heads
    start, stop = head_columns(heads)
    outs = [jax.ShapeDtypeStruct((a.shape[0], stop - start), jnp.bfloat16) for a in (q, k, v)]
    ins = (q, k, v, g, lse_rows, *before)
    specs = [whole(a) for a in ins[:5]]
    for array in before:
        last = array.shape[1] // 128 - 1
        specs.append(pl.BlockSpec((array.shape[0], 128), lambda h, last=last: (0, last)))
    return pl.pallas_call(
        functools.partial(attn_bwd_kernel, tile=tile, first=first, origin=start),
        grid=(count,),
        in_specs=specs,
        out_specs=[whole(a) for a in outs],
        out_shape=outs,
        compiler_params=pltpu.CompilerParams(vmem_limit_bytes=60 << 20),
        cost_estimate=pl.CostEstimate(
            flops=10 * count * rows * keys * WIN,
            bytes_accessed=14 * rows * width,
            transcendentals=count * rows * keys,
        ),
        name="attention_backward",
    )(*ins)


def after(array, *earlier):
    if not earlier:
        return array
    return lax.optimization_barrier((array, earlier))[0]


def swap(array, axis):
    return lax.ppermute(array, axis, SWAP)


def line_hops(block_of):
    return [
        lax.ppermute(block_of(step), "z", [(i, i ^ step) for i in range(4)]) for step in range(1, 4)
    ]


def plane_gather(line):
    return swap(line, "x"), swap(line, "y")


def corner_swap(array, first):
    pairs = []
    for x, c, y in itertools.product(range(2), repeat=3):
        along_x = c == first
        target = (1 - x, c, y) if along_x else (x, c, 1 - y)
        pairs.append((x * 4 + c * 2 + y, target[0] * 4 + target[1] * 2 + target[2]))
    return lax.ppermute(array, ("x", "c", "y"), pairs)


def corner_gather(from_x, from_y):
    return corner_swap(jnp.where(lax.axis_index("c") == 0, from_x, from_y), 1)


def add_low(*terms):
    total = terms[0].astype(jnp.float32)
    for term in terms[1:]:
        total = total + term.astype(jnp.float32)
    return total.astype(jnp.bfloat16)


def rows_of(half, yy, xx):
    width = half.shape[1]
    cut = lax.dynamic_slice(
        half.reshape(2, 4, 2, 144, width), (yy, 0, xx, 0, 0), (1, 4, 1, 144, width)
    )
    return cut.reshape(4, 144, width)


def columns_of(half, yy, xx):
    width = half.shape[1] // 2
    cut = lax.dynamic_slice(
        half.reshape(4, 2, 144, 2 * width), (0, xx, 0, yy * width), (4, 1, 144, width)
    )
    return cut.reshape(4, 144, width)


class ScatterSum:
    def __init__(self, part, half, quarters):
        self.part, self.half = part, half
        self.mine, self.theirs = quarters
        self.zi, self.xi = lax.axis_index("z"), lax.axis_index("x")

    def corner(self):
        self.sent = (self.part(self.half, self.theirs, 1 - self.xi),)
        self.got = (corner_swap(self.sent[0], 0),)

    def plane(self, *earlier):
        half, got = after(self.half, *earlier), self.got[0]
        to_y, to_x = self.part(half, self.theirs, self.xi), self.part(half, self.mine, 1 - self.xi)
        even = lax.axis_index("c") == 0
        to_y = jnp.where(even, add_low(to_y, got), to_y)
        to_x = jnp.where(even, to_x, add_low(to_x, got))
        self.sent = to_y, to_x
        self.got = swap(to_y, "y"), swap(to_x, "x")

    def line(self, *earlier):
        half = after(self.half, *earlier)
        own = add_low(self.part(half, self.mine, self.xi), *self.got)
        blocks = [lax.dynamic_index_in_dim(own, self.zi ^ step, 0, False) for step in range(4)]
        self.own, self.sent = blocks[0], blocks[1:]
        self.got = line_hops(lambda step: blocks[step])

    def total(self, *earlier):
        total = after(self.own, *earlier).astype(jnp.float32)
        for hop in self.got:
            total = total + hop.astype(jnp.float32)
        return total


def load_quarter(where_ref, pieces, quarter, buf, sems):
    copies = []
    for x_bit in range(2):
        piece = pieces[quarter * 2 + x_bit]
        xi = where_ref[1] if x_bit == 0 else 1 - where_ref[1]
        height = piece.shape[1]
        for block in range(4):
            row = pl.multiple_of(((where_ref[0] ^ block) * 2 + xi) * height, 16)
            copies.append(
                pltpu.make_async_copy(
                    piece.at[block], buf.at[pl.ds(row, height), :], sems.at[len(copies)]
                )
            )
    return copies


class Quarters:
    def __init__(self, where_ref, pieces, buf, sems):
        self.buf, self.first = buf, pl.program_id(0) == 0
        self.loads = [
            load_quarter(where_ref, pieces, i, buf.at[i], sems.at[i]) for i in range(4)
        ]

    def start(self, i):
        @pl.when(self.first)
        def _():
            for copy in self.loads[i]:
                copy.start()

    def wait(self, i):
        @pl.when(self.first)
        def _():
            for copy in self.loads[i]:
                copy.wait()

        return self.buf.at[i]


def stream_quarters(where_ref, pieces, buf, sems):
    step = pl.program_id(0)
    for i in range(4):

        @pl.when(step == i)
        def _(i=i):
            quarter = load_quarter(where_ref, pieces, i, buf.at[i % 2], sems.at[i % 2])
            if i == 0:
                for copy in quarter:
                    copy.start()
            if i < 3:
                other = (i + 1) % 2
                for copy in load_quarter(
                    where_ref, pieces, i + 1, buf.at[other], sems.at[other]
                ):
                    copy.start()
            for copy in quarter:
                copy.wait()

    return lax.rem(step, 2)


def quarter_scratch(width):
    return [pltpu.VMEM((2, width, width), jnp.bfloat16), pltpu.SemaphoreType.DMA((2, 8))]


def times_t(left, right):
    return lax.dot_general(
        left, right, (((1,), (1,)), ((), ())), preferred_element_type=jnp.float32
    )


def quarter_call(body, where, ins, in_specs, pieces, outs, out_specs, scratch, flops, name):
    return pl.pallas_call(
        body,
        grid_spec=pltpu.PrefetchScalarGridSpec(
            num_scalar_prefetch=1,
            grid=(4,),
            in_specs=in_specs + [pl.BlockSpec(memory_space=pl.ANY)] * len(pieces),
            out_specs=out_specs,
            scratch_shapes=scratch,
        ),
        out_shape=outs,
        compiler_params=pltpu.CompilerParams(vmem_limit_bytes=58 << 20),
        cost_estimate=pl.CostEstimate(
            flops=flops, bytes_accessed=30 << 20, transcendentals=0
        ),
        name=name,
    )(where, *ins, *pieces)


def fixed(array):
    shape = array.shape
    return pl.BlockSpec(shape, lambda i, w: (0,) * len(shape), pipeline_mode=pl.Buffered(1))


def moving(rows, width):
    return pl.BlockSpec((rows, width), lambda i, w: (0, i))


TILE = 512


def feed_up(where, inputs, bias, pieces):
    rows, width = inputs.shape

    def body(where_ref, x_ref, bias_ref, *refs):
        ins, (act_ref, slope_ref, buf, sems) = refs[:8], refs[8:]
        slot = stream_quarters(where_ref, ins, buf, sems)
        weights = buf.at[slot]
        for t in range(rows // TILE):
            r = pl.ds(t * TILE, TILE)
            u = jnp.dot(x_ref[r, :], weights[...], preferred_element_type=jnp.float32)
            u = u + bias_ref[...]
            square = u * u
            bend = jnp.tanh(u * (GELU_COEF + (GELU_COEF * 0.044715) * square))
            half = 0.5 + 0.5 * bend
            slope = (0.5 * GELU_COEF) + (1.5 * GELU_COEF * 0.044715) * square
            act_ref[r, :] = (u * half).astype(jnp.bfloat16)
            slope_ref[r, :] = (half + u * (1.0 - bend * bend) * slope).astype(jnp.bfloat16)

    out = jax.ShapeDtypeStruct((rows, 4 * width), jnp.bfloat16)
    return quarter_call(
        body,
        where,
        (inputs, bias),
        [fixed(inputs), moving(1, width)],
        pieces,
        [out, out],
        [moving(rows, width)] * 2,
        quarter_scratch(width),
        8 * rows * width * width,
        "feed_up",
    )


def feed_down(where, activated, middle, gate, bias, pieces):
    rows, width = middle.shape

    def body(where_ref, act_ref, middle_ref, gate_ref, bias_ref, *refs):
        ins, (feed_ref, out_ref, buf, sems) = refs[:8], refs[8:]
        quarters = Quarters(where_ref, ins, buf, sems)
        for i in range(4):
            quarters.start(i)
        feed = None
        for i in range(4):
            weights = quarters.wait(i)
            term = jnp.dot(
                act_ref[:, i * width : (i + 1) * width],
                weights[...],
                preferred_element_type=jnp.float32,
            )
            feed = term if feed is None else feed + term
        feed = feed + bias_ref[...]
        feed_ref[...] = feed
        out_ref[...] = (middle_ref[...] + gate_ref[...] * feed).astype(jnp.bfloat16)

    outs = [
        jax.ShapeDtypeStruct((rows, width), jnp.float32),
        jax.ShapeDtypeStruct((rows, width), jnp.bfloat16),
    ]
    def tiles(array):
        return pl.BlockSpec((256, array.shape[1]), lambda i, w: (i, 0))

    return pl.pallas_call(
        body,
        grid_spec=pltpu.PrefetchScalarGridSpec(
            num_scalar_prefetch=1,
            grid=(rows // 256,),
            in_specs=[tiles(activated), tiles(middle), fixed(gate), fixed(bias)]
            + [pl.BlockSpec(memory_space=pl.ANY)] * 8,
            out_specs=[tiles(a) for a in outs],
            scratch_shapes=[
                pltpu.VMEM((4, width, width), jnp.bfloat16),
                pltpu.SemaphoreType.DMA((4, 8)),
            ],
        ),
        out_shape=outs,
        compiler_params=pltpu.CompilerParams(vmem_limit_bytes=58 << 20),
        cost_estimate=pl.CostEstimate(
            flops=8 * rows * width * width, bytes_accessed=30 << 20, transcendentals=0
        ),
        name="feed_down",
    )(where, activated, middle, gate, bias, *pieces)


def feed_back(where, d_feed, slope, down_pieces, up_pieces):
    rows, width = d_feed.shape

    def body(where_ref, d_ref, slope_ref, *refs):
        down_ins, up_ins = refs[:8], refs[8:16]
        before_ref, normed_ref, sum_ref, down_buf, down_sems, up_buf, up_sems = refs[16:]
        slot = stream_quarters(where_ref, down_ins, down_buf, down_sems)
        stream_quarters(where_ref, up_ins, up_buf, up_sems)
        down_weights, up_weights = down_buf.at[slot], up_buf.at[slot]
        step = pl.program_id(0)
        total = jnp.zeros((1, width), jnp.float32)
        for t in range(rows // TILE):
            r = pl.ds(t * TILE, TILE)
            d_act = times_t(d_ref[r, :], down_weights[...])
            d_before = (d_act * slope_ref[r, :].astype(jnp.float32)).astype(jnp.bfloat16)
            before_ref[r, :] = d_before
            total = total + jnp.sum(d_before.astype(jnp.float32), axis=0, keepdims=True)
            term = times_t(d_before, up_weights[...])

            @pl.when(step == 0)
            def _():
                normed_ref[r, :] = term

            @pl.when(step > 0)
            def _():
                normed_ref[r, :] += term

        sum_ref[...] = total

    outs = [
        jax.ShapeDtypeStruct((rows, 4 * width), jnp.bfloat16),
        jax.ShapeDtypeStruct((rows, width), jnp.float32),
        jax.ShapeDtypeStruct((1, 4 * width), jnp.float32),
    ]
    return quarter_call(
        body,
        where,
        (d_feed, slope),
        [fixed(d_feed), moving(rows, width)],
        list(down_pieces) + list(up_pieces),
        outs,
        [moving(rows, width), fixed(outs[1]), moving(1, width)],
        quarter_scratch(width) * 2,
        16 * rows * width * width,
        "feed_back",
    )


def project(where, inputs, query_bias, value_bias, pieces):
    rows, width = inputs.shape

    def body(where_ref, x_ref, query_ref, value_ref, *refs):
        ins, (q_ref, k_ref, v_ref, all_ref, buf, sems, out_sems) = refs[:8], refs[8:]
        base = where_ref[2] * 2 + where_ref[3]

        def loads(quarter, place):
            return load_quarter(where_ref, ins, quarter, buf.at[place], sems.at[place])

        for place in range(4):
            for quarter in range(4):

                @pl.when((base ^ place) == quarter)
                def _(place=place, quarter=quarter):
                    for copy in loads(quarter, place):
                        copy.start()

        stores = []
        biases = (query_ref, None, value_ref, None)
        for place, out_ref in enumerate((q_ref, k_ref, v_ref, None)):
            for copy in loads(0, place):
                copy.wait()
            stores.append(
                pltpu.make_async_copy(buf.at[place], all_ref.at[place], out_sems.at[place])
            )
            stores[-1].start()
            if out_ref is None:
                continue
            for t in range(rows // TILE):
                r = pl.ds(t * TILE, TILE)
                term = jnp.dot(x_ref[r, :], buf[place], preferred_element_type=jnp.float32)
                if biases[place] is not None:
                    term = term + biases[place][...]
                out_ref[r, :] = term.astype(jnp.bfloat16)
        for store in stores:
            store.wait()

    low = jax.ShapeDtypeStruct((rows, width), jnp.bfloat16)
    every = jax.ShapeDtypeStruct((4, width, width), jnp.bfloat16)
    spec = pl.BlockSpec((rows, width), lambda i, w: (0, 0), pipeline_mode=pl.Buffered(1))
    return pl.pallas_call(
        body,
        grid_spec=pltpu.PrefetchScalarGridSpec(
            num_scalar_prefetch=1,
            grid=(1,),
            in_specs=[spec, fixed(query_bias), fixed(value_bias)]
            + [pl.BlockSpec(memory_space=pl.ANY)] * 8,
            out_specs=[spec] * 3 + [pl.BlockSpec(memory_space=pl.ANY)],
            scratch_shapes=[
                pltpu.VMEM((4, width, width), jnp.bfloat16),
                pltpu.SemaphoreType.DMA((4, 8)),
                pltpu.SemaphoreType.DMA((4,)),
            ],
        ),
        out_shape=[low, low, low, every],
        compiler_params=pltpu.CompilerParams(vmem_limit_bytes=58 << 20),
        cost_estimate=pl.CostEstimate(
            flops=6 * rows * width * width, bytes_accessed=30 << 20, transcendentals=0
        ),
        name="project",
    )(where, inputs, query_bias, value_bias, *pieces)


def project_back(parts, matrices):
    rows = parts[0].shape[0]
    width = matrices.shape[1]
    cut = width - parts[1].shape[1]

    def body(*refs):
        ins, (w_ref, out_ref) = refs[:6], refs[6:]
        total = None
        for i in range(3):
            for ref, start, stop in ((ins[2 * i], 0, cut), (ins[2 * i + 1], cut, width)):
                term = times_t(ref[:, : stop - start], w_ref[i, :, start:stop])
                total = term if total is None else total + term
        out_ref[...] = total

    return pl.pallas_call(
        body,
        grid=(rows // TILE,),
        in_specs=[pl.BlockSpec((TILE, a.shape[1]), lambda i: (i, 0)) for a in parts]
        + [
            pl.BlockSpec(
                (3, width, width), lambda i: (0, 0, 0), pipeline_mode=pl.Buffered(1)
            )
        ],
        out_specs=pl.BlockSpec((TILE, width), lambda i: (i, 0)),
        out_shape=jax.ShapeDtypeStruct((rows, width), jnp.float32),
        compiler_params=pltpu.CompilerParams(vmem_limit_bytes=40 << 20),
        cost_estimate=pl.CostEstimate(
            flops=6 * rows * width * width, bytes_accessed=20 << 20, transcendentals=0
        ),
        name="project_back",
    )(*parts, matrices)


def bias_sums(mods, parts, d_branch, up_sums, d_feed):
    width = d_feed.shape[1]
    cut = width - parts[1].shape[1]

    def body(mods_ref, qa_ref, qb_ref, va_ref, vb_ref, branch_ref, up_ref, feed_ref, out_ref):
        @pl.when(pl.program_id(0) == 0)
        def _():
            out_ref[...] = jnp.zeros_like(out_ref)
            out_ref[0:6, :] = mods_ref[...].astype(jnp.float32)
            out_ref[9:13, :] = up_ref[...]

        for row, ref, start, stop in (
            (6, qa_ref, 0, cut),
            (6, qb_ref, cut, width),
            (7, va_ref, 0, cut),
            (7, vb_ref, cut, width),
            (8, branch_ref, 0, width),
            (13, feed_ref, 0, width),
        ):
            terms = ref[:, : stop - start].astype(jnp.float32)
            out_ref[row : row + 1, start:stop] += jnp.sum(terms, axis=0, keepdims=True)

    def tile(array):
        return pl.BlockSpec((256, array.shape[1]), lambda i: (i, 0))

    def held(array):
        return pl.BlockSpec(array.shape, lambda i: (0, 0))

    out = jax.ShapeDtypeStruct((14, width), jnp.float32)
    return pl.pallas_call(
        body,
        grid=(d_feed.shape[0] // 256,),
        in_specs=[held(mods)]
        + [tile(a) for a in parts]
        + [tile(d_branch), held(up_sums), tile(d_feed)],
        out_specs=held(out),
        out_shape=out,
        compiler_params=pltpu.CompilerParams(vmem_limit_bytes=16 << 20),
        cost_estimate=pl.CostEstimate(flops=8 << 20, bytes_accessed=10 << 20, transcendentals=0),
        name="bias_sums",
    )(mods, *parts, d_branch, up_sums, d_feed)


def local_pairs(
    latent_in,
    conditioning,
    ada_weight,
    qkv_weight,
    proj_weight,
    up_weight,
    down_weight,
    bias_pack,
    cotangent,
):
    width = latent_in.shape[2]
    half_rows = latent_in.shape[1]
    zi, xi, ci, yi = [lax.axis_index(name) for name in ALL]
    device = ((zi * 2 + xi) * 2 + ci) * 2 + yi
    where = jnp.stack([zi, xi, ci, yi]).astype(jnp.int32)
    rows = width // 32

    quarter = ci * 2 + yi

    def in_order(array):
        return jnp.stack(
            [lax.dynamic_index_in_dim(array, quarter ^ step, 0, False) for step in range(4)]
        )

    def exchange(array):
        return lax.all_to_all(array, ALL, 0, 0, tiled=True)

    def exchange_quarters(array):
        got = [lax.dynamic_index_in_dim(array, quarter, 0, False)]
        for step, axes in ((1, "y"), (2, "c"), (3, ("c", "y"))):
            entry = lax.dynamic_index_in_dim(array, quarter ^ step, 0, False)
            got.append(
                swap(entry, axes)
                if step < 3
                else lax.ppermute(entry, axes, [(i, i ^ 3) for i in range(4)])
            )
        return in_order(jnp.stack(got))

    def to_all(vector):
        return exchange(jnp.broadcast_to(vector, (32,) + vector.shape))

    def over_tokens(left, right):
        return lax.dot_general(
            left, right, (((0,), (0,)), ((), ())), preferred_element_type=jnp.float32
        )

    def times_transposed(left, right):
        return lax.dot_general(
            left, right, (((1,), (1,)), ((), ())), preferred_element_type=jnp.float32
        )

    qkv_rows = qkv_weight.reshape(rows, 3 * width)
    quarters = jnp.stack(
        [qkv_rows[:, i * width : (i + 1) * width] for i in range(3)]
        + [proj_weight.reshape(rows, width)]
    )
    up_quarters = up_weight.reshape(rows, 8, 4, 144).transpose(2, 0, 1, 3).reshape(4, rows, width)
    units = exchange_quarters(jnp.concatenate([quarters, up_quarters], axis=1))
    unit_a = units[:, :rows].reshape(4 * rows, width)
    unit_u = units[:, rows:].reshape(4 * rows, width)
    unit_d = down_weight.reshape(4 * rows, width)
    hops_a = line_hops(lambda step: unit_a)
    other_half = after(lax.dynamic_index_in_dim(latent_in, 1 - yi, 0, False), unit_a)
    half_received = swap(other_half, "y")
    line_a = jnp.stack([after(unit_a, half_received), *hops_a])
    plane_a = plane_gather(line_a)
    unit_u = after(unit_u, line_a)
    hops_u = line_hops(lambda step: unit_u)
    own_condition = lax.dynamic_index_in_dim(conditioning, yi, 0, False)
    small = jnp.concatenate([bias_pack, own_condition]).reshape(2, -1)
    small = to_all(after(small, line_a)).reshape(32, -1)
    bias_share = bias_pack.shape[0]
    biases = small[:, :bias_share].reshape(-1).astype(jnp.float32)
    conditions = small[:, bias_share:].astype(jnp.float32)
    silu_all = jax.nn.silu(conditions).astype(jnp.bfloat16)
    silu_cut = lax.dynamic_slice(silu_all, (0, device * rows), (32, rows))
    ada_rows = ada_weight.reshape(rows, 6 * width)
    shares = jnp.dot(silu_cut, ada_rows, preferred_element_type=jnp.float32)
    first_shares, later_shares = shares[:, : 2 * width], shares[:, 2 * width :]
    line_a, plane_a, hops_u, first_shares = lax.optimization_barrier(
        (line_a, plane_a, hops_u, first_shares)
    )
    corner_a = corner_gather(*plane_a)
    core_a = [swap(p, "c") for p in (line_a, *plane_a)]
    first_shares = after(first_shares, *core_a)
    modulations = jnp.sum(exchange(first_shares), axis=0, keepdims=True)
    modulations = modulations + biases[: 2 * width]
    shift_attention, scale_attention = jnp.split(modulations, 2, axis=1)
    own_half = lax.dynamic_index_in_dim(latent_in, yi, 0, False)
    tokens_low = jnp.concatenate([own_half, half_received])
    tokens = tokens_low.astype(jnp.float32)
    normed = norm_modulate(tokens, shift_attention, scale_attention).astype(jnp.bfloat16)
    line_u = jnp.stack([unit_u, *hops_u])
    unit_d = after(unit_d, line_u, *core_a)
    hops_d = line_hops(lambda step: unit_d)
    corner_a = after(corner_a, unit_d, modulations)
    core_a.append(swap(corner_a, "c"))
    line_u = after(line_u, core_a[3])
    plane_u = plane_gather(line_u)
    query_bias = biases[None, 6 * width : 7 * width]
    value_bias = biases[None, 7 * width : 8 * width]
    proj_bias = biases[8 * width : 9 * width]
    up_bias = biases[9 * width : 9 * width + FF].reshape(8, 4, 144).transpose(1, 0, 2)
    up_bias = in_order(up_bias.reshape(4, width)).reshape(1, FF)
    down_bias = biases[None, 9 * width + FF :]
    queries, keys, values, matrices = project(
        where,
        normed,
        query_bias,
        value_bias,
        after([line_a, *plane_a, corner_a, *core_a], line_u, unit_d),
    )
    proj_matrix = matrices[3]
    line_d = jnp.stack([after(unit_d, values), *hops_d])
    plane_u = after(plane_u, line_d)
    corner_u = corner_gather(*plane_u)
    core_u = [swap(p, "c") for p in (after(line_u, line_d), *plane_u)]
    part_one = attn_fwd(after(queries, *plane_u, line_d), keys, values, (0, 8))
    line_d, corner_u, core_u = after((line_d, corner_u, core_u), *part_one)
    core_u.append(swap(corner_u, "c"))
    plane_d = plane_gather(line_d)
    attended, log_total = attn_fwd(
        after(queries, line_d, *core_u[:3]), keys, values, (8, 8), tuple(part_one)
    )
    later_modulations = jnp.sum(after(exchange(after(later_shares, line_u)), *part_one), axis=0, keepdims=True)
    later_modulations = later_modulations + biases[2 * width : 6 * width]
    gate_attention, shift_feed, scale_feed, gate_feed = jnp.split(later_modulations, 4, axis=1)
    branch = (
        jnp.dot(attended, proj_matrix, preferred_element_type=jnp.float32)
        + proj_bias
    )
    middle = tokens + gate_attention * branch
    normed_feed = norm_modulate(middle, shift_feed, scale_feed).astype(jnp.bfloat16)
    pieces_u = after([line_u, *plane_u, corner_u, *core_u], normed_feed)
    plane_d = after(plane_d, normed_feed)
    corner_d = corner_gather(*plane_d)
    core_d = [swap(p, "c") for p in (after(line_d, normed_feed), *plane_d)]
    other_cotangent = after(lax.dynamic_index_in_dim(cotangent, 1 - yi, 0, False), *plane_d)
    cotangent_received = swap(other_cotangent, "y")
    activated, slope = feed_up(
        where,
        after(normed_feed, *core_d[:3], other_cotangent),
        up_bias,
        pieces_u,
    )
    activated, corner_d = lax.optimization_barrier((activated, corner_d))
    core_d.append(swap(corner_d, "c"))
    pieces_d = after([line_d, *plane_d, corner_d, *core_d], activated)
    feed_out, output_low = feed_down(where, activated, middle, gate_feed, down_bias, pieces_d)
    cotangent_received, output_low = lax.optimization_barrier((cotangent_received, output_low))
    own_cotangent = lax.dynamic_index_in_dim(cotangent, yi, 0, False)
    upstream = jnp.concatenate([own_cotangent, cotangent_received]).astype(jnp.float32)
    d_feed = (gate_feed * upstream).astype(jnp.bfloat16)
    ours, others = slice(None, 2 * width), slice(2 * width, None)
    down_sent = over_tokens(activated[:, others], d_feed).astype(jnp.bfloat16)
    down_received = swap(down_sent, "c")
    output_received = swap(after(output_low, down_sent)[half_rows:], "y")
    d_gate_feed = jnp.sum(upstream * feed_out, axis=0, keepdims=True)
    down_half = over_tokens(after(activated, down_sent)[:, ours], d_feed)
    down = ScatterSum(rows_of, add_low(down_half, down_received), (0, 1))
    down.corner()
    d_before, d_normed_feed, before_sums = feed_back(
        where, after(d_feed, *down.sent), slope, pieces_d, pieces_u
    )
    output_received, d_before = lax.optimization_barrier((output_received, d_before))
    down.plane(d_normed_feed)
    up_sent = over_tokens(after(normed_feed, *down.sent), d_before[:, others])
    up_sent = up_sent.astype(jnp.bfloat16)
    up_received = swap(up_sent, "c")
    unused_norm, norm_pull = jax.vjp(norm_modulate, middle, shift_feed, scale_feed)
    d_middle_part, d_shift_feed, d_scale_feed = norm_pull(
        after(d_normed_feed, up_sent)
    )
    d_middle = upstream + d_middle_part
    d_gate_attention = jnp.sum(d_middle * branch, axis=0, keepdims=True)
    d_branch = (gate_attention * d_middle).astype(jnp.bfloat16)
    d_attended = times_transposed(d_branch, proj_matrix).astype(jnp.bfloat16)
    mods_early = jnp.concatenate([d_gate_attention, d_shift_feed, d_scale_feed, d_gate_feed], 1)
    mods_early = mods_early.astype(jnp.bfloat16)
    up_half = over_tokens(after(normed_feed, d_attended), d_before[:, ours])
    up = ScatterSum(columns_of, add_low(up_half, up_received), (0, 1))
    down.line(up.half)
    up.corner()
    log_rows = log_total[:, :H].T
    part_a = attn_bwd(
        queries,
        keys,
        values,
        after(d_attended, *up.sent, *down.sent, mods_early),
        log_rows,
        (0, 8),
    )

    def attention_terms(gradients, d_b, core, received, *earlier):
        d_q, d_k, d_v = gradients
        left = after(normed, *earlier)
        first = over_tokens(left, jnp.where(core == 0, d_q, d_v))
        second = over_tokens(
            jnp.where(core == 0, left, attended), jnp.where(core == 0, d_k, d_b)
        )
        if received is not None:
            first, second = first + received[:width], second + received[width:]
        return jnp.concatenate([first.astype(jnp.bfloat16), second.astype(jnp.bfloat16)])

    left_terms = [a[:, :512] for a in part_a], d_branch[:, :512]
    left_sent = attention_terms(*left_terms, 1 - ci, None, *part_a, *down.got, *up.got)
    left_received = swap(left_sent, "c")
    up.plane(left_sent)
    left_half = attention_terms(*left_terms, ci, left_received, left_sent, *up.sent)
    left = ScatterSum(rows_of, left_half, (yi, 1 - yi))
    left.corner()
    down_sum = down.total(left_half)
    part_b = attn_bwd(
        queries,
        keys,
        values,
        after(d_attended, *left.sent, down_sum),
        log_rows,
        (8, 4),
        part_a,
    )
    part_b = after(tuple(part_b), *left.got, *up.got)
    left.plane(*part_b)
    up.line(*part_b)
    part_c = attn_bwd(
        queries,
        keys,
        values,
        after(d_attended, *left.sent, *up.sent),
        log_rows,
        (12, 4),
        part_b,
    )
    part_c = after(tuple(part_c), *left.got, *up.got)
    right_parts = [
        jnp.concatenate([b[:, :256], c], axis=1) for b, c in zip(part_b, part_c)
    ]
    right_terms = right_parts, d_branch[:, 512:]
    left.line(*part_c)
    right_sent = attention_terms(*right_terms, 1 - ci, None, *left.sent)
    right_received = swap(right_sent, "c")
    right_half = attention_terms(*right_terms, ci, right_received, right_sent)
    right = ScatterSum(rows_of, right_half, (yi, 1 - yi))
    right.corner()
    parts = [array for pair in zip(part_a, right_parts) for array in pair]
    d_normed = project_back(after(parts, *right.sent, *left.got), matrices)
    right.plane(d_normed)
    up_sum = exchange_quarters(up.total(*right.sent).reshape(4, rows, width))
    unused_first, first_pull = jax.vjp(norm_modulate, tokens, shift_attention, scale_attention)
    d_tokens_part, d_shift_attention, d_scale_attention = first_pull(after(d_normed, *right.sent))
    grad_low = (d_middle + d_tokens_part).astype(jnp.bfloat16)
    grad_low, up_sum = lax.optimization_barrier((grad_low, up_sum))
    mods = jnp.concatenate([d_shift_attention, d_scale_attention], axis=1).astype(jnp.bfloat16)
    mods = jnp.concatenate([mods, mods_early], axis=1)
    every_mods = to_all(mods.reshape(2, 3 * width)).reshape(32, 6 * width)
    right.line(grad_low, mods)
    quarter_rows = half_rows // 2
    grad_first = swap(grad_low[half_rows : half_rows + quarter_rows], "y")

    def both_halves(own_rows, *received):
        both = jnp.stack([own_rows, own_rows])
        row = 0
        for piece in received:
            both = lax.dynamic_update_slice(both, piece[None], (1 - yi, row, 0))
            row += piece.shape[0]
        return both

    left_totals = left.total(*right.sent)
    down_sum, output_low, output_received, up_sum = after(
        (down_sum, output_low, output_received, up_sum), *right.sent
    )
    output = both_halves(output_low[:half_rows], output_received)
    grad_down = down_sum.reshape(-1)
    grad_up = up_sum.reshape(4, rows, 8, 144).transpose(1, 2, 0, 3).reshape(-1)
    up_sums = in_order(before_sums.reshape(4, width)).reshape(4, 8, 144).transpose(1, 0, 2)
    bias_terms = bias_sums(
        mods.reshape(6, width),
        after((part_a[0], right_parts[0], part_a[2], right_parts[2]), *right.sent),
        d_branch,
        up_sums.reshape(4, width),
        d_feed,
    ).reshape(32, -1)
    right_totals = right.total(left_totals, output, grad_down, grad_up, bias_terms)
    sums = jnp.concatenate([left_totals, right_totals], axis=1).reshape(4, rows, width)
    sums = exchange_quarters(sums)
    every_mods, grad_first = lax.optimization_barrier((every_mods, grad_first))
    grad_last = swap(after(grad_low, grad_first)[half_rows + quarter_rows :], "y")
    d_silu_rows = times_transposed(every_mods, ada_rows)
    d_silu_parts = jnp.repeat(d_silu_rows.reshape(16, 1, 2, rows), 2, axis=1)
    parts = exchange(
        jnp.concatenate([d_silu_parts.reshape(32, 2 * rows), bias_terms], axis=1)
    )
    grad_ada = over_tokens(silu_cut, every_mods).reshape(-1)
    parts, grad_last = lax.optimization_barrier((parts, grad_last))
    d_silu = parts[:, : 2 * rows].reshape(32, 2, rows).transpose(1, 0, 2).reshape(2, width)
    grad_bias = jnp.sum(parts[:, 2 * rows :], axis=0)
    unused_silu, silu_pull = jax.vjp(jax.nn.silu, conditioning.astype(jnp.float32))
    grad_cond = silu_pull(d_silu)[0].astype(jnp.bfloat16)
    grad_input = both_halves(grad_low[:half_rows], grad_first, grad_last)
    grad_qkv = jnp.concatenate([sums[0], sums[1], sums[2]], axis=1).reshape(-1)
    grad_proj = sums[3].reshape(-1)
    return (
        output,
        grad_input,
        grad_cond,
        grad_ada,
        grad_qkv,
        grad_proj,
        grad_up,
        grad_down,
        grad_bias,
    )


def local_any(
    latent_in,
    conditioning,
    ada_weight,
    qkv_weight,
    proj_weight,
    up_weight,
    down_weight,
    bias_pack,
    cotangent,
):
    model_width = latent_in.shape[2]
    every_param = (
        lax.all_gather(ada_weight, ("batch", "seq"), axis=0, tiled=True),
        lax.all_gather(qkv_weight, ("batch", "seq"), axis=0, tiled=True),
        lax.all_gather(proj_weight, ("batch", "seq"), axis=0, tiled=True),
        lax.all_gather(up_weight, ("batch", "seq"), axis=0, tiled=True),
        lax.all_gather(down_weight, ("batch", "seq"), axis=0, tiled=True),
        lax.all_gather(bias_pack, ("batch", "seq"), axis=0, tiled=True),
    )
    ada_matrix, qkv_matrix, proj_matrix, up_matrix, down_matrix, biases = shape_all(
        every_param, model_width
    )
    ada_bias = biases[: 6 * model_width]
    query_bias = biases[6 * model_width : 7 * model_width]
    value_bias = biases[7 * model_width : 8 * model_width]
    proj_bias = biases[8 * model_width : 9 * model_width]
    up_bias = biases[9 * model_width : 9 * model_width + FF]
    down_bias = biases[9 * model_width + FF :]
    tokens = latent_in.astype(jnp.float32)
    conditions = conditioning.astype(jnp.float32)
    silu_cond = jax.nn.silu(conditions).astype(jnp.bfloat16)
    modulations = jnp.dot(silu_cond, ada_matrix, preferred_element_type=jnp.float32) + ada_bias
    shift_attention, scale_attention, gate_attention, shift_feed, scale_feed, gate_feed = jnp.split(
        modulations[:, None, :], 6, axis=2
    )
    normed = norm_modulate(tokens, shift_attention, scale_attention).astype(jnp.bfloat16)
    projected = jnp.einsum("btd,df->btf", normed, qkv_matrix, preferred_element_type=jnp.float32)
    queries = (projected[..., :model_width] + query_bias).astype(jnp.bfloat16)
    own_keys = jnp.concatenate(
        [
            projected[..., model_width : 2 * model_width],
            projected[..., 2 * model_width :] + value_bias,
        ],
        axis=2,
    ).astype(jnp.bfloat16)
    every_keys = lax.all_gather(own_keys, "seq", axis=1, tiled=True)
    attended, log_total = lax.map(attend_latent, (queries, every_keys))
    attended = attended.astype(jnp.bfloat16)
    branch = (
        jnp.einsum("btd,de->bte", attended, proj_matrix, preferred_element_type=jnp.float32)
        + proj_bias
    )
    middle = tokens + gate_attention * branch
    normed_feed = norm_modulate(middle, shift_feed, scale_feed).astype(jnp.bfloat16)
    before = (
        jnp.einsum("btd,df->btf", normed_feed, up_matrix, preferred_element_type=jnp.float32)
        + up_bias
    )
    activated = gelu_tanh(before).astype(jnp.bfloat16)
    feed_out = (
        jnp.einsum("btf,fd->btd", activated, down_matrix, preferred_element_type=jnp.float32)
        + down_bias
    )
    output = (middle + gate_feed * feed_out).astype(jnp.bfloat16)
    param_again = (
        lax.all_gather(ada_weight, ("batch", "seq"), axis=0, tiled=True),
        lax.all_gather(qkv_weight, ("batch", "seq"), axis=0, tiled=True),
        lax.all_gather(proj_weight, ("batch", "seq"), axis=0, tiled=True),
        lax.all_gather(up_weight, ("batch", "seq"), axis=0, tiled=True),
        lax.all_gather(down_weight, ("batch", "seq"), axis=0, tiled=True),
        lax.all_gather(bias_pack, ("batch", "seq"), axis=0, tiled=True),
    )
    ada_matrix, qkv_matrix, proj_matrix, up_matrix, down_matrix, biases = shape_all(
        param_again, model_width
    )
    upstream = cotangent.astype(jnp.float32)
    d_gate_feed = jnp.sum(upstream * feed_out, axis=1, keepdims=True)
    d_feed = (gate_feed * upstream).astype(jnp.bfloat16)
    d_activated = jnp.einsum("btd,fd->btf", d_feed, down_matrix, preferred_element_type=jnp.float32)
    unused_gelu, gelu_pull = jax.vjp(gelu_tanh, before)
    d_before = gelu_pull(d_activated)[0].astype(jnp.bfloat16)
    d_normed_feed = jnp.einsum(
        "btf,df->btd", d_before, up_matrix, preferred_element_type=jnp.float32
    )
    unused_norm, norm_pull = jax.vjp(norm_modulate, middle, shift_feed, scale_feed)
    d_middle_part, d_shift_feed, d_scale_feed = norm_pull(d_normed_feed)
    d_middle = upstream + d_middle_part
    d_gate_attention = jnp.sum(d_middle * branch, axis=1, keepdims=True)
    d_branch = (gate_attention * d_middle).astype(jnp.bfloat16)
    d_attended = jnp.einsum(
        "bte,de->btd", d_branch, proj_matrix, preferred_element_type=jnp.float32
    ).astype(jnp.bfloat16)
    d_queries, d_every = lax.map(attend_back, (queries, every_keys, log_total, d_attended))
    d_queries = d_queries.astype(jnp.bfloat16)
    d_own = lax.psum_scatter(d_every.astype(jnp.bfloat16), "seq", scatter_dimension=1, tiled=True)
    d_projected = jnp.concatenate([d_queries, d_own], axis=2)
    d_normed = jnp.einsum(
        "btf,df->btd", d_projected, qkv_matrix, preferred_element_type=jnp.float32
    )
    unused_first, first_pull = jax.vjp(norm_modulate, tokens, shift_attention, scale_attention)
    d_tokens_part, d_shift_attention, d_scale_attention = first_pull(d_normed)
    grad_input = (d_middle + d_tokens_part).astype(jnp.bfloat16)
    local_mods = jnp.concatenate(
        [
            d_shift_attention,
            d_scale_attention,
            d_gate_attention,
            d_shift_feed,
            d_scale_feed,
            d_gate_feed,
        ],
        axis=2,
    )[:, 0, :]
    d_mods = lax.psum(local_mods.astype(jnp.bfloat16), "seq")
    d_silu = jnp.einsum("bf,df->bd", d_mods, ada_matrix, preferred_element_type=jnp.float32)
    unused_silu, silu_pull = jax.vjp(jax.nn.silu, conditions)
    grad_cond = silu_pull(d_silu)[0].astype(jnp.bfloat16)
    is_owner = lax.axis_index("seq") == 0
    owned_mods = jnp.where(is_owner, d_mods, jnp.zeros_like(d_mods))
    bias_terms = jnp.concatenate(
        [
            jnp.sum(owned_mods, axis=0, dtype=jnp.float32),
            jnp.sum(d_queries, axis=(0, 1), dtype=jnp.float32),
            jnp.sum(d_own[..., model_width:], axis=(0, 1), dtype=jnp.float32),
            jnp.sum(d_branch, axis=(0, 1), dtype=jnp.float32),
            jnp.sum(d_before, axis=(0, 1), dtype=jnp.float32),
            jnp.sum(d_feed, axis=(0, 1), dtype=jnp.float32),
        ]
    )
    matrix_terms = [
        (silu_cond, owned_mods, ada_weight.shape[0]),
        (
            normed.reshape(-1, model_width),
            d_projected.reshape(-1, 3 * model_width),
            qkv_weight.shape[0],
        ),
        (
            attended.reshape(-1, model_width),
            d_branch.reshape(-1, model_width),
            proj_weight.shape[0],
        ),
        (normed_feed.reshape(-1, model_width), d_before.reshape(-1, FF), up_weight.shape[0]),
        (activated.reshape(-1, FF), d_feed.reshape(-1, model_width), down_weight.shape[0]),
    ]
    bias_share = bias_pack.shape[0]
    shard_rows = sum((entry[2] for entry in matrix_terms)) + bias_share
    block_count = shard_rows * lax.axis_size(("batch", "seq")) // shard_rows
    pieces = []
    for left, right, grad_shard_size in matrix_terms:
        pieces.append(flat_term(left, right).reshape(block_count, grad_shard_size))
    pieces.append(bias_terms.reshape(block_count, bias_share))
    owned_grads = lax.psum_scatter(
        jnp.concatenate(pieces, axis=1).reshape(-1),
        ("batch", "seq"),
        scatter_dimension=0,
        tiled=True,
    )
    results = []
    cursor = 0
    for shard_size in [entry[2] for entry in matrix_terms] + [bias_share]:
        results.append(owned_grads[cursor : cursor + shard_size])
        cursor = cursor + shard_size
    grad_ada, grad_qkv, grad_proj, grad_up, grad_down, grad_bias = results
    return (
        output,
        grad_input,
        grad_cond,
        grad_ada,
        grad_qkv,
        grad_proj,
        grad_up,
        grad_down,
        grad_bias,
    )


def solution(mesh):
    batch, seq = mesh.shape["batch"], mesh.shape["seq"]
    if (batch, seq) == (16, 2):
        inner = Mesh(mesh.devices.reshape(4, 2, 2, 2), ALL)
        body, tokens = local_pairs, ("z", "x", "c")
        flat, split = P(ALL), "y"
    else:
        inner, body, tokens, split = mesh, local_any, "batch", "seq"
        flat = P(("batch", "seq"))
    activations = P(tokens, split, None)
    vectors = P(tokens, None)
    in_specs = (activations, vectors) + (flat,) * 6 + (activations,)
    out_specs = (activations, activations, vectors) + (flat,) * 6
    return jax.shard_map(body, mesh=inner, in_specs=in_specs, out_specs=out_specs, check_vma=False)
```
